256 devices in a mesh: seq: 32 (over y, z), wide: 8 (over x, core).
Axes of the slice: x: 4, y: 4, z: 8, core: 2. Of those that a mesh axis runs over, the one named last changes fastest.
Arguments:
- queries: bfloat16 [16384, 4096], P('seq', 'wide'), may hold values from -500 to 500
- keys: bfloat16 [16384, 4096], P('seq', 'wide'), may hold values from -500 to 500
- values: bfloat16 [16384, 4096], P('seq', 'wide'), may hold values from -6 to 6
- log_decay: float32 [16384, 32], P('seq', 'wide'), may hold values from -0.8 to 0, as said below
- ridge: float32 [4096], P('wide'), may hold values from 0.05 to 2
- out_weight: bfloat16 [4096, 4096], P('wide'), may hold values from -0.09375 to 0.09375
Outputs:
- mixed: bfloat16 [16384, 4096], P(('seq', 'wide'))
The draws below stay inside these ranges and needn't reach their ends.
Inputs may be any that keep to these rules, and one draw needn't show every extreme that they name: `log_decay`: negative.
All inputs are finite; a program needn't handle non-finite values.
Results may differ from the reference program's by a relative error of at most 0.0065.
Values sent between devices are 32-bit elements; how exact they have to be, the bound alone decides.
A program may use at most 128 MiB of HBM per device.

```python
import math
import jax
import jax.numpy as jnp
from jax import lax

D = 4096
HD = 128
TOK_DEV = 512
SPAN = 128
ITERS = 8
HEADS = 32
TOKENS = 16384


def scaled_field(key, salt):
    base_key = jax.random.fold_in(key, salt)
    key_base, key_row, key_col = jax.random.split(base_key, 3)
    width = HEADS * HD
    column_scale = jnp.exp(jax.random.uniform(key_col, (1, width), jnp.float32, 0.0, math.log(10.0)))
    base = jnp.clip(jax.random.normal(key_base, (TOKENS, width), jnp.float32), -5.0, 5.0)
    row_scale = jnp.exp(jax.random.uniform(key_row, (TOKENS, 1), jnp.float32, 0.0, math.log(10.0)))
    return (base * row_scale * column_scale).astype(jnp.bfloat16)


def draw_queries(key, part):
    return scaled_field(key, 101)


def draw_keys(key, part):
    return scaled_field(key, 202)


def draw_log_decay(key, part):
    subkeys = jax.random.split(jax.random.fold_in(key, 303), 7)
    share = 0.5
    lasting = jax.random.uniform(subkeys[0], (HEADS,), jnp.float32) < share
    quick_rate = 1.0 / jax.random.uniform(subkeys[1], (HEADS,), jnp.float32, 30.0, 50.0)
    slow_rate = jax.random.uniform(subkeys[2], (HEADS,), jnp.float32, 0.03, 0.08) / TOKENS
    base_rate = jnp.where(lasting, slow_rate, quick_rate)
    jitter = jax.random.uniform(subkeys[3], (TOKENS, HEADS), jnp.float32, 0.5, 1.5)
    block_count = TOKENS // TOK_DEV
    block_factor = jnp.exp(jax.random.uniform(subkeys[4], (block_count, 1, 1), jnp.float32, -0.69, 0.69))
    forgetting_coefficient = ((base_rate[None, :] * jitter).reshape(block_count, TOK_DEV, HEADS) * block_factor).reshape(TOKENS, HEADS)
    positions = jax.random.randint(subkeys[5], (3,), 0, TOKENS)
    forgetting_factor_series = jax.random.uniform(subkeys[6], (3, HEADS), jnp.float32, math.log(0.52), math.log(0.8))
    agreement_counter = (jnp.arange(TOKENS)[:, None] == positions[None, :]).astype(jnp.float32)
    segment_partition = jnp.dot(agreement_counter, forgetting_factor_series, precision=jax.lax.Precision.HIGHEST)
    return (segment_partition - forgetting_coefficient).astype(jnp.float32)


def shard_levels(own_key, shape, cuts, least, top_value):
    def one(position, blocks):
        draws = jax.random.uniform(jax.random.fold_in(jax.random.fold_in(own_key, 6), position), (blocks,), jnp.float32, least / len(cuts), top_value / len(cuts))
        return jnp.repeat(jnp.exp(draws), shape[position] // blocks).reshape((-1,) + (1,) * (len(shape) - position - 1))

    factor_of = one(*cuts[0])
    for cut in cuts[1:]:
        factor_of = factor_of * one(*cut)
    return factor_of


def normal_values(key, extent, scale, most, pieces=(), held_as=jnp.bfloat16):
    gain = shard_levels(key, extent, pieces, -0.22, 0.18) if pieces else 1.0
    drawn = jax.random.normal(key, extent, jnp.float32) * scale * gain
    return jnp.minimum(jnp.maximum(drawn, -most), most).astype(held_as)


def setup_inputs(seed: int = 0) -> dict:
    splits = jax.random.split(jax.random.key(seed), 7)
    return {
        "queries": draw_queries(jax.random.fold_in(splits[6], 71), 0),
        "keys": draw_keys(jax.random.fold_in(splits[6], 71), 0),
        "values": normal_values(splits[2], (TOKENS, HEADS * HD), 1.0, 6.0, ((0, 32), (1, 8))),
        "log_decay": draw_log_decay(jax.random.fold_in(splits[6], 71), 0),
        "ridge": jnp.clip(jnp.exp(math.log(2.0) - 3.6888794 * jax.random.uniform(splits[4], (HEADS * HD,), jnp.float32) ** shard_levels(splits[4], (HEADS * HD,), ((0, 8),), -0.2, 0.2)), 0.05, 2.0),
        "out_weight": normal_values(splits[5], (HEADS * HD, D), (HEADS * HD) ** -0.5, 0.09375, ((0, 8),)),
    }


highest = lax.Precision.HIGHEST

def unit_rows(matrix, head_count, head_size):
    entries = matrix.astype(jnp.float32).reshape(matrix.shape[0], head_count, head_size)
    return entries * lax.rsqrt(lax.optimization_barrier(jnp.sum(entries * entries, axis=-1, keepdims=True)) + 1e-06)

def span_read(query, key_rows, value_rows, cumulative, state_h, state_g, ridge_rows):
    length = query.shape[-2]
    places = jnp.arange(length)
    causal = places[:, None] >= places[None, :]
    spread = cumulative[..., :, None] - cumulative[..., None, :]
    weight = jnp.where(causal, jnp.exp(jnp.where(causal, spread, 0.0)), 0.0)
    opening = jnp.exp(cumulative)[..., None]

    def operate(vector):
        scores = jnp.einsum('...td,...sd->...ts', vector, key_rows, precision=highest) * weight
        carried = jnp.einsum('...td,...ed->...te', vector, state_h, precision=highest)
        local_part = jnp.einsum('...ts,...sd->...td', scores, key_rows, precision=highest)
        return opening * carried + local_part + ridge_rows * vector
    solved = jnp.zeros_like(query)
    residual = query
    direction = query
    norm_now = lax.optimization_barrier(jnp.sum(residual * residual, axis=-1, keepdims=True))
    for sweep in range(ITERS):
        image = operate(direction)
        alpha = norm_now / lax.optimization_barrier(jnp.sum(direction * image, axis=-1, keepdims=True))
        solved = solved + alpha * direction
        residual = residual - alpha * image
        norm_next = lax.optimization_barrier(jnp.sum(residual * residual, axis=-1, keepdims=True))
        direction = residual + norm_next / norm_now * direction
        norm_now = norm_next
    scores = jnp.einsum('...td,...sd->...ts', solved, key_rows, precision=highest) * weight
    carried = jnp.einsum('...td,...ed->...te', solved, state_g, precision=highest)
    return opening * carried + jnp.einsum('...ts,...se->...te', scores, value_rows, precision=highest)

def span_summary(key_rows, value_rows, cumulative):
    closing = cumulative[..., -1]
    fading = jnp.exp(closing[..., None] - cumulative)[..., None]
    gram = jnp.einsum('...sd,...se->...de', key_rows * fading, key_rows, precision=highest)
    memory = jnp.einsum('...se,...sd->...ed', value_rows * fading, key_rows, precision=highest)
    return (closing, gram, memory)

def reference(queries, keys, values, log_decay, ridge, out_weight):
    row_count = queries.shape[0]
    head_count = log_decay.shape[1]
    head_size = ridge.shape[0] // head_count
    block_list = row_count // SPAN

    def arrange(entries):
        return entries.reshape(block_list, SPAN, head_count, head_size).transpose(0, 2, 1, 3)
    query_rows = arrange(unit_rows(queries, head_count, head_size))
    key_rows = arrange(unit_rows(keys, head_count, head_size))
    value_rows = arrange(values.astype(jnp.float32).reshape(row_count, head_count, head_size))
    cumulative = jnp.cumsum(log_decay.reshape(block_list, SPAN, head_count).transpose(0, 2, 1), axis=-1)
    ridge_rows = ridge.reshape(head_count, 1, head_size)

    def step_forward(carry, items):
        state_h, state_g = carry
        query, key_block, value_block, cum_block = items
        read = span_read(query, key_block, value_block, cum_block, state_h, state_g, ridge_rows)
        closing, gram, memory = span_summary(key_block, value_block, cum_block)
        factor = jnp.exp(closing)[:, None, None]
        return ((factor * state_h + gram, factor * state_g + memory), read)
    blank_state = jnp.zeros((head_count, head_size, head_size), jnp.float32)
    final_state, reads = lax.scan(step_forward, (blank_state, blank_state), (query_rows, key_rows, value_rows, cumulative))
    reads = reads.transpose(0, 2, 1, 3).reshape(row_count, head_count, head_size)
    normed = reads * lax.rsqrt(lax.optimization_barrier(jnp.mean(reads * reads, axis=-1, keepdims=True)) + 1e-06)
    normed = normed.reshape(row_count, head_count * head_size).astype(jnp.bfloat16)
    return jnp.dot(normed, out_weight, preferred_element_type=jnp.float32).astype(jnp.bfloat16)
```

```python
import functools

import jax
import jax.numpy as jnp
from jax import lax
from jax.experimental import pallas as pl
from jax.experimental.pallas import tpu as pltpu
from jax.sharding import PartitionSpec as P

MESH = pl.DeviceIdType.MESH
F32 = jnp.float32
BF16 = jnp.bfloat16
HD = 128
SPAN = 128
ITERS = 8
HL = 4
NJ = 4
NCH = 8
ORDER = (2, 1, 3, 0)
highest = lax.Precision.HIGHEST


def parts(value):
    high = value.astype(BF16)
    return high, (value - high.astype(F32)).astype(BF16)


def stacked(value):
    return jnp.concatenate(parts(value), axis=0)


def dot(a, b):
    return jnp.dot(a, b, preferred_element_type=F32)


def kernel(
    ny, nz, nx,
    q_ref, k_ref, v_ref, ld_ref, ridge_ref, w_hbm, o_ref,
    w_vm, st, buf1, tot, buf2, pre, lb, sdec, crow, w1, w2, k2, kt2, vt2, qt, ridge_m,
    a1, a2, xs, rs, ps, nm, pown, pout, pin, ra, rb, f1, f2,
    w_sem, z_send, z_recv, y_send, y_recv, p_send, p_recv, r_send, r_recv, f_send, f_recv,
):
    seq = lax.axis_index("seq")
    wide = lax.axis_index("wide")
    y, z = lax.div(seq, nz), lax.rem(seq, nz)
    x, c = lax.div(wide, 2), lax.rem(wide, 2)
    rows = HD // nz
    partner = x * 2 + (1 - c)
    right = lax.rem(x + 1, nx) * 2 + c
    left = lax.rem(x + nx - 1, nx) * 2 + c

    load_w = pltpu.make_async_copy(w_hbm, w_vm, w_sem)
    load_w.start()

    barrier = pltpu.get_barrier_semaphore()
    for step in range(1, nz):
        to = y * nz + lax.rem(z + step, nz)
        pl.semaphore_signal(barrier, inc=1, device_id=(to, wide), device_id_type=MESH)
    for step in range(1, ny):
        to = lax.rem(y + step, ny) * nz + z
        pl.semaphore_signal(barrier, inc=1, device_id=(to, wide), device_id_type=MESH)
    for to in (partner, right, left):
        pl.semaphore_signal(barrier, inc=1, device_id=(seq, to), device_id_type=MESH)

    place_r = lax.broadcasted_iota(jnp.int32, (SPAN, SPAN), 0)
    place_c = lax.broadcasted_iota(jnp.int32, (SPAN, SPAN), 1)
    lower = (place_r >= place_c).astype(F32)
    upper = (place_r <= place_c).astype(F32)
    ccols, norms = [], {}
    total = jnp.zeros((1, HL), F32)
    closings = []
    for j in range(NJ):
        decay = ld_ref[j * SPAN : (j + 1) * SPAN, :]
        ccol = jnp.dot(lower, decay, precision=highest, preferred_element_type=F32)
        ccols.append(ccol)
        crow[j, 0:HL, :] = lax.dot_general(
            decay, upper, (((0,), (0,)), ((), ())), precision=highest, preferred_element_type=F32
        )
        for h in range(HL):
            sdec[j, h : h + 1, :] = jnp.exp(jnp.broadcast_to(total[:, h : h + 1], (1, HD)))
        closing = ccol[SPAN - 1 : SPAN, :]
        closings.append(closing)
        total = total + closing
    group = lax.rem(place_r, rows)
    marks = jnp.zeros((HD, HD), F32)
    for h in range(HL):
        marks = jnp.where(group == h, jnp.broadcast_to(total[:, h : h + 1], (HD, HD)), marks)
    st[0] = marks

    for h in range(HL):
        hc = slice(h * HD, (h + 1) * HD)
        run = jnp.zeros((HD, HD), F32)
        for j in range(NJ):
            keys = k_ref[j * SPAN : (j + 1) * SPAN, hc]
            k2[j, h, :, 0:HD] = keys
            k2[j, h, :, HD : 2 * HD] = keys
            keyf = keys.astype(F32)
            norm = lax.rsqrt(jnp.sum(keyf * keyf, axis=1, keepdims=True) + 1e-06)
            norms[j, h] = norm
            keyt = keyf.T.astype(BF16)
            kt2[j, h, :, 0:HD] = keyt
            kt2[j, h, :, HD : 2 * HD] = keyt
            fade = jnp.exp(closings[j][:, h : h + 1] - ccols[j][:, h : h + 1])
            gram = dot(kt2[j, h], stacked(keyf * (fade * norm * norm)))
            lb[j, h] = run
            run = jnp.exp(closings[j][:, h : h + 1]) * run + gram
        st[1 + h] = run

    pl.semaphore_wait(barrier, nz + ny + 1)

    def z_copy(src, dst, slot, step):
        to = y * nz + lax.rem(z + step, nz)
        return pltpu.make_async_remote_copy(
            src_ref=src, dst_ref=dst, send_sem=z_send.at[slot, step], recv_sem=z_recv.at[slot, step],
            device_id=(to, wide), device_id_type=MESH,
        )

    bands = ((0, HL + 1), (HL + 1, 2 * HL + 1))

    def scatter(band):
        lo, hi = bands[band]
        copies = []
        for step in range(1, nz):
            peer = lax.rem(z + step, nz)
            start = pl.multiple_of(peer * rows, rows)
            copies.append(z_copy(st.at[lo:hi, pl.ds(start, rows), :], buf1.at[z, lo:hi], band, step))
            copies[-1].start()
        mine = pl.multiple_of(z * rows, rows)
        buf1[z, lo:hi] = st[lo:hi, pl.ds(mine, rows), :]
        return copies

    sends = scatter(0)
    sent = list(sends)

    for h in range(HL):
        hc = slice(h * HD, (h + 1) * HD)
        run = jnp.zeros((HD, HD), F32)
        for j in range(NJ):
            keyf = k_ref[j * SPAN : (j + 1) * SPAN, hc].astype(F32)
            valt = v_ref[j * SPAN : (j + 1) * SPAN, hc].astype(F32).T.astype(BF16)
            vt2[j, h, :, 0:HD] = valt
            vt2[j, h, :, HD : 2 * HD] = valt
            fade = jnp.exp(closings[j][:, h : h + 1] - ccols[j][:, h : h + 1])
            memory = dot(vt2[j, h], stacked(keyf * (fade * norms[j, h])))
            lb[j, HL + h] = run
            run = jnp.exp(closings[j][:, h : h + 1]) * run + memory
        st[1 + HL + h] = run
    g_sends = scatter(1)
    sent += g_sends

    def row_total(band, copies):
        for copy in copies:
            copy.wait_recv()
        lo, hi = bands[band]
        first = 1 + band * HL
        sums = [jnp.zeros((rows, HD), F32) for _ in range(HL)]
        decay = jnp.zeros((8, HD), F32)
        for other in range(nz):
            marks = buf1[other, 0, 0:8, :]
            factor = jnp.exp(marks)
            decay = decay + marks
            for h in range(HL):
                sums[h] = factor[h : h + 1] * sums[h] + buf1[other, first + h]
        for h in range(HL):
            tot[y, first + h] = sums[h]
        if band == 0:
            tot[y, 0] = jnp.zeros((rows, HD), F32)
            tot[y, 0, 0:8, :] = decay
        copies = []
        for step in range(1, ny):
            to = lax.rem(y + step, ny) * nz + z
            copies.append(
                pltpu.make_async_remote_copy(
                    src_ref=tot.at[y, lo:hi], dst_ref=tot.at[y, lo:hi],
                    send_sem=y_send.at[band, step], recv_sem=y_recv.at[band, step],
                    device_id=(to, wide), device_id_type=MESH,
                )
            )
            copies[-1].start()
        return copies

    def give_back(band, copies):
        for copy in copies:
            copy.wait_recv()
        first = 1 + band * HL
        runs = [jnp.zeros((rows, HD), F32) for _ in range(HL)]
        for other in range(ny):
            factor = jnp.exp(tot[other, 0, 0:8, :])
            for h in range(HL):
                runs[h] = jnp.where(other < y, factor[h : h + 1] * runs[h] + tot[other, first + h], runs[h])
        for other in range(nz):
            factor = jnp.exp(buf1[other, 0, 0:8, :])
            for h in range(HL):
                buf2[other, band * HL + h] = runs[h]
                runs[h] = factor[h : h + 1] * runs[h] + buf1[other, first + h]
        lo, hi = band * HL, (band + 1) * HL
        mine = pl.multiple_of(z * rows, rows)
        copies = []
        for step in range(1, nz):
            peer = lax.rem(z + step, nz)
            copies.append(z_copy(buf2.at[peer, lo:hi], pre.at[lo:hi, pl.ds(mine, rows), :], 2 + band, step))
            copies[-1].start()
        pre[lo:hi, pl.ds(mine, rows), :] = buf2[z, lo:hi]
        return copies

    for h in range(HL):
        hc = slice(h * HD, (h + 1) * HD)
        ridge_m[h] = jnp.broadcast_to(ridge_ref[:, hc], (HD, HD)).T
        a1[h, 2 * HD : 3 * HD, HD : 2 * HD] = jnp.zeros((HD, HD), BF16)
        a2[h, 2 * HD : 3 * HD, HD : 2 * HD] = jnp.zeros((HD, HD), BF16)

    def weights_of(j):
        for h in range(HL):
            hc = slice(h * HD, (h + 1) * HD)
            lag = crow[j, h : h + 1, :] - ccols[j][:, h : h + 1]
            causal = place_r <= place_c
            weight = jnp.where(causal, jnp.exp(jnp.where(causal, lag, 0.0)), 0.0) * norms[j, h]
            w1[j, h] = weight
            w2[j, h] = weight * norms[j, h]
            query = q_ref[j * SPAN : (j + 1) * SPAN, hc].astype(F32).T
            qt[j, h] = query * lax.rsqrt(jnp.sum(query * query, axis=0, keepdims=True) + 1e-06)

    weights_of(0)
    weights_of(1)
    y_sends = row_total(0, sends)
    weights_of(2)
    back = give_back(0, y_sends)
    sent += y_sends + back
    y_sends = row_total(1, g_sends)
    weights_of(3)
    g_back = give_back(1, y_sends)
    sent += y_sends + g_back
    for copy in back:
        copy.wait_recv()

    def system(ref, j, h, state):
        high, low = parts(state)
        ref[h, 0:HD, :] = k2[j, h]
        ref[h, HD : 2 * HD, 0:HD] = high
        ref[h, HD : 2 * HD, HD : 2 * HD] = high
        ref[h, 2 * HD : 3 * HD, 0:HD] = low

    def solve(j):
        norm0, opening = [], []
        for h in range(HL):
            system(a1, j, h, sdec[j, h : h + 1, :] * pre[h] + lb[j, h])
            query = qt[j, h]
            xs[h] = jnp.zeros((HD, SPAN), F32)
            rs[h] = query
            ps[h] = query
            norm0.append(jnp.sum(query * query, axis=0, keepdims=True))
            opening.append(jnp.exp(crow[j, h : h + 1, :]))

        def sweep(_, norm):
            after = []
            for h in range(HL):
                direction = ps[h]
                out = dot(a1[h], stacked(direction))
                scores = out[0:HD] * w2[j, h]
                image = (
                    opening[h] * (out[HD : 2 * HD] + out[2 * HD : 3 * HD])
                    + dot(kt2[j, h], stacked(scores))
                    + ridge_m[h] * direction
                )
                alpha = norm[h] / jnp.sum(direction * image, axis=0, keepdims=True)
                xs[h] = xs[h] + alpha * direction
                residual = rs[h] - alpha * image
                fresh = jnp.sum(residual * residual, axis=0, keepdims=True)
                rs[h] = residual
                ps[h] = residual + (fresh / norm[h]) * direction
                after.append(fresh)
            return tuple(after)

        lax.fori_loop(0, ITERS, sweep, tuple(norm0))
        return opening

    def finish(j, opening):
        for h in range(HL):
            system(a2, j, h, sdec[j, h : h + 1, :] * pre[HL + h] + lb[j, HL + h])
            out = dot(a2[h], stacked(xs[h]))
            scores = out[0:HD] * w1[j, h]
            read = opening[h] * (out[HD : 2 * HD] + out[2 * HD : 3 * HD]) + dot(vt2[j, h], stacked(scores))
            read = read * lax.rsqrt(jnp.sum(read * read, axis=0, keepdims=True) * (1.0 / HD) + 1e-06)
            nm[:, h * HD : (h + 1) * HD] = read.T.astype(BF16)

    half = SPAN // 2
    width = w_vm.shape[1] // NCH

    def p_copy(k, n):
        return pltpu.make_async_remote_copy(
            src_ref=pout.at[k, n], dst_ref=pin.at[k, n], send_sem=p_send.at[k, n], recv_sem=p_recv.at[k, n],
            device_id=(seq, partner), device_id_type=MESH,
        )

    def project(k, first):
        mine = pl.multiple_of(c * half, half)
        other = pl.multiple_of((1 - c) * half, half)
        lhs = jnp.concatenate([nm[pl.ds(mine, half), :], nm[pl.ds(other, half), :]], axis=0)
        copies = {}
        for i in range(NCH):
            n = (first + i) % NCH
            out = dot(lhs, w_vm[:, n * width : (n + 1) * width])
            pown[k, n] = out[0:half]
            pout[k, n] = out[half:]
            copies[n] = p_copy(k, n)
            copies[n].start()
        return copies

    def x_copy(src, dst, send, recv, to):
        copy = pltpu.make_async_remote_copy(
            src_ref=src, dst_ref=dst, send_sem=send, recv_sem=recv,
            device_id=(seq, to), device_id_type=MESH,
        )
        copy.start()
        return copy

    middle = NCH // 2
    js = [lax.rem(x + o, nx) for o in ORDER]

    opening = solve(js[0])
    for copy in g_back:
        copy.wait_recv()
    finish(js[0], opening)
    load_w.wait()
    copies = project(0, 0)
    relay = {}
    for i in range(NCH):
        n = (i % 2) * middle + i // 2
        copies[n].wait_recv()
        pown[0, n] = pown[0, n] + pin[0, n]
        if n < middle:
            relay[n] = x_copy(pown.at[0, n], ra.at[n], r_send.at[n], r_recv.at[n], right)
        else:
            relay[n] = x_copy(pown.at[0, n], rb.at[n - middle], r_send.at[n], r_recv.at[n], left)
    sent += list(copies.values()) + list(relay.values())

    final1, final2 = {}, {}
    opening = solve(js[1])
    finish(js[1], opening)
    copies1 = project(1, middle)
    for n in range(middle, NCH):
        copies1[n].wait_recv()
        pown[1, n] = pown[1, n] + pin[1, n]
        final1[n] = x_copy(pown.at[1, n], f1.at[n], f_send.at[0, n], f_recv.at[0, n], right)
    opening = solve(js[2])
    finish(js[2], opening)
    copies2 = project(2, 0)
    for n in range(middle):
        copies2[n].wait_recv()
        pown[2, n] = pown[2, n] + pin[2, n]
        final2[n] = x_copy(pown.at[2, n], f2.at[n], f_send.at[1, n], f_recv.at[1, n], left)
    for n in range(middle):
        copies1[n].wait_recv()
        relay[n].wait_recv()
        pown[1, n] = pown[1, n] + pin[1, n] + ra[n]
        final1[n] = x_copy(pown.at[1, n], f1.at[n], f_send.at[0, n], f_recv.at[0, n], right)
        m = n + middle
        copies2[m].wait_recv()
        relay[m].wait_recv()
        pown[2, m] = pown[2, m] + pin[2, m] + rb[n]
        final2[m] = x_copy(pown.at[2, m], f2.at[m], f_send.at[1, m], f_recv.at[1, m], left)
    sent += list(copies1.values()) + list(copies2.values()) + list(final1.values()) + list(final2.values())

    opening = solve(js[3])
    finish(js[3], opening)
    copies3 = project(3, 0)
    sent += list(copies3.values())
    for n in range(NCH):
        copies3[n].wait_recv()
        pown[3, n] = pown[3, n] + pin[3, n]
    for i in range(NCH):
        n = (i % 2) * middle + i // 2
        m = (n + middle) % NCH
        final1[m].wait_recv()
        final2[n].wait_recv()
        if i % 2 == 1:
            for e in (n, m):
                o_ref[:, e * width : (e + 1) * width] = (pown[3, e] + f1[e] + f2[e]).astype(BF16)
    for copy in sent:
        copy.wait_send()


def solution(mesh, ny=4, nz=8):
    nx = mesh.shape["wide"] // 2

    def body(queries, keys, values, log_decay, ridge, out_weight):
        columns = out_weight.shape[1]
        width = columns // NCH
        half = SPAN // 2
        rows = HD // nz
        vm = pltpu.VMEM
        dma = pltpu.SemaphoreType.DMA
        scratch = [
            vm(out_weight.shape, BF16),
            vm((2 * HL + 1, HD, HD), F32),
            vm((nz, 2 * HL + 1, rows, HD), F32),
            vm((ny, 2 * HL + 1, rows, HD), F32),
            vm((nz, 2 * HL, rows, HD), F32),
            vm((2 * HL, HD, HD), F32),
            vm((NJ, 2 * HL, HD, HD), F32),
            vm((NJ, 8, HD), F32),
            vm((NJ, 8, HD), F32),
            vm((NJ, HL, SPAN, SPAN), F32),
            vm((NJ, HL, SPAN, SPAN), F32),
            vm((NJ, HL, SPAN, 2 * HD), BF16),
            vm((NJ, HL, HD, 2 * SPAN), BF16),
            vm((NJ, HL, HD, 2 * SPAN), BF16),
            vm((NJ, HL, HD, SPAN), F32),
            vm((HL, HD, SPAN), F32),
            vm((HL, 3 * HD, 2 * HD), BF16),
            vm((HL, 3 * HD, 2 * HD), BF16),
            vm((HL, HD, SPAN), F32),
            vm((HL, HD, SPAN), F32),
            vm((HL, HD, SPAN), F32),
            vm((SPAN, HL * HD), BF16),
            vm((NJ, NCH, half, width), F32),
            vm((NJ, NCH, half, width), F32),
            vm((NJ, NCH, half, width), F32),
            vm((NCH // 2, half, width), F32),
            vm((NCH // 2, half, width), F32),
            vm((NCH, half, width), F32),
            vm((NCH, half, width), F32),
            dma,
            dma((4, nz)),
            dma((4, nz)),
            dma((2, ny)),
            dma((2, ny)),
            dma((NJ, NCH)),
            dma((NJ, NCH)),
            dma((NCH,)),
            dma((NCH,)),
            dma((2, NCH)),
            dma((2, NCH)),
        ]
        space = pl.BlockSpec(memory_space=pltpu.VMEM)
        return pl.pallas_call(
            functools.partial(kernel, ny, nz, nx),
            out_shape=jax.ShapeDtypeStruct((queries.shape[0] // (2 * nx), columns), BF16),
            in_specs=[space] * 5 + [pl.BlockSpec(memory_space=pl.ANY)],
            out_specs=space,
            scratch_shapes=scratch,
            compiler_params=pltpu.CompilerParams(
                collective_id=0, has_side_effects=True, vmem_limit_bytes=60 << 20
            ),
        )(queries, keys, values, log_decay, ridge[None, :], out_weight)

    placed = (
        P("seq", "wide"),
        P("seq", "wide"),
        P("seq", "wide"),
        P("seq", "wide"),
        P("wide"),
        P("wide", None),
    )
    return jax.shard_map(
        body, mesh=mesh, in_specs=placed, out_specs=P(("seq", "wide"), None), check_vma=False
    )
```

```python
import functools

import jax
import jax.numpy as jnp
from jax import lax
from jax.experimental import pallas as pl
from jax.experimental.pallas import tpu as pltpu
from jax.sharding import PartitionSpec as P

MESH = pl.DeviceIdType.MESH
F32 = jnp.float32
BF16 = jnp.bfloat16
HD = 128
SPAN = 128
ITERS = 8
UNROLL = 2
HL = 4
NJ = 4
NCH = 8
ORDER = (2, 1, 3, 0)
highest = lax.Precision.HIGHEST


def parts(value):
    high = value.astype(BF16)
    return high, (value - high.astype(F32)).astype(BF16)


def stacked(value):
    return jnp.concatenate(parts(value), axis=0)


def dot(a, b):
    return jnp.dot(a, b, preferred_element_type=F32)


def kernel(
    ny, nz, nx,
    q_ref, k_ref, v_ref, ld_ref, ridge_ref, w_hbm, o_ref,
    w_vm, st, buf1, tot, buf2, pre, lb, sdec, crow, w1, w2, k2, kt2, vt2, qt, ridge_m,
    a1, a2, xs, rs, ps, nm, pown, pout, pin, ra, rb, f1, f2,
    w_sem, z_send, z_recv, y_send, y_recv, p_send, p_recv, r_send, r_recv, f_send, f_recv,
):
    seq = lax.axis_index("seq")
    wide = lax.axis_index("wide")
    y, z = lax.div(seq, nz), lax.rem(seq, nz)
    x, c = lax.div(wide, 2), lax.rem(wide, 2)
    rows = HD // nz
    partner = x * 2 + (1 - c)
    right = lax.rem(x + 1, nx) * 2 + c
    left = lax.rem(x + nx - 1, nx) * 2 + c

    load_w = pltpu.make_async_copy(w_hbm, w_vm, w_sem)
    load_w.start()

    barrier = pltpu.get_barrier_semaphore()
    for step in range(1, nz):
        to = y * nz + lax.rem(z + step, nz)
        pl.semaphore_signal(barrier, inc=1, device_id=(to, wide), device_id_type=MESH)
    for step in range(1, ny):
        to = lax.rem(y + step, ny) * nz + z
        pl.semaphore_signal(barrier, inc=1, device_id=(to, wide), device_id_type=MESH)
    for to in (partner, right, left):
        pl.semaphore_signal(barrier, inc=1, device_id=(seq, to), device_id_type=MESH)

    place_r = lax.broadcasted_iota(jnp.int32, (SPAN, SPAN), 0)
    place_c = lax.broadcasted_iota(jnp.int32, (SPAN, SPAN), 1)
    lower = (place_r >= place_c).astype(F32)
    upper = (place_r <= place_c).astype(F32)
    ccols, norms = [], {}
    total = jnp.zeros((1, HL), F32)
    closings = []
    for j in range(NJ):
        decay = ld_ref[j * SPAN : (j + 1) * SPAN, :]
        ccol = jnp.dot(lower, decay, precision=highest, preferred_element_type=F32)
        ccols.append(ccol)
        crow[j, 0:HL, :] = lax.dot_general(
            decay, upper, (((0,), (0,)), ((), ())), precision=highest, preferred_element_type=F32
        )
        for h in range(HL):
            sdec[j, h : h + 1, :] = jnp.exp(jnp.broadcast_to(total[:, h : h + 1], (1, HD)))
        closing = ccol[SPAN - 1 : SPAN, :]
        closings.append(closing)
        total = total + closing
    group = lax.rem(place_r, rows)
    marks = jnp.zeros((HD, HD), F32)
    for h in range(HL):
        marks = jnp.where(group == h, jnp.broadcast_to(total[:, h : h + 1], (HD, HD)), marks)
    st[0] = marks

    for h in range(HL):
        hc = slice(h * HD, (h + 1) * HD)
        run = jnp.zeros((HD, HD), F32)
        for j in range(NJ):
            keys = k_ref[j * SPAN : (j + 1) * SPAN, hc]
            k2[j, h, :, 0:HD] = keys
            k2[j, h, :, HD : 2 * HD] = keys
            keyf = keys.astype(F32)
            norm = lax.rsqrt(jnp.sum(keyf * keyf, axis=1, keepdims=True) + 1e-06)
            norms[j, h] = norm
            keyt = keyf.T.astype(BF16)
            kt2[j, h, :, 0:HD] = keyt
            kt2[j, h, :, HD : 2 * HD] = keyt
            fade = jnp.exp(closings[j][:, h : h + 1] - ccols[j][:, h : h + 1])
            gram = dot(kt2[j, h], stacked(keyf * (fade * norm * norm)))
            lb[j, h] = run
            run = jnp.exp(closings[j][:, h : h + 1]) * run + gram
        st[1 + h] = run

    pl.semaphore_wait(barrier, nz + ny + 1)

    def z_copy(src, dst, slot, step):
        to = y * nz + lax.rem(z + step, nz)
        return pltpu.make_async_remote_copy(
            src_ref=src, dst_ref=dst, send_sem=z_send.at[slot, step], recv_sem=z_recv.at[slot, step],
            device_id=(to, wide), device_id_type=MESH,
        )

    bands = ((0, HL + 1), (HL + 1, 2 * HL + 1))

    def scatter(band):
        lo, hi = bands[band]
        copies = []
        for step in range(1, nz):
            peer = lax.rem(z + step, nz)
            start = pl.multiple_of(peer * rows, rows)
            copies.append(z_copy(st.at[lo:hi, pl.ds(start, rows), :], buf1.at[z, lo:hi], band, step))
            copies[-1].start()
        mine = pl.multiple_of(z * rows, rows)
        buf1[z, lo:hi] = st[lo:hi, pl.ds(mine, rows), :]
        return copies

    sends = scatter(0)
    sent = list(sends)

    for h in range(HL):
        hc = slice(h * HD, (h + 1) * HD)
        run = jnp.zeros((HD, HD), F32)
        for j in range(NJ):
            keyf = k_ref[j * SPAN : (j + 1) * SPAN, hc].astype(F32)
            valt = v_ref[j * SPAN : (j + 1) * SPAN, hc].astype(F32).T.astype(BF16)
            vt2[j, h, :, 0:HD] = valt
            vt2[j, h, :, HD : 2 * HD] = valt
            fade = jnp.exp(closings[j][:, h : h + 1] - ccols[j][:, h : h + 1])
            memory = dot(vt2[j, h], stacked(keyf * (fade * norms[j, h])))
            lb[j, HL + h] = run
            run = jnp.exp(closings[j][:, h : h + 1]) * run + memory
        st[1 + HL + h] = run
    g_sends = scatter(1)
    sent += g_sends

    def row_total(band, copies):
        for copy in copies:
            copy.wait_recv()
        lo, hi = bands[band]
        first = 1 + band * HL
        sums = [jnp.zeros((rows, HD), F32) for _ in range(HL)]
        decay = jnp.zeros((8, HD), F32)
        for other in range(nz):
            marks = buf1[other, 0, 0:8, :]
            factor = jnp.exp(marks)
            decay = decay + marks
            for h in range(HL):
                sums[h] = factor[h : h + 1] * sums[h] + buf1[other, first + h]
        for h in range(HL):
            tot[y, first + h] = sums[h]
        if band == 0:
            tot[y, 0] = jnp.zeros((rows, HD), F32)
            tot[y, 0, 0:8, :] = decay
        copies = []
        for step in range(1, ny):
            to = lax.rem(y + step, ny) * nz + z
            copies.append(
                pltpu.make_async_remote_copy(
                    src_ref=tot.at[y, lo:hi], dst_ref=tot.at[y, lo:hi],
                    send_sem=y_send.at[band, step], recv_sem=y_recv.at[band, step],
                    device_id=(to, wide), device_id_type=MESH,
                )
            )
            copies[-1].start()
        return copies

    def give_back(band, copies):
        for copy in copies:
            copy.wait_recv()
        first = 1 + band * HL
        runs = [jnp.zeros((rows, HD), F32) for _ in range(HL)]
        for other in range(ny):
            factor = jnp.exp(tot[other, 0, 0:8, :])
            for h in range(HL):
                runs[h] = jnp.where(other < y, factor[h : h + 1] * runs[h] + tot[other, first + h], runs[h])
        for other in range(nz):
            factor = jnp.exp(buf1[other, 0, 0:8, :])
            for h in range(HL):
                buf2[other, band * HL + h] = runs[h]
                runs[h] = factor[h : h + 1] * runs[h] + buf1[other, first + h]
        lo, hi = band * HL, (band + 1) * HL
        mine = pl.multiple_of(z * rows, rows)
        copies = []
        for step in range(1, nz):
            peer = lax.rem(z + step, nz)
            copies.append(z_copy(buf2.at[peer, lo:hi], pre.at[lo:hi, pl.ds(mine, rows), :], 2 + band, step))
            copies[-1].start()
        pre[lo:hi, pl.ds(mine, rows), :] = buf2[z, lo:hi]
        return copies

    for h in range(HL):
        hc = slice(h * HD, (h + 1) * HD)
        ridge_m[h] = jnp.broadcast_to(ridge_ref[:, hc], (HD, HD)).T
        for i in range(2):
            a1[i * HL + h, 2 * HD : 3 * HD, HD : 2 * HD] = jnp.zeros((HD, HD), BF16)
            a2[i * HL + h, 2 * HD : 3 * HD, HD : 2 * HD] = jnp.zeros((HD, HD), BF16)

    def weights_of(j):
        for h in range(HL):
            hc = slice(h * HD, (h + 1) * HD)
            lag = crow[j, h : h + 1, :] - ccols[j][:, h : h + 1]
            causal = place_r <= place_c
            weight = jnp.where(causal, jnp.exp(jnp.where(causal, lag, 0.0)), 0.0) * norms[j, h]
            w1[j, h] = weight
            w2[j, h] = weight * norms[j, h]
            query = q_ref[j * SPAN : (j + 1) * SPAN, hc].astype(F32).T
            qt[j, h] = query * lax.rsqrt(jnp.sum(query * query, axis=0, keepdims=True) + 1e-06)

    weights_of(0)
    weights_of(1)
    y_sends = row_total(0, sends)
    weights_of(2)
    back = give_back(0, y_sends)
    sent += y_sends + back
    y_sends = row_total(1, g_sends)
    weights_of(3)
    g_back = give_back(1, y_sends)
    sent += y_sends + g_back
    for copy in back:
        copy.wait_recv()

    def system(ref, slot, j, h, state):
        high, low = parts(state)
        ref[slot, 0:HD, :] = k2[j, h]
        ref[slot, HD : 2 * HD, 0:HD] = high
        ref[slot, HD : 2 * HD, HD : 2 * HD] = high
        ref[slot, 2 * HD : 3 * HD, 0:HD] = low

    def blocks_of(spans):
        return [(i * HL + h, j, h) for i, j in enumerate(spans) for h in range(HL)]

    def solve(spans):
        blocks = blocks_of(spans)
        norm0, opening = [], []
        for slot, j, h in blocks:
            system(a1, slot, j, h, sdec[j, h : h + 1, :] * pre[h] + lb[j, h])
            query = qt[j, h]
            xs[slot] = jnp.zeros((HD, SPAN), F32)
            rs[slot] = query
            ps[slot] = query
            norm0.append(jnp.sum(query * query, axis=0, keepdims=True))
            opening.append(jnp.exp(crow[j, h : h + 1, :]))

        def sweep(_, norm):
            n = len(blocks)
            outs, locals_, after = [None] * n, [None] * n, [None] * n
            for i, (slot, j, h) in enumerate(blocks):
                outs[i] = dot(a1[slot], stacked(ps[slot]))
            for i, (slot, j, h) in enumerate(blocks):
                locals_[i] = dot(kt2[j, h], stacked(outs[i][0:HD] * w2[j, h]))
            for i, (slot, j, h) in enumerate(blocks):
                direction = ps[slot]
                carried = outs[i][HD : 2 * HD] + outs[i][2 * HD : 3 * HD]
                image = opening[i] * carried + locals_[i] + ridge_m[h] * direction
                alpha = norm[i] / jnp.sum(direction * image, axis=0, keepdims=True)
                xs[slot] = xs[slot] + alpha * direction
                residual = rs[slot] - alpha * image
                fresh = jnp.sum(residual * residual, axis=0, keepdims=True)
                rs[slot] = residual
                ps[slot] = residual + (fresh / norm[i]) * direction
                after[i] = fresh
            return tuple(after)

        lax.fori_loop(0, ITERS, sweep, tuple(norm0), unroll=UNROLL)
        return opening

    def finish(k, i, j, opening):
        outs = []
        for h in range(HL):
            slot = i * HL + h
            system(a2, slot, j, h, sdec[j, h : h + 1, :] * pre[HL + h] + lb[j, HL + h])
        for h in range(HL):
            slot = i * HL + h
            outs.append(dot(a2[slot], stacked(xs[slot])))
        reads = []
        for h in range(HL):
            reads.append(dot(vt2[j, h], stacked(outs[h][0:HD] * w1[j, h])))
        for h in range(HL):
            read = opening[i * HL + h] * (outs[h][HD : 2 * HD] + outs[h][2 * HD : 3 * HD]) + reads[h]
            read = read * lax.rsqrt(jnp.sum(read * read, axis=0, keepdims=True) * (1.0 / HD) + 1e-06)
            nm[k, :, h * HD : (h + 1) * HD] = read.T.astype(BF16)

    half = SPAN // 2
    width = w_vm.shape[1] // NCH

    def p_copy(k, n):
        return pltpu.make_async_remote_copy(
            src_ref=pout.at[k, n], dst_ref=pin.at[k, n], send_sem=p_send.at[k, n], recv_sem=p_recv.at[k, n],
            device_id=(seq, partner), device_id_type=MESH,
        )

    def project(k, first):
        mine = pl.multiple_of(c * half, half)
        other = pl.multiple_of((1 - c) * half, half)
        lhs = jnp.concatenate([nm[k, pl.ds(mine, half), :], nm[k, pl.ds(other, half), :]], axis=0)
        copies = {}
        for i in range(NCH):
            n = (first + i) % NCH
            out = dot(lhs, w_vm[:, n * width : (n + 1) * width])
            pown[k, n] = out[0:half]
            pout[k, n] = out[half:]
            copies[n] = p_copy(k, n)
            copies[n].start()
        return copies

    def x_copy(src, dst, send, recv, to):
        copy = pltpu.make_async_remote_copy(
            src_ref=src, dst_ref=dst, send_sem=send, recv_sem=recv,
            device_id=(seq, to), device_id_type=MESH,
        )
        copy.start()
        return copy

    middle = NCH // 2
    js = [lax.rem(x + o, nx) for o in ORDER]

    opening = solve(js[0:1])
    for copy in g_back:
        copy.wait_recv()
    finish(0, 0, js[0], opening)
    load_w.wait()
    copies = project(0, 0)
    relay = {}
    for i in range(NCH):
        n = (i % 2) * middle + i // 2
        copies[n].wait_recv()
        pown[0, n] = pown[0, n] + pin[0, n]
        if n < middle:
            relay[n] = x_copy(pown.at[0, n], ra.at[n], r_send.at[n], r_recv.at[n], right)
        else:
            relay[n] = x_copy(pown.at[0, n], rb.at[n - middle], r_send.at[n], r_recv.at[n], left)
    sent += list(copies.values()) + list(relay.values())

    final1, final2 = {}, {}
    opening = solve(js[1:3])
    finish(1, 0, js[1], opening)
    copies1 = project(1, middle)
    finish(2, 1, js[2], opening)
    copies2 = project(2, 0)
    for n in range(middle):
        m = n + middle
        copies1[m].wait_recv()
        pown[1, m] = pown[1, m] + pin[1, m]
        final1[m] = x_copy(pown.at[1, m], f1.at[m], f_send.at[0, m], f_recv.at[0, m], right)
        copies2[n].wait_recv()
        pown[2, n] = pown[2, n] + pin[2, n]
        final2[n] = x_copy(pown.at[2, n], f2.at[n], f_send.at[1, n], f_recv.at[1, n], left)
    for n in range(middle):
        copies1[n].wait_recv()
        relay[n].wait_recv()
        pown[1, n] = pown[1, n] + pin[1, n] + ra[n]
        final1[n] = x_copy(pown.at[1, n], f1.at[n], f_send.at[0, n], f_recv.at[0, n], right)
        m = n + middle
        copies2[m].wait_recv()
        relay[m].wait_recv()
        pown[2, m] = pown[2, m] + pin[2, m] + rb[n]
        final2[m] = x_copy(pown.at[2, m], f2.at[m], f_send.at[1, m], f_recv.at[1, m], left)
    sent += list(copies1.values()) + list(copies2.values()) + list(final1.values()) + list(final2.values())

    opening = solve(js[3:4])
    finish(3, 0, js[3], opening)
    copies3 = project(3, 0)
    sent += list(copies3.values())
    for n in range(NCH):
        copies3[n].wait_recv()
        pown[3, n] = pown[3, n] + pin[3, n]
    for i in range(NCH):
        n = (i % 2) * middle + i // 2
        m = (n + middle) % NCH
        final1[m].wait_recv()
        final2[n].wait_recv()
        if i % 2 == 1:
            for e in (n, m):
                o_ref[:, e * width : (e + 1) * width] = (pown[3, e] + f1[e] + f2[e]).astype(BF16)
    for copy in sent:
        copy.wait_send()


def solution(mesh, ny=4, nz=8):
    nx = mesh.shape["wide"] // 2

    def body(queries, keys, values, log_decay, ridge, out_weight):
        columns = out_weight.shape[1]
        width = columns // NCH
        half = SPAN // 2
        rows = HD // nz
        vm = pltpu.VMEM
        dma = pltpu.SemaphoreType.DMA
        scratch = [
            vm(out_weight.shape, BF16),
            vm((2 * HL + 1, HD, HD), F32),
            vm((nz, 2 * HL + 1, rows, HD), F32),
            vm((ny, 2 * HL + 1, rows, HD), F32),
            vm((nz, 2 * HL, rows, HD), F32),
            vm((2 * HL, HD, HD), F32),
            vm((NJ, 2 * HL, HD, HD), F32),
            vm((NJ, 8, HD), F32),
            vm((NJ, 8, HD), F32),
            vm((NJ, HL, SPAN, SPAN), F32),
            vm((NJ, HL, SPAN, SPAN), F32),
            vm((NJ, HL, SPAN, 2 * HD), BF16),
            vm((NJ, HL, HD, 2 * SPAN), BF16),
            vm((NJ, HL, HD, 2 * SPAN), BF16),
            vm((NJ, HL, HD, SPAN), F32),
            vm((HL, HD, SPAN), F32),
            vm((2 * HL, 3 * HD, 2 * HD), BF16),
            vm((2 * HL, 3 * HD, 2 * HD), BF16),
            vm((2 * HL, HD, SPAN), F32),
            vm((2 * HL, HD, SPAN), F32),
            vm((2 * HL, HD, SPAN), F32),
            vm((NJ, SPAN, HL * HD), BF16),
            vm((NJ, NCH, half, width), F32),
            vm((NJ, NCH, half, width), F32),
            vm((NJ, NCH, half, width), F32),
            vm((NCH // 2, half, width), F32),
            vm((NCH // 2, half, width), F32),
            vm((NCH, half, width), F32),
            vm((NCH, half, width), F32),
            dma,
            dma((4, nz)),
            dma((4, nz)),
            dma((2, ny)),
            dma((2, ny)),
            dma((NJ, NCH)),
            dma((NJ, NCH)),
            dma((NCH,)),
            dma((NCH,)),
            dma((2, NCH)),
            dma((2, NCH)),
        ]
        space = pl.BlockSpec(memory_space=pltpu.VMEM)
        return pl.pallas_call(
            functools.partial(kernel, ny, nz, nx),
            out_shape=jax.ShapeDtypeStruct((queries.shape[0] // (2 * nx), columns), BF16),
            in_specs=[space] * 5 + [pl.BlockSpec(memory_space=pl.ANY)],
            out_specs=space,
            scratch_shapes=scratch,
            compiler_params=pltpu.CompilerParams(
                collective_id=0, has_side_effects=True, vmem_limit_bytes=60 << 20
            ),
        )(queries, keys, values, log_decay, ridge[None, :], out_weight)

    placed = (
        P("seq", "wide"),
        P("seq", "wide"),
        P("seq", "wide"),
        P("seq", "wide"),
        P("wide"),
        P("wide", None),
    )
    return jax.shard_map(
        body, mesh=mesh, in_specs=placed, out_specs=P(("seq", "wide"), None), check_vma=False
    )
```

```python
import functools

import jax
import jax.numpy as jnp
from jax import lax
from jax.experimental import pallas as pl
from jax.experimental.pallas import tpu as pltpu
from jax.sharding import PartitionSpec as P

MESH = pl.DeviceIdType.MESH
F32 = jnp.float32
BF16 = jnp.bfloat16
HD = 128
SPAN = 128
ITERS = 8
UNROLL = 2
HL = 4
NJ = 4
NCH = 8
ORDER = (2, 1, 3, 0)
highest = lax.Precision.HIGHEST


def parts(value):
    high = value.astype(BF16)
    return high, (value - high.astype(F32)).astype(BF16)


def stacked(value):
    return jnp.concatenate(parts(value), axis=0)


def dot(a, b):
    return jnp.dot(a, b, preferred_element_type=F32)


def kernel(
    ny, nz, nx,
    q_hbm, k_hbm, v_hbm, ld_hbm, ridge_hbm, w_hbm, o_ref,
    q_ref, k_ref, v_ref, ld_ref, ridge_ref, w_vm,
    st_h, st_g, buf_h, buf_g, tot_h, tot_g, out_h, out_g, pre_h, pre, lb, sdec, crow, w1, w2, k2, kt2, vt2, qt, ridge_m,
    gram_in, a1, a2, xs, rs, ps, nm, pown, pout, pin, ra, rb, f1, f2,
    load_sem, z_send, z_recv, y_send, y_recv, p_send, p_recv, r_send, r_recv, f_send, f_recv,
):
    seq = lax.axis_index("seq")
    wide = lax.axis_index("wide")
    y, z = lax.div(seq, nz), lax.rem(seq, nz)
    x, c = lax.div(wide, 2), lax.rem(wide, 2)
    rows_h, rows_g = HD // 2 // nz, HD // nz
    partner = x * 2 + (1 - c)
    right = lax.rem(x + 1, nx) * 2 + c
    left = lax.rem(x + nx - 1, nx) * 2 + c

    loads = [
        pltpu.make_async_copy(src, dst, load_sem.at[i])
        for i, (src, dst) in enumerate(
            (
                (ld_hbm, ld_ref), (k_hbm, k_ref), (v_hbm, v_ref),
                (q_hbm, q_ref), (ridge_hbm, ridge_ref), (w_hbm, w_vm),
            )
        )
    ]
    for load in loads[:5]:
        load.start()

    barrier = pltpu.get_barrier_semaphore()
    for step in range(1, nz):
        to = y * nz + lax.rem(z + step, nz)
        pl.semaphore_signal(barrier, inc=1, device_id=(to, wide), device_id_type=MESH)
    for step in range(1, ny):
        to = lax.rem(y + step, ny) * nz + z
        pl.semaphore_signal(barrier, inc=1, device_id=(to, wide), device_id_type=MESH)
    for to in (partner, right, left):
        pl.semaphore_signal(barrier, inc=1, device_id=(seq, to), device_id_type=MESH)

    place_r = lax.broadcasted_iota(jnp.int32, (SPAN, SPAN), 0)
    place_c = lax.broadcasted_iota(jnp.int32, (SPAN, SPAN), 1)
    lower = (place_r >= place_c).astype(F32)
    upper = (place_r <= place_c).astype(F32)
    ccols, norms = [], {}
    loads[0].wait()
    total = jnp.zeros((1, HL), F32)
    closings = []
    for j in range(NJ):
        decay = ld_ref[:, j * SPAN : (j + 1) * SPAN]
        ccol = lax.dot_general(
            lower, decay, (((1,), (1,)), ((), ())), precision=highest, preferred_element_type=F32
        )
        ccols.append(ccol)
        crow[j, 0:HL, :] = jnp.dot(decay, upper, precision=highest, preferred_element_type=F32)
        for h in range(HL):
            sdec[j, h : h + 1, :] = jnp.exp(jnp.broadcast_to(total[:, h : h + 1], (1, HD)))
        closing = ccol[SPAN - 1 : SPAN, :]
        closings.append(closing)
        total = total + closing
    group = lax.rem(lax.broadcasted_iota(jnp.int32, (HD // 2, HD), 0), rows_h)
    near = lax.rem(place_c - place_r + HD, HD)
    keep = near[0 : HD // 2] < HD // 2
    marks = jnp.zeros((HD // 2, HD), F32)
    loads[1].wait()

    for h in range(HL):
        hc = slice(h * HD, (h + 1) * HD)
        run = jnp.zeros((HD, HD), F32)
        for j in range(NJ):
            keys = k_ref[j * SPAN : (j + 1) * SPAN, hc]
            k2[j, h, :, 0:HD] = keys
            k2[j, h, :, HD : 2 * HD] = keys
            keyf = keys.astype(F32)
            norm = lax.rsqrt(jnp.sum(keyf * keyf, axis=1, keepdims=True) + 1e-06)
            norms[j, h] = norm
            keyt = keyf.T.astype(BF16)
            kt2[j, h, :, 0:HD] = keyt
            kt2[j, h, :, HD : 2 * HD] = keyt
            fade = jnp.exp(closings[j][:, h : h + 1] - ccols[j][:, h : h + 1])
            gram = dot(kt2[j, h], stacked(keyf * (fade * norm * norm)))
            lb[j, h] = run
            run = jnp.exp(closings[j][:, h : h + 1]) * run + gram
        st_h[1 + h] = jnp.where(keep, run[0 : HD // 2], run[HD // 2 :])
        edge = jnp.sum(jnp.where(near == HD // 2, run, 0.0), axis=0, keepdims=True)
        marks = jnp.where(group == h, jnp.broadcast_to(total[:, h : h + 1], marks.shape), marks)
        marks = jnp.where(group == HL + h, edge, marks)
    st_h[0] = marks

    pl.semaphore_wait(barrier, nz + ny + 1)

    def z_copy(src, dst, slot, step):
        to = y * nz + lax.rem(z + step, nz)
        return pltpu.make_async_remote_copy(
            src_ref=src, dst_ref=dst, send_sem=z_send.at[slot, step], recv_sem=z_recv.at[slot, step],
            device_id=(to, wide), device_id_type=MESH,
        )

    def scatter(st, buf, slot, rows):
        copies = []
        for step in range(1, nz):
            peer = lax.rem(z + step, nz)
            start = pl.multiple_of(peer * rows, rows)
            copies.append(z_copy(st.at[:, pl.ds(start, rows), :], buf.at[z], slot, step))
            copies[-1].start()
        mine = pl.multiple_of(z * rows, rows)
        buf[z] = st[:, pl.ds(mine, rows), :]
        return copies

    sends = scatter(st_h, buf_h, 0, rows_h)
    sent = list(sends)
    loads[2].wait()

    for h in range(HL):
        hc = slice(h * HD, (h + 1) * HD)
        run = jnp.zeros((HD, HD), F32)
        for j in range(NJ):
            keyf = k_ref[j * SPAN : (j + 1) * SPAN, hc].astype(F32)
            valt = v_ref[j * SPAN : (j + 1) * SPAN, hc].astype(F32).T.astype(BF16)
            vt2[j, h, :, 0:HD] = valt
            vt2[j, h, :, HD : 2 * HD] = valt
            fade = jnp.exp(closings[j][:, h : h + 1] - ccols[j][:, h : h + 1])
            memory = dot(vt2[j, h], stacked(keyf * (fade * norms[j, h])))
            lb[j, HL + h] = run
            run = jnp.exp(closings[j][:, h : h + 1]) * run + memory
        st_g[h] = run
    g_sends = scatter(st_g, buf_g, 1, rows_g)

    def y_copies(buf, slot):
        copies = []
        for step in range(1, ny):
            to = lax.rem(y + step, ny) * nz + z
            copies.append(
                pltpu.make_async_remote_copy(
                    src_ref=buf.at[y], dst_ref=buf.at[y],
                    send_sem=y_send.at[slot, step], recv_sem=y_recv.at[slot, step],
                    device_id=(to, wide), device_id_type=MESH,
                )
            )
            copies[-1].start()
        return copies

    def give_back(buf, pre, slot, rows):
        mine = pl.multiple_of(z * rows, rows)
        copies = []
        for step in range(1, nz):
            peer = lax.rem(z + step, nz)
            copies.append(z_copy(buf.at[peer], pre.at[:, pl.ds(mine, rows), :], slot, step))
            copies[-1].start()
        pre[:, pl.ds(mine, rows), :] = buf[z]
        return copies

    def total_h(copies):
        for copy in copies:
            copy.wait_recv()
        sums = [jnp.zeros((rows_h, HD), F32) for _ in range(HL)]
        edges = [jnp.zeros((1, HD), F32) for _ in range(HL)]
        decay = jnp.zeros((8, HD), F32)
        for other in range(nz):
            marks = buf_h[other, 0, 0:8, :]
            factor = jnp.exp(marks[0:HL])
            decay = decay + marks
            for h in range(HL):
                sums[h] = factor[h : h + 1] * sums[h] + buf_h[other, 1 + h]
                edges[h] = factor[h : h + 1] * edges[h] + marks[HL + h : HL + h + 1]
        tot_h[y, 0, 0:8, :] = decay
        for h in range(HL):
            tot_h[y, 1 + h] = sums[h]
            tot_h[y, 0, HL + h : HL + h + 1, :] = edges[h]
        return y_copies(tot_h, 0)

    def prefix_h(copies):
        for copy in copies:
            copy.wait_recv()
        runs = [jnp.zeros((rows_h, HD), F32) for _ in range(HL)]
        edges = [jnp.zeros((1, HD), F32) for _ in range(HL)]
        for other in range(ny):
            marks = tot_h[other, 0, 0:8, :]
            factor = jnp.exp(marks[0:HL])
            for h in range(HL):
                runs[h] = jnp.where(other < y, factor[h : h + 1] * runs[h] + tot_h[other, 1 + h], runs[h])
                edges[h] = jnp.where(
                    other < y, factor[h : h + 1] * edges[h] + marks[HL + h : HL + h + 1], edges[h]
                )
        for other in range(nz):
            marks = buf_h[other, 0, 0:8, :]
            factor = jnp.exp(marks[0:HL])
            for h in range(HL):
                out_h[other, 1 + h] = runs[h]
                out_h[other, 0, HL + h : HL + h + 1, :] = edges[h]
                runs[h] = factor[h : h + 1] * runs[h] + buf_h[other, 1 + h]
                edges[h] = factor[h : h + 1] * edges[h] + marks[HL + h : HL + h + 1]
        return give_back(out_h, pre_h, 2, rows_h)

    def total_g(copies):
        for copy in copies:
            copy.wait_recv()
        sums = [jnp.zeros((rows_g, HD), F32) for _ in range(HL)]
        for other in range(nz):
            factor = jnp.exp(buf_h[other, 0, 0:HL, :])
            for h in range(HL):
                sums[h] = factor[h : h + 1] * sums[h] + buf_g[other, h]
        for h in range(HL):
            tot_g[y, h] = sums[h]
        return y_copies(tot_g, 1)

    def prefix_g(copies):
        for copy in copies:
            copy.wait_recv()
        runs = [jnp.zeros((rows_g, HD), F32) for _ in range(HL)]
        for other in range(ny):
            factor = jnp.exp(tot_h[other, 0, 0:HL, :])
            for h in range(HL):
                runs[h] = jnp.where(other < y, factor[h : h + 1] * runs[h] + tot_g[other, h], runs[h])
        for other in range(nz):
            factor = jnp.exp(buf_h[other, 0, 0:HL, :])
            for h in range(HL):
                out_g[other, h] = runs[h]
                runs[h] = factor[h : h + 1] * runs[h] + buf_g[other, h]
        return give_back(out_g, pre, 3, rows_g)

    loads[3].wait()
    loads[4].wait()
    loads[5].start()
    out_h[:, 0] = jnp.zeros((nz, rows_h, HD), F32)
    for h in range(HL):
        hc = slice(h * HD, (h + 1) * HD)
        ridge_m[h] = jnp.broadcast_to(ridge_ref[:, hc], (HD, HD)).T
        for i in range(2):
            a1[i * HL + h, 2 * HD : 3 * HD, HD : 2 * HD] = jnp.zeros((HD, HD), BF16)
            a2[i * HL + h, 2 * HD : 3 * HD, HD : 2 * HD] = jnp.zeros((HD, HD), BF16)

    def weights_of(j):
        for h in range(HL):
            hc = slice(h * HD, (h + 1) * HD)
            lag = crow[j, h : h + 1, :] - ccols[j][:, h : h + 1]
            causal = place_r <= place_c
            weight = jnp.where(causal, jnp.exp(jnp.where(causal, lag, 0.0)), 0.0) * norms[j, h]
            w1[j, h] = weight
            w2[j, h] = weight * norms[j, h]
            query = q_ref[j * SPAN : (j + 1) * SPAN, hc].astype(F32).T
            qt[j, h] = query * lax.rsqrt(jnp.sum(query * query, axis=0, keepdims=True) + 1e-06)

    weights_of(0)
    weights_of(1)
    y_sends = total_h(sends)
    sent += y_sends
    weights_of(2)
    back = prefix_h(y_sends)
    sent += back
    weights_of(3)
    y_sends = total_g(g_sends)
    sent += y_sends + g_sends
    g_back = prefix_g(y_sends)
    sent += g_back
    for copy in back:
        copy.wait_recv()
    for h in range(HL):
        packed = pre_h[1 + h]
        spread = jnp.concatenate([jnp.where(keep, packed, 0.0), jnp.where(keep, 0.0, packed)], axis=0)
        both = jnp.where(near == 0, spread, spread + spread.T)
        gram_in[h] = jnp.where(near == HD // 2, pre_h[0, HL + h : HL + h + 1, :], both)

    def system(ref, slot, j, h, state):
        high, low = parts(state)
        ref[slot, 0:HD, :] = k2[j, h]
        ref[slot, HD : 2 * HD, 0:HD] = high
        ref[slot, HD : 2 * HD, HD : 2 * HD] = high
        ref[slot, 2 * HD : 3 * HD, 0:HD] = low

    def blocks_of(spans):
        return [(i * HL + h, j, h) for i, j in enumerate(spans) for h in range(HL)]

    def solve(spans):
        blocks = blocks_of(spans)
        norm0, opening = [], []
        for slot, j, h in blocks:
            system(a1, slot, j, h, sdec[j, h : h + 1, :] * gram_in[h] + lb[j, h])
            query = qt[j, h]
            xs[slot] = jnp.zeros((HD, SPAN), F32)
            rs[slot] = query
            ps[slot] = query
            norm0.append(jnp.sum(query * query, axis=0, keepdims=True))
            opening.append(jnp.exp(crow[j, h : h + 1, :]))

        def sweep(_, norm):
            n = len(blocks)
            outs, locals_, after = [None] * n, [None] * n, [None] * n
            for i, (slot, j, h) in enumerate(blocks):
                outs[i] = dot(a1[slot], stacked(ps[slot]))
            for i, (slot, j, h) in enumerate(blocks):
                locals_[i] = dot(kt2[j, h], stacked(outs[i][0:HD] * w2[j, h]))
            for i, (slot, j, h) in enumerate(blocks):
                direction = ps[slot]
                carried = outs[i][HD : 2 * HD] + outs[i][2 * HD : 3 * HD]
                image = opening[i] * carried + locals_[i] + ridge_m[h] * direction
                alpha = norm[i] / jnp.sum(direction * image, axis=0, keepdims=True)
                xs[slot] = xs[slot] + alpha * direction
                residual = rs[slot] - alpha * image
                fresh = jnp.sum(residual * residual, axis=0, keepdims=True)
                rs[slot] = residual
                ps[slot] = residual + (fresh / norm[i]) * direction
                after[i] = fresh
            return tuple(after)

        lax.fori_loop(0, ITERS, sweep, tuple(norm0), unroll=UNROLL)
        return opening

    def finish(k, i, j, opening):
        outs = []
        for h in range(HL):
            slot = i * HL + h
            system(a2, slot, j, h, sdec[j, h : h + 1, :] * pre[h] + lb[j, HL + h])
        for h in range(HL):
            slot = i * HL + h
            outs.append(dot(a2[slot], stacked(xs[slot])))
        reads = []
        for h in range(HL):
            reads.append(dot(vt2[j, h], stacked(outs[h][0:HD] * w1[j, h])))
        for h in range(HL):
            read = opening[i * HL + h] * (outs[h][HD : 2 * HD] + outs[h][2 * HD : 3 * HD]) + reads[h]
            read = read * lax.rsqrt(jnp.sum(read * read, axis=0, keepdims=True) * (1.0 / HD) + 1e-06)
            nm[k, :, h * HD : (h + 1) * HD] = read.T.astype(BF16)

    half = SPAN // 2
    width = w_vm.shape[1] // NCH

    def p_copy(k, n):
        return pltpu.make_async_remote_copy(
            src_ref=pout.at[k, n], dst_ref=pin.at[k, n], send_sem=p_send.at[k, n], recv_sem=p_recv.at[k, n],
            device_id=(seq, partner), device_id_type=MESH,
        )

    def project(k, first):
        mine = pl.multiple_of(c * half, half)
        other = pl.multiple_of((1 - c) * half, half)
        lhs = jnp.concatenate([nm[k, pl.ds(mine, half), :], nm[k, pl.ds(other, half), :]], axis=0)
        copies = {}
        for i in range(NCH):
            n = (first + i) % NCH
            out = dot(lhs, w_vm[:, n * width : (n + 1) * width])
            pown[k, n] = out[0:half]
            pout[k, n] = out[half:]
            copies[n] = p_copy(k, n)
            copies[n].start()
        return copies

    def x_copy(src, dst, send, recv, to):
        copy = pltpu.make_async_remote_copy(
            src_ref=src, dst_ref=dst, send_sem=send, recv_sem=recv,
            device_id=(seq, to), device_id_type=MESH,
        )
        copy.start()
        return copy

    middle = NCH // 2
    js = [lax.rem(x + o, nx) for o in ORDER]

    opening = solve(js[0:1])
    for copy in g_back:
        copy.wait_recv()
    finish(0, 0, js[0], opening)
    loads[5].wait()
    copies = project(0, 0)
    relay = {}
    for i in range(NCH):
        n = (i % 2) * middle + i // 2
        copies[n].wait_recv()
        pown[0, n] = pown[0, n] + pin[0, n]
        if n < middle:
            relay[n] = x_copy(pown.at[0, n], ra.at[n], r_send.at[n], r_recv.at[n], right)
        else:
            relay[n] = x_copy(pown.at[0, n], rb.at[n - middle], r_send.at[n], r_recv.at[n], left)
    sent += list(copies.values()) + list(relay.values())

    final1, final2 = {}, {}
    opening = solve(js[1:3])
    finish(1, 0, js[1], opening)
    copies1 = project(1, middle)
    finish(2, 1, js[2], opening)
    copies2 = project(2, 0)
    for n in range(middle):
        m = n + middle
        copies1[m].wait_recv()
        pown[1, m] = pown[1, m] + pin[1, m]
        final1[m] = x_copy(pown.at[1, m], f1.at[m], f_send.at[0, m], f_recv.at[0, m], right)
        copies2[n].wait_recv()
        pown[2, n] = pown[2, n] + pin[2, n]
        final2[n] = x_copy(pown.at[2, n], f2.at[n], f_send.at[1, n], f_recv.at[1, n], left)
    for n in range(middle):
        copies1[n].wait_recv()
        relay[n].wait_recv()
        pown[1, n] = pown[1, n] + pin[1, n] + ra[n]
        final1[n] = x_copy(pown.at[1, n], f1.at[n], f_send.at[0, n], f_recv.at[0, n], right)
        m = n + middle
        copies2[m].wait_recv()
        relay[m].wait_recv()
        pown[2, m] = pown[2, m] + pin[2, m] + rb[n]
        final2[m] = x_copy(pown.at[2, m], f2.at[m], f_send.at[1, m], f_recv.at[1, m], left)
    sent += list(copies1.values()) + list(copies2.values()) + list(final1.values()) + list(final2.values())

    opening = solve(js[3:4])
    finish(3, 0, js[3], opening)
    copies3 = project(3, 0)
    sent += list(copies3.values())
    for n in range(NCH):
        copies3[n].wait_recv()
        pown[3, n] = pown[3, n] + pin[3, n]
    for i in range(NCH):
        n = (i % 2) * middle + i // 2
        m = (n + middle) % NCH
        final1[m].wait_recv()
        final2[n].wait_recv()
        if i % 2 == 1:
            for e in (n, m):
                o_ref[:, e * width : (e + 1) * width] = (pown[3, e] + f1[e] + f2[e]).astype(BF16)
    for copy in sent:
        copy.wait_send()


def solution(mesh, ny=4, nz=8):
    nx = mesh.shape["wide"] // 2

    def body(queries, keys, values, log_decay, ridge, out_weight):
        columns = out_weight.shape[1]
        width = columns // NCH
        half = SPAN // 2
        rows_h, rows_g = HD // 2 // nz, HD // nz
        tokens, inner = queries.shape
        vm = pltpu.VMEM
        dma = pltpu.SemaphoreType.DMA
        scratch = [
            vm((tokens, inner), BF16),
            vm((tokens, inner), BF16),
            vm((tokens, inner), BF16),
            vm((HL, tokens), F32),
            vm((1, inner), F32),
            vm(out_weight.shape, BF16),
            vm((HL + 1, HD // 2, HD), F32),
            vm((HL, HD, HD), F32),
            vm((nz, HL + 1, rows_h, HD), F32),
            vm((nz, HL, rows_g, HD), F32),
            vm((ny, HL + 1, rows_h, HD), F32),
            vm((ny, HL, rows_g, HD), F32),
            vm((nz, HL + 1, rows_h, HD), F32),
            vm((nz, HL, rows_g, HD), F32),
            vm((HL + 1, HD // 2, HD), F32),
            vm((HL, HD, HD), F32),
            vm((NJ, 2 * HL, HD, HD), F32),
            vm((NJ, 8, HD), F32),
            vm((NJ, 8, HD), F32),
            vm((NJ, HL, SPAN, SPAN), F32),
            vm((NJ, HL, SPAN, SPAN), F32),
            vm((NJ, HL, SPAN, 2 * HD), BF16),
            vm((NJ, HL, HD, 2 * SPAN), BF16),
            vm((NJ, HL, HD, 2 * SPAN), BF16),
            vm((NJ, HL, HD, SPAN), F32),
            vm((HL, HD, SPAN), F32),
            vm((HL, HD, HD), F32),
            vm((2 * HL, 3 * HD, 2 * HD), BF16),
            vm((2 * HL, 3 * HD, 2 * HD), BF16),
            vm((2 * HL, HD, SPAN), F32),
            vm((2 * HL, HD, SPAN), F32),
            vm((2 * HL, HD, SPAN), F32),
            vm((NJ, SPAN, HL * HD), BF16),
            vm((NJ, NCH, half, width), F32),
            vm((NJ, NCH, half, width), F32),
            vm((NJ, NCH, half, width), F32),
            vm((NCH // 2, half, width), F32),
            vm((NCH // 2, half, width), F32),
            vm((NCH, half, width), F32),
            vm((NCH, half, width), F32),
            dma((6,)),
            dma((4, nz)),
            dma((4, nz)),
            dma((2, ny)),
            dma((2, ny)),
            dma((NJ, NCH)),
            dma((NJ, NCH)),
            dma((NCH,)),
            dma((NCH,)),
            dma((2, NCH)),
            dma((2, NCH)),
        ]
        space = pl.BlockSpec(memory_space=pltpu.VMEM)
        return pl.pallas_call(
            functools.partial(kernel, ny, nz, nx),
            out_shape=jax.ShapeDtypeStruct((queries.shape[0] // (2 * nx), columns), BF16),
            in_specs=[pl.BlockSpec(memory_space=pl.ANY)] * 6,
            out_specs=space,
            scratch_shapes=scratch,
            compiler_params=pltpu.CompilerParams(
                collective_id=0, has_side_effects=True, vmem_limit_bytes=60 << 20
            ),
        )(queries, keys, values, log_decay.T, ridge[None, :], out_weight)

    placed = (
        P("seq", "wide"),
        P("seq", "wide"),
        P("seq", "wide"),
        P("seq", "wide"),
        P("wide"),
        P("wide", None),
    )
    return jax.shard_map(
        body, mesh=mesh, in_specs=placed, out_specs=P(("seq", "wide"), None), check_vma=False
    )
```

```python
import functools

import jax
import jax.numpy as jnp
from jax import lax
from jax.experimental import pallas as pl
from jax.experimental.pallas import tpu as pltpu
from jax.sharding import PartitionSpec as P

MESH = pl.DeviceIdType.MESH
F32 = jnp.float32
BF16 = jnp.bfloat16
HD = 128
SPAN = 128
ITERS = 8
UNROLL = 2
LAG = 4
HL = 4
NJ = 4
NCH = 8
ORDER = (2, 1, 3, 0)
highest = lax.Precision.HIGHEST


def parts(value):
    high = value.astype(BF16)
    return high, (value - high.astype(F32)).astype(BF16)


def stacked(value):
    return jnp.concatenate(parts(value), axis=0)


def dot(a, b):
    return jnp.dot(a, b, preferred_element_type=F32)


def kernel(
    ny, nz, nx,
    q_hbm, k_hbm, v_hbm, ld_hbm, ridge_hbm, w_hbm, o_ref,
    q_ref, k_ref, v_ref, ld_ref, ridge_ref, w_vm,
    st_h, st_g, buf_h, buf_g, tot_h, tot_g, out_h, out_g, pre_h, pre, lb, sdec, crow, w1, w2, kt2, vt2, qt, ridge_m,
    gram_in, g_in, a1, a2, xs, rs, ps, nm, pown, pout, pin, ra, rb, f1, f2,
    load_sem, z_send, z_recv, y_send, y_recv, p_send, p_recv, r_send, r_recv, f_send, f_recv,
):
    seq = lax.axis_index("seq")
    wide = lax.axis_index("wide")
    y, z = lax.div(seq, nz), lax.rem(seq, nz)
    x, c = lax.div(wide, 2), lax.rem(wide, 2)
    rows_h, rows_g = HD // 2 // nz, HD // nz
    partner = x * 2 + (1 - c)
    right = lax.rem(x + 1, nx) * 2 + c
    left = lax.rem(x + nx - 1, nx) * 2 + c

    loads = [
        pltpu.make_async_copy(src, dst, load_sem.at[i])
        for i, (src, dst) in enumerate(
            (
                (ld_hbm, ld_ref), (k_hbm, k_ref), (v_hbm, v_ref),
                (q_hbm, q_ref), (ridge_hbm, ridge_ref), (w_hbm, w_vm),
            )
        )
    ]
    for load in loads[:5]:
        load.start()

    barrier = pltpu.get_barrier_semaphore()
    for step in range(1, nz):
        to = y * nz + lax.rem(z + step, nz)
        pl.semaphore_signal(barrier, inc=1, device_id=(to, wide), device_id_type=MESH)
    for step in range(1, ny):
        to = lax.rem(y + step, ny) * nz + z
        pl.semaphore_signal(barrier, inc=1, device_id=(to, wide), device_id_type=MESH)
    for to in (partner, right, left):
        pl.semaphore_signal(barrier, inc=1, device_id=(seq, to), device_id_type=MESH)

    place_r = lax.broadcasted_iota(jnp.int32, (SPAN, SPAN), 0)
    place_c = lax.broadcasted_iota(jnp.int32, (SPAN, SPAN), 1)
    lower = (place_r >= place_c).astype(F32)
    upper = (place_r <= place_c).astype(F32)
    ccols, norms = [], {}
    loads[0].wait()
    total = jnp.zeros((1, HL), F32)
    closings = []
    for j in range(NJ):
        decay = ld_ref[:, j * SPAN : (j + 1) * SPAN]
        ccol = lax.dot_general(
            lower, decay, (((1,), (1,)), ((), ())), precision=highest, preferred_element_type=F32
        )
        ccols.append(ccol)
        crow[j, 0:HL, :] = jnp.dot(decay, upper, precision=highest, preferred_element_type=F32)
        for h in range(HL):
            sdec[j, h : h + 1, :] = jnp.exp(jnp.broadcast_to(total[:, h : h + 1], (1, HD)))
        closing = ccol[SPAN - 1 : SPAN, :]
        closings.append(closing)
        total = total + closing
    group = lax.rem(lax.broadcasted_iota(jnp.int32, (HD // 2, HD), 0), rows_h)
    near = lax.rem(place_c - place_r + HD, HD)
    keep = near[0 : HD // 2] < HD // 2
    marks = jnp.zeros((HD // 2, HD), F32)
    loads[1].wait()

    for h in range(HL):
        hc = slice(h * HD, (h + 1) * HD)
        run = jnp.zeros((HD, HD), F32)
        for j in range(NJ):
            keys = k_ref[j * SPAN : (j + 1) * SPAN, hc]
            a2[j, h, 0:HD, 0:HD] = keys
            a2[j, h, 0:HD, HD : 2 * HD] = keys
            keyf = keys.astype(F32)
            norm = lax.rsqrt(jnp.sum(keyf * keyf, axis=1, keepdims=True) + 1e-06)
            norms[j, h] = norm
            keyt = keyf.T.astype(BF16)
            kt2[j, h, :, 0:HD] = keyt
            kt2[j, h, :, HD : 2 * HD] = keyt
            fade = jnp.exp(closings[j][:, h : h + 1] - ccols[j][:, h : h + 1])
            gram = dot(kt2[j, h], stacked(keyf * (fade * norm * norm)))
            lb[j, h] = run
            run = jnp.exp(closings[j][:, h : h + 1]) * run + gram
        st_h[1 + h] = jnp.where(keep, run[0 : HD // 2], run[HD // 2 :])
        edge = jnp.sum(jnp.where(near == HD // 2, run, 0.0), axis=0, keepdims=True)
        marks = jnp.where(group == h, jnp.broadcast_to(total[:, h : h + 1], marks.shape), marks)
        marks = jnp.where(group == HL + h, edge, marks)
    st_h[0] = marks

    pl.semaphore_wait(barrier, nz + ny + 1)

    def z_copy(src, dst, slot, step):
        to = y * nz + lax.rem(z + step, nz)
        return pltpu.make_async_remote_copy(
            src_ref=src, dst_ref=dst, send_sem=z_send.at[slot, step], recv_sem=z_recv.at[slot, step],
            device_id=(to, wide), device_id_type=MESH,
        )

    def scatter(st, buf, slot, rows, part):
        copies = []
        for step in range(1, nz):
            peer = lax.rem(z + step, nz)
            start = pl.multiple_of(peer * rows, rows)
            copies.append(z_copy(st.at[part, pl.ds(start, rows), :], buf.at[z, part], slot, step))
            copies[-1].start()
        mine = pl.multiple_of(z * rows, rows)
        buf[z, part] = st[part, pl.ds(mine, rows), :]
        return copies

    sends = scatter(st_h, buf_h, 0, rows_h, slice(0, HL + 1))
    sent = list(sends)
    g_sends = []
    loads[2].wait()

    for h in range(HL):
        hc = slice(h * HD, (h + 1) * HD)
        run = jnp.zeros((HD, HD), F32)
        for j in range(NJ):
            keyf = k_ref[j * SPAN : (j + 1) * SPAN, hc].astype(F32)
            valt = v_ref[j * SPAN : (j + 1) * SPAN, hc].astype(F32).T.astype(BF16)
            vt2[j, h, :, 0:HD] = valt
            vt2[j, h, :, HD : 2 * HD] = valt
            fade = jnp.exp(closings[j][:, h : h + 1] - ccols[j][:, h : h + 1])
            memory = dot(vt2[j, h], stacked(keyf * (fade * norms[j, h])))
            lb[j, HL + h] = run
            run = jnp.exp(closings[j][:, h : h + 1]) * run + memory
        st_g[h] = run
        g_sends.append(scatter(st_g, buf_g, 1 + h, rows_g, h))
        sent += g_sends[h]

    def y_copies(buf, slot, part):
        copies = []
        for step in range(1, ny):
            to = lax.rem(y + step, ny) * nz + z
            copies.append(
                pltpu.make_async_remote_copy(
                    src_ref=buf.at[y, part], dst_ref=buf.at[y, part],
                    send_sem=y_send.at[slot, step], recv_sem=y_recv.at[slot, step],
                    device_id=(to, wide), device_id_type=MESH,
                )
            )
            copies[-1].start()
        return copies

    def give_back(buf, pre, slot, rows, part):
        mine = pl.multiple_of(z * rows, rows)
        copies = []
        for step in range(1, nz):
            peer = lax.rem(z + step, nz)
            copies.append(
                z_copy(buf.at[peer, part], pre.at[part, pl.ds(mine, rows), :], slot, step)
            )
            copies[-1].start()
        pre[part, pl.ds(mine, rows), :] = buf[z, part]
        return copies

    def total_h(copies):
        for copy in copies:
            copy.wait_recv()
        sums = [jnp.zeros((rows_h, HD), F32) for _ in range(HL)]
        edges = [jnp.zeros((1, HD), F32) for _ in range(HL)]
        decay = jnp.zeros((8, HD), F32)
        for other in range(nz):
            marks = buf_h[other, 0, 0:8, :]
            factor = jnp.exp(marks[0:HL])
            decay = decay + marks
            for h in range(HL):
                sums[h] = factor[h : h + 1] * sums[h] + buf_h[other, 1 + h]
                edges[h] = factor[h : h + 1] * edges[h] + marks[HL + h : HL + h + 1]
        tot_h[y, 0, 0:8, :] = decay
        for h in range(HL):
            tot_h[y, 1 + h] = sums[h]
            tot_h[y, 0, HL + h : HL + h + 1, :] = edges[h]
        return y_copies(tot_h, 0, slice(0, HL + 1))

    def prefix_h(copies):
        for copy in copies:
            copy.wait_recv()
        runs = [jnp.zeros((rows_h, HD), F32) for _ in range(HL)]
        edges = [jnp.zeros((1, HD), F32) for _ in range(HL)]
        for other in range(ny):
            marks = tot_h[other, 0, 0:8, :]
            factor = jnp.exp(marks[0:HL])
            for h in range(HL):
                runs[h] = jnp.where(other < y, factor[h : h + 1] * runs[h] + tot_h[other, 1 + h], runs[h])
                edges[h] = jnp.where(
                    other < y, factor[h : h + 1] * edges[h] + marks[HL + h : HL + h + 1], edges[h]
                )
        for other in range(nz):
            marks = buf_h[other, 0, 0:8, :]
            factor = jnp.exp(marks[0:HL])
            for h in range(HL):
                out_h[other, 1 + h] = runs[h]
                out_h[other, 0, HL + h : HL + h + 1, :] = edges[h]
                runs[h] = factor[h : h + 1] * runs[h] + buf_h[other, 1 + h]
                edges[h] = factor[h : h + 1] * edges[h] + marks[HL + h : HL + h + 1]
        return give_back(out_h, pre_h, 1 + HL, rows_h, slice(0, HL + 1))

    def total_g(h, copies):
        for copy in copies:
            copy.wait_recv()
        run = jnp.zeros((rows_g, HD), F32)
        for other in range(nz):
            run = jnp.exp(buf_h[other, 0, h : h + 1, :]) * run + buf_g[other, h]
        tot_g[y, h] = run
        return y_copies(tot_g, 1 + h, h)

    def prefix_g(h, copies):
        for copy in copies:
            copy.wait_recv()
        run = jnp.zeros((rows_g, HD), F32)
        for other in range(ny):
            factor = jnp.exp(tot_h[other, 0, h : h + 1, :])
            run = jnp.where(other < y, factor * run + tot_g[other, h], run)
        for other in range(nz):
            out_g[other, h] = run
            run = jnp.exp(buf_h[other, 0, h : h + 1, :]) * run + buf_g[other, h]
        return give_back(out_g, pre, 2 + HL + h, rows_g, h)

    loads[3].wait()
    loads[4].wait()
    loads[5].start()
    out_h[:, 0] = jnp.zeros((nz, rows_h, HD), F32)
    for h in range(HL):
        hc = slice(h * HD, (h + 1) * HD)
        ridge_m[h] = jnp.broadcast_to(ridge_ref[:, hc], (HD, HD)).T
        g_in[h, HD : 2 * HD, HD : 2 * HD] = jnp.zeros((HD, HD), BF16)
        for i in range(2):
            a1[i * HL + h, 2 * HD : 3 * HD, HD : 2 * HD] = jnp.zeros((HD, HD), BF16)

    def weights_of(j):
        for h in range(HL):
            hc = slice(h * HD, (h + 1) * HD)
            lag = crow[j, h : h + 1, :] - ccols[j][:, h : h + 1]
            causal = place_r <= place_c
            weight = jnp.where(causal, jnp.exp(jnp.where(causal, lag, 0.0)), 0.0) * norms[j, h]
            high, low = parts(lb[j, HL + h])
            a2[j, h, HD : 2 * HD, 0:HD] = high
            a2[j, h, HD : 2 * HD, HD : 2 * HD] = high
            a2[j, h, 2 * HD : 3 * HD, 0:HD] = low
            a2[j, h, 2 * HD : 3 * HD, HD : 2 * HD] = jnp.zeros((HD, HD), BF16)
            w1[j, h] = weight
            w2[j, h] = weight * norms[j, h]
            query = q_ref[j * SPAN : (j + 1) * SPAN, hc].astype(F32).T
            qt[j, h] = query * lax.rsqrt(jnp.sum(query * query, axis=0, keepdims=True) + 1e-06)

    weights_of(0)
    weights_of(1)
    y_sends = total_h(sends)
    sent += y_sends
    weights_of(2)
    back = prefix_h(y_sends)
    sent += back
    weights_of(3)
    gy_sends = [total_g(h, g_sends[h]) for h in range(HL)]
    g_back = [prefix_g(h, gy_sends[h]) for h in range(HL)]
    for h in range(HL):
        sent += gy_sends[h] + g_back[h]
    for copy in back:
        copy.wait_recv()
    for h in range(HL):
        packed = pre_h[1 + h]
        spread = jnp.concatenate([jnp.where(keep, packed, 0.0), jnp.where(keep, 0.0, packed)], axis=0)
        both = jnp.where(near == 0, spread, spread + spread.T)
        gram_in[h] = jnp.where(near == HD // 2, pre_h[0, HL + h : HL + h + 1, :], both)

    def system(slot, j, h, state):
        high, low = parts(state)
        a1[slot, 0:HD, :] = a2[j, h, 0:HD, :]
        a1[slot, HD : 2 * HD, 0:HD] = high
        a1[slot, HD : 2 * HD, HD : 2 * HD] = high
        a1[slot, 2 * HD : 3 * HD, 0:HD] = low

    def blocks_of(spans):
        return [(i * HL + h, j, h) for i, j in enumerate(spans) for h in range(HL)]

    def solve(spans):
        blocks = blocks_of(spans)
        norm0, opening = [], []
        for slot, j, h in blocks:
            system(slot, j, h, sdec[j, h : h + 1, :] * gram_in[h] + lb[j, h])
            query = qt[j, h]
            xs[slot] = jnp.zeros((HD, SPAN), F32)
            rs[slot] = query
            ps[slot] = query
            norm0.append(jnp.sum(query * query, axis=0, keepdims=True))
            opening.append(jnp.exp(crow[j, h : h + 1, :]))

        def sweep(_, norm):
            n = len(blocks)
            outs, locals_, after = [None] * n, [None] * n, [None] * n
            for i, (slot, j, h) in enumerate(blocks):
                outs[i] = dot(a1[slot], stacked(ps[slot]))
            for i, (slot, j, h) in enumerate(blocks):
                locals_[i] = dot(kt2[j, h], stacked(outs[i][0:HD] * w2[j, h]))
            for i, (slot, j, h) in enumerate(blocks):
                direction = ps[slot]
                carried = outs[i][HD : 2 * HD] + outs[i][2 * HD : 3 * HD]
                image = opening[i] * carried + locals_[i] + ridge_m[h] * direction
                alpha = norm[i] / jnp.sum(direction * image, axis=0, keepdims=True)
                xs[slot] = xs[slot] + alpha * direction
                residual = rs[slot] - alpha * image
                fresh = jnp.sum(residual * residual, axis=0, keepdims=True)
                rs[slot] = residual
                ps[slot] = residual + (fresh / norm[i]) * direction
                after[i] = fresh
            return tuple(after)

        lax.fori_loop(0, ITERS, sweep, tuple(norm0), unroll=UNROLL)
        return opening

    def read_local(i, j, opening):
        outs = [dot(a2[j, h], stacked(xs[i * HL + h])) for h in range(HL)]
        for h in range(HL):
            near_part = dot(vt2[j, h], stacked(outs[h][0:HD] * w1[j, h]))
            rs[i * HL + h] = near_part + opening[i * HL + h] * (outs[h][HD : 2 * HD] + outs[h][2 * HD :])

    def take_memory(h):
        high, low = parts(pre[h])
        g_in[h, 0:HD, 0:HD] = high
        g_in[h, 0:HD, HD : 2 * HD] = high
        g_in[h, HD : 2 * HD, 0:HD] = low

    def read_out(k, i, j, opening, heads):
        outs = [dot(g_in[h], stacked(xs[i * HL + h])) for h in heads]
        for h, out in zip(heads, outs):
            lifted = opening[i * HL + h] * sdec[j, h : h + 1, :]
            read = rs[i * HL + h] + lifted * (out[0:HD] + out[HD : 2 * HD])
            read = read * lax.rsqrt(jnp.sum(read * read, axis=0, keepdims=True) * (1.0 / HD) + 1e-06)
            nm[k, :, h * HD : (h + 1) * HD] = read.T.astype(BF16)

    half = SPAN // 2
    width = w_vm.shape[1] // NCH

    def p_copy(k, n):
        return pltpu.make_async_remote_copy(
            src_ref=pout.at[k, n], dst_ref=pin.at[k, n], send_sem=p_send.at[k, n], recv_sem=p_recv.at[k, n],
            device_id=(seq, partner), device_id_type=MESH,
        )

    def project(k, order, use):
        mine = pl.multiple_of(c * half, half)
        other = pl.multiple_of((1 - c) * half, half)
        lhs = jnp.concatenate([nm[k, pl.ds(mine, half), :], nm[k, pl.ds(other, half), :]], axis=0)
        copies = {}
        for i in range(NCH + LAG):
            if i < NCH:
                n = order[i]
                out = dot(lhs, w_vm[:, n * width : (n + 1) * width])
                pown[k, n] = out[0:half]
                pout[k, n] = out[half:]
                copies[n] = p_copy(k, n)
                copies[n].start()
            if i >= LAG:
                use(order[i - LAG], copies)
        return copies

    def join(k, n, copies):
        copies[n].wait_recv()
        pown[k, n] = pown[k, n] + pin[k, n]

    def x_copy(src, dst, send, recv, to):
        copy = pltpu.make_async_remote_copy(
            src_ref=src, dst_ref=dst, send_sem=send, recv_sem=recv,
            device_id=(seq, to), device_id_type=MESH,
        )
        copy.start()
        return copy

    middle = NCH // 2
    js = [lax.rem(x + o, nx) for o in ORDER]

    mixed_order = [(i % 2) * middle + i // 2 for i in range(NCH)]
    relay, final1, final2 = {}, {}, {}

    opening = solve(js[0:1])
    read_local(0, js[0], opening)
    loads[5].wait()
    for h in range(HL):
        for copy in g_back[h]:
            copy.wait_recv()
        take_memory(h)
        read_out(0, 0, js[0], opening, (h,))

    def send_relay(n, copies):
        join(0, n, copies)
        if n < middle:
            relay[n] = x_copy(pown.at[0, n], ra.at[n], r_send.at[n], r_recv.at[n], right)
        else:
            relay[n] = x_copy(pown.at[0, n], rb.at[n - middle], r_send.at[n], r_recv.at[n], left)

    copies = project(0, mixed_order, send_relay)
    sent += list(copies.values()) + list(relay.values())

    def send_right(n, copies):
        if n >= middle:
            join(1, n, copies)
            final1[n] = x_copy(pown.at[1, n], f1.at[n], f_send.at[0, n], f_recv.at[0, n], right)

    def send_left(n, copies):
        if n < middle:
            join(2, n, copies)
            final2[n] = x_copy(pown.at[2, n], f2.at[n], f_send.at[1, n], f_recv.at[1, n], left)

    opening = solve(js[1:3])
    every = tuple(range(HL))
    read_local(0, js[1], opening)
    read_out(1, 0, js[1], opening, every)
    copies1 = project(1, list(range(middle, NCH)) + list(range(middle)), send_right)
    read_local(1, js[2], opening)
    read_out(2, 1, js[2], opening, every)
    copies2 = project(2, list(range(NCH)), send_left)
    for n in range(middle):
        relay[n].wait_recv()
        join(1, n, copies1)
        pown[1, n] = pown[1, n] + ra[n]
        final1[n] = x_copy(pown.at[1, n], f1.at[n], f_send.at[0, n], f_recv.at[0, n], right)
        m = n + middle
        relay[m].wait_recv()
        join(2, m, copies2)
        pown[2, m] = pown[2, m] + rb[n]
        final2[m] = x_copy(pown.at[2, m], f2.at[m], f_send.at[1, m], f_recv.at[1, m], left)
    sent += list(copies1.values()) + list(copies2.values()) + list(final1.values()) + list(final2.values())

    opening = solve(js[3:4])
    read_local(0, js[3], opening)
    read_out(3, 0, js[3], opening, every)
    copies3 = project(3, list(range(NCH)), functools.partial(join, 3))
    sent += list(copies3.values())
    for i in range(NCH):
        n = (i % 2) * middle + i // 2
        m = (n + middle) % NCH
        final1[m].wait_recv()
        final2[n].wait_recv()
        if i % 2 == 1:
            for e in (n, m):
                o_ref[:, e * width : (e + 1) * width] = (pown[3, e] + f1[e] + f2[e]).astype(BF16)
    for copy in sent:
        copy.wait_send()


def solution(mesh, ny=4, nz=8):
    nx = mesh.shape["wide"] // 2

    def body(queries, keys, values, log_decay, ridge, out_weight):
        columns = out_weight.shape[1]
        width = columns // NCH
        half = SPAN // 2
        rows_h, rows_g = HD // 2 // nz, HD // nz
        tokens, inner = queries.shape
        vm = pltpu.VMEM
        dma = pltpu.SemaphoreType.DMA
        scratch = [
            vm((tokens, inner), BF16),
            vm((tokens, inner), BF16),
            vm((tokens, inner), BF16),
            vm((HL, tokens), F32),
            vm((1, inner), F32),
            vm(out_weight.shape, BF16),
            vm((HL + 1, HD // 2, HD), F32),
            vm((HL, HD, HD), F32),
            vm((nz, HL + 1, rows_h, HD), F32),
            vm((nz, HL, rows_g, HD), F32),
            vm((ny, HL + 1, rows_h, HD), F32),
            vm((ny, HL, rows_g, HD), F32),
            vm((nz, HL + 1, rows_h, HD), F32),
            vm((nz, HL, rows_g, HD), F32),
            vm((HL + 1, HD // 2, HD), F32),
            vm((HL, HD, HD), F32),
            vm((NJ, 2 * HL, HD, HD), F32),
            vm((NJ, 8, HD), F32),
            vm((NJ, 8, HD), F32),
            vm((NJ, HL, SPAN, SPAN), F32),
            vm((NJ, HL, SPAN, SPAN), F32),
            vm((NJ, HL, HD, 2 * SPAN), BF16),
            vm((NJ, HL, HD, 2 * SPAN), BF16),
            vm((NJ, HL, HD, SPAN), F32),
            vm((HL, HD, SPAN), F32),
            vm((HL, HD, HD), F32),
            vm((HL, 2 * HD, 2 * HD), BF16),
            vm((2 * HL, 3 * HD, 2 * HD), BF16),
            vm((NJ, HL, 3 * HD, 2 * HD), BF16),
            vm((2 * HL, HD, SPAN), F32),
            vm((2 * HL, HD, SPAN), F32),
            vm((2 * HL, HD, SPAN), F32),
            vm((NJ, SPAN, HL * HD), BF16),
            vm((NJ, NCH, half, width), F32),
            vm((NJ, NCH, half, width), F32),
            vm((NJ, NCH, half, width), F32),
            vm((NCH // 2, half, width), F32),
            vm((NCH // 2, half, width), F32),
            vm((NCH, half, width), F32),
            vm((NCH, half, width), F32),
            dma((6,)),
            dma((2 * HL + 2, nz)),
            dma((2 * HL + 2, nz)),
            dma((HL + 1, ny)),
            dma((HL + 1, ny)),
            dma((NJ, NCH)),
            dma((NJ, NCH)),
            dma((NCH,)),
            dma((NCH,)),
            dma((2, NCH)),
            dma((2, NCH)),
        ]
        space = pl.BlockSpec(memory_space=pltpu.VMEM)
        return pl.pallas_call(
            functools.partial(kernel, ny, nz, nx),
            out_shape=jax.ShapeDtypeStruct((queries.shape[0] // (2 * nx), columns), BF16),
            in_specs=[pl.BlockSpec(memory_space=pl.ANY)] * 6,
            out_specs=space,
            scratch_shapes=scratch,
            compiler_params=pltpu.CompilerParams(
                collective_id=0, has_side_effects=True, vmem_limit_bytes=60 << 20
            ),
        )(queries, keys, values, log_decay.T, ridge[None, :], out_weight)

    placed = (
        P("seq", "wide"),
        P("seq", "wide"),
        P("seq", "wide"),
        P("seq", "wide"),
        P("wide"),
        P("wide", None),
    )
    return jax.shard_map(
        body, mesh=mesh, in_specs=placed, out_specs=P(("seq", "wide"), None), check_vma=False
    )
```

```python
import functools

import jax
import jax.numpy as jnp
from jax import lax
from jax.experimental import pallas as pl
from jax.experimental.pallas import tpu as pltpu
from jax.sharding import PartitionSpec as P

MESH = pl.DeviceIdType.MESH
F32 = jnp.float32
BF16 = jnp.bfloat16
HD = 128
SPAN = 128
ITERS = 8
UNROLL = 3
FULL = 6
LAG = 4
PAIR = 2
HL = 4
NJ = 4
NCH = 8
ORDER = (2, 1, 3, 0)
highest = lax.Precision.HIGHEST


def parts(value):
    high = value.astype(BF16)
    return high, (value - high.astype(F32)).astype(BF16)


def stacked(value):
    return jnp.concatenate(parts(value), axis=0)


def dot(a, b):
    return jnp.dot(a, b, preferred_element_type=F32)


def kernel(
    ny, nz, nx,
    q_hbm, k_hbm, v_hbm, ld_hbm, ridge_hbm, w_hbm, o_ref,
    q_ref, k_ref, v_ref, ld_ref, ridge_ref, w_vm,
    st_h, st_g, buf_h, buf_g, tot_h, tot_g, out_h, out_g, pre_h, pre, lb, sdec, crow, w1, w2, kt2, vt2, qt, ridge_m,
    gram_in, g_in, a1, b1, a2, xs, rs, ps, nm, pown, pout, pin, ra, rb, f1, f2,
    load_sem, z_send, z_recv, y_send, y_recv, p_send, p_recv, r_send, r_recv, f_send, f_recv,
):
    seq = lax.axis_index("seq")
    wide = lax.axis_index("wide")
    y, z = lax.div(seq, nz), lax.rem(seq, nz)
    x, c = lax.div(wide, 2), lax.rem(wide, 2)
    rows_h, rows_g = HD // 2 // nz, HD // nz
    partner = x * 2 + (1 - c)
    right = lax.rem(x + 1, nx) * 2 + c
    left = lax.rem(x + nx - 1, nx) * 2 + c

    loads = [
        pltpu.make_async_copy(src, dst, load_sem.at[i])
        for i, (src, dst) in enumerate(
            (
                (ld_hbm, ld_ref), (k_hbm, k_ref), (v_hbm, v_ref),
                (q_hbm, q_ref), (ridge_hbm, ridge_ref), (w_hbm, w_vm),
            )
        )
    ]
    for load in loads[:5]:
        load.start()

    barrier = pltpu.get_barrier_semaphore()
    for step in range(1, nz):
        to = y * nz + lax.rem(z + step, nz)
        pl.semaphore_signal(barrier, inc=1, device_id=(to, wide), device_id_type=MESH)
    for step in range(1, ny):
        to = lax.rem(y + step, ny) * nz + z
        pl.semaphore_signal(barrier, inc=1, device_id=(to, wide), device_id_type=MESH)
    for to in (partner, right, left):
        pl.semaphore_signal(barrier, inc=1, device_id=(seq, to), device_id_type=MESH)

    place_r = lax.broadcasted_iota(jnp.int32, (SPAN, SPAN), 0)
    place_c = lax.broadcasted_iota(jnp.int32, (SPAN, SPAN), 1)
    lower = (place_r >= place_c).astype(F32)
    upper = (place_r <= place_c).astype(F32)
    ccols, norms = [], {}
    loads[0].wait()
    total = jnp.zeros((1, HL), F32)
    closings = []
    for j in range(NJ):
        decay = ld_ref[:, j * SPAN : (j + 1) * SPAN]
        ccol = lax.dot_general(
            lower, decay, (((1,), (1,)), ((), ())), precision=highest, preferred_element_type=F32
        )
        ccols.append(ccol)
        crow[j, 0:HL, :] = jnp.dot(decay, upper, precision=highest, preferred_element_type=F32)
        for h in range(HL):
            sdec[j, h : h + 1, :] = jnp.exp(jnp.broadcast_to(total[:, h : h + 1], (1, HD)))
        closing = ccol[SPAN - 1 : SPAN, :]
        closings.append(closing)
        total = total + closing
    group = lax.rem(lax.broadcasted_iota(jnp.int32, (HD // 2, HD), 0), rows_h)
    near = lax.rem(place_c - place_r + HD, HD)
    keep = near[0 : HD // 2] < HD // 2
    marks = jnp.zeros((HD // 2, HD), F32)
    loads[1].wait()

    for h in range(HL):
        hc = slice(h * HD, (h + 1) * HD)
        run = jnp.zeros((HD, HD), F32)
        for j in range(NJ):
            keys = k_ref[j * SPAN : (j + 1) * SPAN, hc]
            a2[j, h, 0:HD, 0:HD] = keys
            a2[j, h, 0:HD, HD : 2 * HD] = keys
            keyf = keys.astype(F32)
            norm = lax.rsqrt(jnp.sum(keyf * keyf, axis=1, keepdims=True) + 1e-06)
            norms[j, h] = norm
            keyt = keyf.T.astype(BF16)
            kt2[j, h, :, 0:HD] = keyt
            kt2[j, h, :, HD : 2 * HD] = keyt
            fade = jnp.exp(closings[j][:, h : h + 1] - ccols[j][:, h : h + 1])
            gram = dot(kt2[j, h], stacked(keyf * (fade * norm * norm)))
            lb[j, h] = run
            run = jnp.exp(closings[j][:, h : h + 1]) * run + gram
        st_h[1 + h] = jnp.where(keep, run[0 : HD // 2], run[HD // 2 :])
        edge = jnp.sum(jnp.where(near == HD // 2, run, 0.0), axis=0, keepdims=True)
        marks = jnp.where(group == h, jnp.broadcast_to(total[:, h : h + 1], marks.shape), marks)
        marks = jnp.where(group == HL + h, edge, marks)
    st_h[0] = marks

    pl.semaphore_wait(barrier, nz + ny + 1)

    def z_copy(src, dst, slot, step):
        to = y * nz + lax.rem(z + step, nz)
        return pltpu.make_async_remote_copy(
            src_ref=src, dst_ref=dst, send_sem=z_send.at[slot, step], recv_sem=z_recv.at[slot, step],
            device_id=(to, wide), device_id_type=MESH,
        )

    def scatter(st, buf, slot, rows, part):
        copies = []
        for step in range(1, nz):
            peer = lax.rem(z + step, nz)
            start = pl.multiple_of(peer * rows, rows)
            copies.append(z_copy(st.at[part, pl.ds(start, rows), :], buf.at[z, part], slot, step))
            copies[-1].start()
        mine = pl.multiple_of(z * rows, rows)
        buf[z, part] = st[part, pl.ds(mine, rows), :]
        return copies

    sends = scatter(st_h, buf_h, 0, rows_h, slice(0, HL + 1))
    sent = list(sends)
    g_sends = []
    loads[2].wait()

    for h in range(HL):
        hc = slice(h * HD, (h + 1) * HD)
        run = jnp.zeros((HD, HD), F32)
        for j in range(NJ):
            keyf = k_ref[j * SPAN : (j + 1) * SPAN, hc].astype(F32)
            valt = v_ref[j * SPAN : (j + 1) * SPAN, hc].astype(F32).T.astype(BF16)
            vt2[j, h, :, 0:HD] = valt
            vt2[j, h, :, HD : 2 * HD] = valt
            fade = jnp.exp(closings[j][:, h : h + 1] - ccols[j][:, h : h + 1])
            memory = dot(vt2[j, h], stacked(keyf * (fade * norms[j, h])))
            lb[j, HL + h] = run
            run = jnp.exp(closings[j][:, h : h + 1]) * run + memory
        st_g[h] = run
        if h % PAIR == PAIR - 1:
            g_sends.append(scatter(st_g, buf_g, 1 + h, rows_g, slice(h + 1 - PAIR, h + 1)))
            sent += g_sends[-1]

    def y_copies(buf, slot, part):
        copies = []
        for step in range(1, ny):
            to = lax.rem(y + step, ny) * nz + z
            copies.append(
                pltpu.make_async_remote_copy(
                    src_ref=buf.at[y, part], dst_ref=buf.at[y, part],
                    send_sem=y_send.at[slot, step], recv_sem=y_recv.at[slot, step],
                    device_id=(to, wide), device_id_type=MESH,
                )
            )
            copies[-1].start()
        return copies

    def give_back(buf, pre, slot, rows, part):
        mine = pl.multiple_of(z * rows, rows)
        copies = []
        for step in range(1, nz):
            peer = lax.rem(z + step, nz)
            copies.append(
                z_copy(buf.at[peer, part], pre.at[part, pl.ds(mine, rows), :], slot, step)
            )
            copies[-1].start()
        pre[part, pl.ds(mine, rows), :] = buf[z, part]
        return copies

    def total_h(copies):
        for copy in copies:
            copy.wait_recv()
        sums = [jnp.zeros((rows_h, HD), F32) for _ in range(HL)]
        edges = [jnp.zeros((1, HD), F32) for _ in range(HL)]
        decay = jnp.zeros((8, HD), F32)
        for other in range(nz):
            marks = buf_h[other, 0, 0:8, :]
            factor = jnp.exp(marks[0:HL])
            decay = decay + marks
            for h in range(HL):
                sums[h] = factor[h : h + 1] * sums[h] + buf_h[other, 1 + h]
                edges[h] = factor[h : h + 1] * edges[h] + marks[HL + h : HL + h + 1]
        tot_h[y, 0, 0:8, :] = decay
        for h in range(HL):
            tot_h[y, 1 + h] = sums[h]
            tot_h[y, 0, HL + h : HL + h + 1, :] = edges[h]
        return y_copies(tot_h, 0, slice(0, HL + 1))

    def prefix_h(copies):
        for copy in copies:
            copy.wait_recv()
        runs = [jnp.zeros((rows_h, HD), F32) for _ in range(HL)]
        edges = [jnp.zeros((1, HD), F32) for _ in range(HL)]
        for other in range(ny):
            marks = tot_h[other, 0, 0:8, :]
            factor = jnp.exp(marks[0:HL])
            for h in range(HL):
                runs[h] = jnp.where(other < y, factor[h : h + 1] * runs[h] + tot_h[other, 1 + h], runs[h])
                edges[h] = jnp.where(
                    other < y, factor[h : h + 1] * edges[h] + marks[HL + h : HL + h + 1], edges[h]
                )
        mine = list(edges)
        for other in range(nz):
            marks = buf_h[other, 0, 0:8, :]
            factor = jnp.exp(marks[0:HL])
            for h in range(HL):
                out_h[other, h] = runs[h]
                mine[h] = jnp.where(other == z, edges[h], mine[h])
                runs[h] = factor[h : h + 1] * runs[h] + buf_h[other, 1 + h]
                edges[h] = factor[h : h + 1] * edges[h] + marks[HL + h : HL + h + 1]
        return give_back(out_h, pre_h, 1 + HL, rows_h, slice(0, HL)), mine

    def total_g(first, copies):
        for copy in copies:
            copy.wait_recv()
        for h in range(first, first + PAIR):
            run = jnp.zeros((rows_g, HD), F32)
            for other in range(nz):
                run = jnp.exp(buf_h[other, 0, h : h + 1, :]) * run + buf_g[other, h]
            tot_g[y, h] = run
        return y_copies(tot_g, 1 + first, slice(first, first + PAIR))

    def prefix_g(first, copies):
        for copy in copies:
            copy.wait_recv()
        for h in range(first, first + PAIR):
            run = jnp.zeros((rows_g, HD), F32)
            for other in range(ny):
                factor = jnp.exp(tot_h[other, 0, h : h + 1, :])
                run = jnp.where(other < y, factor * run + tot_g[other, h], run)
            for other in range(nz):
                out_g[other, h] = run
                run = jnp.exp(buf_h[other, 0, h : h + 1, :]) * run + buf_g[other, h]
        return give_back(out_g, pre, 2 + HL + first, rows_g, slice(first, first + PAIR))

    loads[3].wait()
    loads[4].wait()
    loads[5].start()
    for h in range(HL):
        hc = slice(h * HD, (h + 1) * HD)
        ridge_m[h] = jnp.broadcast_to(ridge_ref[:, hc], (HD, HD)).T
        g_in[h, HD : 2 * HD, HD : 2 * HD] = jnp.zeros((HD, HD), BF16)
        for i in range(2):
            a1[i * HL + h, 2 * HD : 3 * HD, HD : 2 * HD] = jnp.zeros((HD, HD), BF16)

    def weights_of(j):
        for h in range(HL):
            hc = slice(h * HD, (h + 1) * HD)
            lag = crow[j, h : h + 1, :] - ccols[j][:, h : h + 1]
            causal = place_r <= place_c
            weight = jnp.where(causal, jnp.exp(jnp.where(causal, lag, 0.0)), 0.0) * norms[j, h]
            high, low = parts(lb[j, HL + h])
            a2[j, h, HD : 2 * HD, 0:HD] = high
            a2[j, h, HD : 2 * HD, HD : 2 * HD] = high
            a2[j, h, 2 * HD : 3 * HD, 0:HD] = low
            a2[j, h, 2 * HD : 3 * HD, HD : 2 * HD] = jnp.zeros((HD, HD), BF16)
            w1[j, h] = weight
            w2[j, h] = weight * norms[j, h]
            query = q_ref[j * SPAN : (j + 1) * SPAN, hc].astype(F32).T
            qt[j, h] = query * lax.rsqrt(jnp.sum(query * query, axis=0, keepdims=True) + 1e-06)

    weights_of(0)
    weights_of(1)
    y_sends = total_h(sends)
    sent += y_sends
    weights_of(2)
    back, edges = prefix_h(y_sends)
    sent += back
    weights_of(3)
    firsts = range(0, HL, PAIR)
    gy_sends = [total_g(first, copies) for first, copies in zip(firsts, g_sends)]
    g_back = [prefix_g(first, copies) for first, copies in zip(firsts, gy_sends)]
    for copies in gy_sends + g_back:
        sent += copies
    for copy in back:
        copy.wait_recv()
    for h in range(HL):
        packed = pre_h[h]
        spread = jnp.concatenate([jnp.where(keep, packed, 0.0), jnp.where(keep, 0.0, packed)], axis=0)
        both = jnp.where(near == 0, spread, spread + spread.T)
        gram_in[h] = jnp.where(near == HD // 2, edges[h], both)

    def system(slot, j, h, state):
        high, low = parts(state)
        a1[slot, 0:HD, :] = a2[j, h, 0:HD, :]
        a1[slot, HD : 2 * HD, 0:HD] = high
        a1[slot, HD : 2 * HD, HD : 2 * HD] = high
        a1[slot, 2 * HD : 3 * HD, 0:HD] = low
        b1[slot, :, 0:HD] = high
        b1[slot, :, HD : 2 * HD] = kt2[j, h, :, 0:SPAN]

    def blocks_of(spans):
        return [(i * HL + h, j, h) for i, j in enumerate(spans) for h in range(HL)]

    def solve(spans):
        blocks = blocks_of(spans)
        norm0, opening = [], []
        for slot, j, h in blocks:
            system(slot, j, h, sdec[j, h : h + 1, :] * gram_in[h] + lb[j, h])
            query = qt[j, h]
            xs[slot] = jnp.zeros((HD, SPAN), F32)
            rs[slot] = query
            ps[slot] = query
            norm0.append(jnp.sum(query * query, axis=0, keepdims=True))
            opening.append(jnp.exp(crow[j, h : h + 1, :]))

        def advance(i, slot, norm, image):
            direction = ps[slot]
            alpha = norm / jnp.sum(direction * image, axis=0, keepdims=True)
            xs[slot] = xs[slot] + alpha * direction
            residual = rs[slot] - alpha * image
            fresh = jnp.sum(residual * residual, axis=0, keepdims=True)
            rs[slot] = residual
            ps[slot] = residual + (fresh / norm) * direction
            return fresh

        def sweep(_, norm):
            n = len(blocks)
            outs, locals_, after = [None] * n, [None] * n, [None] * n
            for i, (slot, j, h) in enumerate(blocks):
                outs[i] = dot(a1[slot], stacked(ps[slot]))
            for i, (slot, j, h) in enumerate(blocks):
                locals_[i] = dot(kt2[j, h], stacked(outs[i][0:HD] * w2[j, h]))
            for i, (slot, j, h) in enumerate(blocks):
                carried = outs[i][HD : 2 * HD] + outs[i][2 * HD : 3 * HD]
                image = opening[i] * carried + locals_[i] + ridge_m[h] * ps[slot]
                after[i] = advance(i, slot, norm[i], image)
            return tuple(after)

        def last_sweep(_, norm):
            n = len(blocks)
            outs, images, after = [None] * n, [None] * n, [None] * n
            for i, (slot, j, h) in enumerate(blocks):
                outs[i] = dot(a1[slot, 0:HD, 0:HD], ps[slot].astype(BF16))
            for i, (slot, j, h) in enumerate(blocks):
                lifted = (opening[i] * ps[slot]).astype(BF16)
                scores = (outs[i] * w2[j, h]).astype(BF16)
                images[i] = dot(b1[slot], jnp.concatenate([lifted, scores], axis=0))
            for i, (slot, j, h) in enumerate(blocks):
                image = images[i] + ridge_m[h] * ps[slot]
                after[i] = advance(i, slot, norm[i], image)
            return tuple(after)

        norm = lax.fori_loop(0, FULL, sweep, tuple(norm0), unroll=UNROLL)
        lax.fori_loop(FULL, ITERS, last_sweep, norm, unroll=2)
        return opening

    def read_local(i, j, opening):
        outs = [dot(a2[j, h], stacked(xs[i * HL + h])) for h in range(HL)]
        for h in range(HL):
            near_part = dot(vt2[j, h], stacked(outs[h][0:HD] * w1[j, h]))
            rs[i * HL + h] = near_part + opening[i * HL + h] * (outs[h][HD : 2 * HD] + outs[h][2 * HD :])

    def take_memory(h):
        high, low = parts(pre[h])
        g_in[h, 0:HD, 0:HD] = high
        g_in[h, 0:HD, HD : 2 * HD] = high
        g_in[h, HD : 2 * HD, 0:HD] = low

    def read_out(k, i, j, opening, heads):
        outs = [dot(g_in[h], stacked(xs[i * HL + h])) for h in heads]
        for h, out in zip(heads, outs):
            lifted = opening[i * HL + h] * sdec[j, h : h + 1, :]
            read = rs[i * HL + h] + lifted * (out[0:HD] + out[HD : 2 * HD])
            read = read * lax.rsqrt(jnp.sum(read * read, axis=0, keepdims=True) * (1.0 / HD) + 1e-06)
            nm[k, :, h * HD : (h + 1) * HD] = read.T.astype(BF16)

    half = SPAN // 2
    width = w_vm.shape[1] // NCH

    def p_copy(k, n):
        return pltpu.make_async_remote_copy(
            src_ref=pout.at[k, n], dst_ref=pin.at[k, n], send_sem=p_send.at[k, n], recv_sem=p_recv.at[k, n],
            device_id=(seq, partner), device_id_type=MESH,
        )

    def project(k, order, use):
        mine = pl.multiple_of(c * half, half)
        other = pl.multiple_of((1 - c) * half, half)
        lhs = jnp.concatenate([nm[k, pl.ds(mine, half), :], nm[k, pl.ds(other, half), :]], axis=0)
        copies = {}
        for i in range(NCH + LAG):
            if i < NCH:
                n = order[i]
                out = dot(lhs, w_vm[:, n * width : (n + 1) * width])
                pown[k, n] = out[0:half]
                pout[k, n] = out[half:]
                copies[n] = p_copy(k, n)
                copies[n].start()
            if i >= LAG:
                use(order[i - LAG], copies)
        return copies

    def join(k, n, copies):
        copies[n].wait_recv()
        pown[k, n] = pown[k, n] + pin[k, n]

    def x_copy(src, dst, send, recv, to):
        copy = pltpu.make_async_remote_copy(
            src_ref=src, dst_ref=dst, send_sem=send, recv_sem=recv,
            device_id=(seq, to), device_id_type=MESH,
        )
        copy.start()
        return copy

    middle = NCH // 2
    js = [lax.rem(x + o, nx) for o in ORDER]

    mixed_order = [(i % 2) * middle + i // 2 for i in range(NCH)]
    relay, final1, final2 = {}, {}, {}

    opening = solve(js[0:1])
    read_local(0, js[0], opening)
    loads[5].wait()
    for first, copies in zip(firsts, g_back):
        for copy in copies:
            copy.wait_recv()
        for h in range(first, first + PAIR):
            take_memory(h)
        read_out(0, 0, js[0], opening, tuple(range(first, first + PAIR)))

    def send_relay(n, copies):
        join(0, n, copies)
        if n < middle:
            relay[n] = x_copy(pown.at[0, n], ra.at[n], r_send.at[n], r_recv.at[n], right)
        else:
            relay[n] = x_copy(pown.at[0, n], rb.at[n - middle], r_send.at[n], r_recv.at[n], left)

    copies = project(0, mixed_order, send_relay)
    sent += list(copies.values()) + list(relay.values())

    def send_right(n, copies):
        if n >= middle:
            join(1, n, copies)
            final1[n] = x_copy(pown.at[1, n], f1.at[n], f_send.at[0, n], f_recv.at[0, n], right)

    def send_left(n, copies):
        if n < middle:
            join(2, n, copies)
            final2[n] = x_copy(pown.at[2, n], f2.at[n], f_send.at[1, n], f_recv.at[1, n], left)

    opening = solve(js[1:3])
    every = tuple(range(HL))
    read_local(0, js[1], opening)
    read_out(1, 0, js[1], opening, every)
    copies1 = project(1, list(range(middle, NCH)) + list(range(middle)), send_right)
    read_local(1, js[2], opening)
    read_out(2, 1, js[2], opening, every)
    copies2 = project(2, list(range(NCH)), send_left)
    for n in range(middle):
        relay[n].wait_recv()
        join(1, n, copies1)
        pown[1, n] = pown[1, n] + ra[n]
        final1[n] = x_copy(pown.at[1, n], f1.at[n], f_send.at[0, n], f_recv.at[0, n], right)
        m = n + middle
        relay[m].wait_recv()
        join(2, m, copies2)
        pown[2, m] = pown[2, m] + rb[n]
        final2[m] = x_copy(pown.at[2, m], f2.at[m], f_send.at[1, m], f_recv.at[1, m], left)
    sent += list(copies1.values()) + list(copies2.values()) + list(final1.values()) + list(final2.values())

    opening = solve(js[3:4])
    read_local(0, js[3], opening)
    read_out(3, 0, js[3], opening, every)
    copies3 = project(3, list(range(NCH)), functools.partial(join, 3))
    sent += list(copies3.values())
    for i in range(NCH):
        n = (i % 2) * middle + i // 2
        m = (n + middle) % NCH
        final1[m].wait_recv()
        final2[n].wait_recv()
        if i % 2 == 1:
            for e in (n, m):
                o_ref[:, e * width : (e + 1) * width] = (pown[3, e] + f1[e] + f2[e]).astype(BF16)
    for copy in sent:
        copy.wait_send()


def solution(mesh, ny=4, nz=8):
    nx = mesh.shape["wide"] // 2

    def body(queries, keys, values, log_decay, ridge, out_weight):
        columns = out_weight.shape[1]
        width = columns // NCH
        half = SPAN // 2
        rows_h, rows_g = HD // 2 // nz, HD // nz
        tokens, inner = queries.shape
        vm = pltpu.VMEM
        dma = pltpu.SemaphoreType.DMA
        scratch = [
            vm((tokens, inner), BF16),
            vm((tokens, inner), BF16),
            vm((tokens, inner), BF16),
            vm((HL, tokens), F32),
            vm((1, inner), F32),
            vm(out_weight.shape, BF16),
            vm((HL + 1, HD // 2, HD), F32),
            vm((HL, HD, HD), F32),
            vm((nz, HL + 1, rows_h, HD), F32),
            vm((nz, HL, rows_g, HD), F32),
            vm((ny, HL + 1, rows_h, HD), F32),
            vm((ny, HL, rows_g, HD), F32),
            vm((nz, HL, rows_h, HD), F32),
            vm((nz, HL, rows_g, HD), F32),
            vm((HL, HD // 2, HD), F32),
            vm((HL, HD, HD), F32),
            vm((NJ, 2 * HL, HD, HD), F32),
            vm((NJ, 8, HD), F32),
            vm((NJ, 8, HD), F32),
            vm((NJ, HL, SPAN, SPAN), F32),
            vm((NJ, HL, SPAN, SPAN), F32),
            vm((NJ, HL, HD, 2 * SPAN), BF16),
            vm((NJ, HL, HD, 2 * SPAN), BF16),
            vm((NJ, HL, HD, SPAN), F32),
            vm((HL, HD, SPAN), F32),
            vm((HL, HD, HD), F32),
            vm((HL, 2 * HD, 2 * HD), BF16),
            vm((2 * HL, 3 * HD, 2 * HD), BF16),
            vm((2 * HL, HD, 2 * HD), BF16),
            vm((NJ, HL, 3 * HD, 2 * HD), BF16),
            vm((2 * HL, HD, SPAN), F32),
            vm((2 * HL, HD, SPAN), F32),
            vm((2 * HL, HD, SPAN), F32),
            vm((NJ, SPAN, HL * HD), BF16),
            vm((NJ, NCH, half, width), F32),
            vm((NJ, NCH, half, width), F32),
            vm((NJ, NCH, half, width), F32),
            vm((NCH // 2, half, width), F32),
            vm((NCH // 2, half, width), F32),
            vm((NCH, half, width), F32),
            vm((NCH, half, width), F32),
            dma((6,)),
            dma((2 * HL + 2, nz)),
            dma((2 * HL + 2, nz)),
            dma((HL + 1, ny)),
            dma((HL + 1, ny)),
            dma((NJ, NCH)),
            dma((NJ, NCH)),
            dma((NCH,)),
            dma((NCH,)),
            dma((2, NCH)),
            dma((2, NCH)),
        ]
        space = pl.BlockSpec(memory_space=pltpu.VMEM)
        return pl.pallas_call(
            functools.partial(kernel, ny, nz, nx),
            out_shape=jax.ShapeDtypeStruct((queries.shape[0] // (2 * nx), columns), BF16),
            in_specs=[pl.BlockSpec(memory_space=pl.ANY)] * 6,
            out_specs=space,
            scratch_shapes=scratch,
            compiler_params=pltpu.CompilerParams(
                collective_id=0, has_side_effects=True, vmem_limit_bytes=60 << 20
            ),
        )(queries, keys, values, log_decay.T, ridge[None, :], out_weight)

    placed = (
        P("seq", "wide"),
        P("seq", "wide"),
        P("seq", "wide"),
        P("seq", "wide"),
        P("wide"),
        P("wide", None),
    )
    return jax.shard_map(
        body, mesh=mesh, in_specs=placed, out_specs=P(("seq", "wide"), None), check_vma=False
    )
```

```python
import functools

import jax
import jax.numpy as jnp
from jax import lax
from jax.experimental import pallas as pl
from jax.experimental.pallas import tpu as pltpu
from jax.sharding import PartitionSpec as P

MESH = pl.DeviceIdType.MESH
F32 = jnp.float32
BF16 = jnp.bfloat16
HD = 128
SPAN = 128
ITERS = 8
UNROLL = 3
FULL = 6
LAG = 4
PAIR = 2
HL = 4
NJ = 4
NCH = 8
ORDER = (2, 1, 3, 0)
highest = lax.Precision.HIGHEST


def parts(value):
    high = value.astype(BF16)
    return high, (value - high.astype(F32)).astype(BF16)


def stacked(value):
    return jnp.concatenate(parts(value), axis=0)


def dot(a, b):
    return jnp.dot(a, b, preferred_element_type=F32)


def kernel(
    ny, nz, nx,
    q_hbm, k_hbm, v_hbm, ld_hbm, ridge_hbm, w_hbm, o_ref,
    q_ref, k_ref, v_ref, ld_ref, ridge_ref, w_vm,
    st_h, st_g, buf_h, buf_g, tot_h, tot_g, out_h, out_g, pre_h, pre, lb, sdec, crow, w1, w2, kt2, vt2, qt, ridge_m,
    gram_in, g_in, a1, b1, a2, xs, rs, ps, nm, pown, pout, pin, ra, rb, f1, f2,
    load_sem, z_send, z_recv, y_send, y_recv, p_send, p_recv, r_send, r_recv, f_send, f_recv,
):
    seq = lax.axis_index("seq")
    wide = lax.axis_index("wide")
    y, z = lax.div(seq, nz), lax.rem(seq, nz)
    x, c = lax.div(wide, 2), lax.rem(wide, 2)
    rows_h, rows_g = HD // 2 // nz, HD // nz
    partner = x * 2 + (1 - c)
    right = lax.rem(x + 1, nx) * 2 + c
    left = lax.rem(x + nx - 1, nx) * 2 + c

    loads = [
        pltpu.make_async_copy(src, dst, load_sem.at[i])
        for i, (src, dst) in enumerate(
            (
                (ld_hbm, ld_ref), (k_hbm, k_ref), (v_hbm, v_ref),
                (q_hbm, q_ref), (ridge_hbm, ridge_ref), (w_hbm, w_vm),
            )
        )
    ]
    for load in loads[:5]:
        load.start()

    barrier = pltpu.get_barrier_semaphore()
    for step in range(1, nz):
        to = y * nz + lax.rem(z + step, nz)
        pl.semaphore_signal(barrier, inc=1, device_id=(to, wide), device_id_type=MESH)
    for step in range(1, ny):
        to = lax.rem(y + step, ny) * nz + z
        pl.semaphore_signal(barrier, inc=1, device_id=(to, wide), device_id_type=MESH)
    for to in (partner, right, left):
        pl.semaphore_signal(barrier, inc=1, device_id=(seq, to), device_id_type=MESH)

    place_r = lax.broadcasted_iota(jnp.int32, (SPAN, SPAN), 0)
    place_c = lax.broadcasted_iota(jnp.int32, (SPAN, SPAN), 1)
    lower = (place_r >= place_c).astype(F32)
    upper = (place_r <= place_c).astype(F32)
    ccols, norms = [], {}
    loads[0].wait()
    total = jnp.zeros((1, HL), F32)
    closings = []
    for j in range(NJ):
        decay = ld_ref[:, j * SPAN : (j + 1) * SPAN]
        ccol = lax.dot_general(
            lower, decay, (((1,), (1,)), ((), ())), precision=highest, preferred_element_type=F32
        )
        ccols.append(ccol)
        crow[j, 0:HL, :] = jnp.dot(decay, upper, precision=highest, preferred_element_type=F32)
        for h in range(HL):
            sdec[j, h : h + 1, :] = jnp.exp(jnp.broadcast_to(total[:, h : h + 1], (1, HD)))
        closing = ccol[SPAN - 1 : SPAN, :]
        closings.append(closing)
        total = total + closing
    group = lax.rem(lax.broadcasted_iota(jnp.int32, (HD // 2, HD), 0), rows_h)
    near = lax.rem(place_c - place_r + HD, HD)
    keep = near[0 : HD // 2] < HD // 2
    marks = jnp.zeros((HD // 2, HD), F32)
    loads[1].wait()

    for h in range(HL):
        hc = slice(h * HD, (h + 1) * HD)
        run = jnp.zeros((HD, HD), F32)
        for j in range(NJ):
            keys = k_ref[j * SPAN : (j + 1) * SPAN, hc]
            a2[j, h, 0:HD, 0:HD] = keys
            a2[j, h, 0:HD, HD : 2 * HD] = keys
            keyf = keys.astype(F32)
            norm = lax.rsqrt(jnp.sum(keyf * keyf, axis=1, keepdims=True) + 1e-06)
            norms[j, h] = norm
            keyt = keyf.T.astype(BF16)
            kt2[j, h, :, 0:HD] = keyt
            kt2[j, h, :, HD : 2 * HD] = keyt
            fade = jnp.exp(closings[j][:, h : h + 1] - ccols[j][:, h : h + 1])
            gram = dot(kt2[j, h], stacked(keyf * (fade * norm * norm)))
            lb[j, h] = run
            run = jnp.exp(closings[j][:, h : h + 1]) * run + gram
        st_h[1 + h] = jnp.where(keep, run[0 : HD // 2], run[HD // 2 :])
        edge = jnp.sum(jnp.where(near == HD // 2, run, 0.0), axis=0, keepdims=True)
        marks = jnp.where(group == h, jnp.broadcast_to(total[:, h : h + 1], marks.shape), marks)
        marks = jnp.where(group == HL + h, edge, marks)
    st_h[0] = marks

    pl.semaphore_wait(barrier, nz + ny + 1)

    def z_copy(src, dst, slot, step):
        to = y * nz + lax.rem(z + step, nz)
        return pltpu.make_async_remote_copy(
            src_ref=src, dst_ref=dst, send_sem=z_send.at[slot, step], recv_sem=z_recv.at[slot, step],
            device_id=(to, wide), device_id_type=MESH,
        )

    def scatter(st, buf, slot, rows, part):
        copies = []
        for step in range(1, nz):
            peer = lax.rem(z + step, nz)
            start = pl.multiple_of(peer * rows, rows)
            copies.append(z_copy(st.at[part, pl.ds(start, rows), :], buf.at[z, part], slot, step))
            copies[-1].start()
        mine = pl.multiple_of(z * rows, rows)
        buf[z, part] = st[part, pl.ds(mine, rows), :]
        return copies

    sends = scatter(st_h, buf_h, 0, rows_h, slice(0, HL + 1))
    sent = list(sends)
    g_sends = []
    loads[2].wait()

    for h in range(HL):
        hc = slice(h * HD, (h + 1) * HD)
        run = jnp.zeros((HD, HD), F32)
        for j in range(NJ):
            keyf = k_ref[j * SPAN : (j + 1) * SPAN, hc].astype(F32)
            valt = v_ref[j * SPAN : (j + 1) * SPAN, hc].astype(F32).T.astype(BF16)
            vt2[j, h, :, 0:HD] = valt
            vt2[j, h, :, HD : 2 * HD] = valt
            fade = jnp.exp(closings[j][:, h : h + 1] - ccols[j][:, h : h + 1])
            memory = dot(vt2[j, h], stacked(keyf * (fade * norms[j, h])))
            lb[j, HL + h] = run
            run = jnp.exp(closings[j][:, h : h + 1]) * run + memory
        st_g[h] = run
        if h % PAIR == PAIR - 1:
            g_sends.append(scatter(st_g, buf_g, 1 + h, rows_g, slice(h + 1 - PAIR, h + 1)))
            sent += g_sends[-1]

    def y_copies(buf, slot, part):
        copies = []
        for step in range(1, ny):
            to = lax.rem(y + step, ny) * nz + z
            copies.append(
                pltpu.make_async_remote_copy(
                    src_ref=buf.at[y, part], dst_ref=buf.at[y, part],
                    send_sem=y_send.at[slot, step], recv_sem=y_recv.at[slot, step],
                    device_id=(to, wide), device_id_type=MESH,
                )
            )
            copies[-1].start()
        return copies

    def give_back(buf, pre, slot, rows, part):
        mine = pl.multiple_of(z * rows, rows)
        copies = []
        for step in range(1, nz):
            peer = lax.rem(z + step, nz)
            copies.append(
                z_copy(buf.at[peer, part], pre.at[part, pl.ds(mine, rows), :], slot, step)
            )
            copies[-1].start()
        pre[part, pl.ds(mine, rows), :] = buf[z, part]
        return copies

    def total_h(copies):
        for copy in copies:
            copy.wait_recv()
        sums = [jnp.zeros((rows_h, HD), F32) for _ in range(HL)]
        edges = [jnp.zeros((1, HD), F32) for _ in range(HL)]
        decay = jnp.zeros((8, HD), F32)
        for other in range(nz):
            marks = buf_h[other, 0, 0:8, :]
            factor = jnp.exp(marks[0:HL])
            decay = decay + marks
            for h in range(HL):
                sums[h] = factor[h : h + 1] * sums[h] + buf_h[other, 1 + h]
                edges[h] = factor[h : h + 1] * edges[h] + marks[HL + h : HL + h + 1]
        tot_h[y, 0, 0:8, :] = decay
        for h in range(HL):
            tot_h[y, 1 + h] = sums[h]
            tot_h[y, 0, HL + h : HL + h + 1, :] = edges[h]
        return y_copies(tot_h, 0, slice(0, HL + 1))

    def prefix_h(copies):
        for copy in copies:
            copy.wait_recv()
        runs = [jnp.zeros((rows_h, HD), F32) for _ in range(HL)]
        edges = [jnp.zeros((1, HD), F32) for _ in range(HL)]
        for other in range(ny):
            marks = tot_h[other, 0, 0:8, :]
            factor = jnp.exp(marks[0:HL])
            for h in range(HL):
                runs[h] = jnp.where(other < y, factor[h : h + 1] * runs[h] + tot_h[other, 1 + h], runs[h])
                edges[h] = jnp.where(
                    other < y, factor[h : h + 1] * edges[h] + marks[HL + h : HL + h + 1], edges[h]
                )
        mine = list(edges)
        for other in range(nz):
            marks = buf_h[other, 0, 0:8, :]
            factor = jnp.exp(marks[0:HL])
            for h in range(HL):
                out_h[other, h] = runs[h]
                mine[h] = jnp.where(other == z, edges[h], mine[h])
                runs[h] = factor[h : h + 1] * runs[h] + buf_h[other, 1 + h]
                edges[h] = factor[h : h + 1] * edges[h] + marks[HL + h : HL + h + 1]
        return give_back(out_h, pre_h, 1 + HL, rows_h, slice(0, HL)), mine

    def total_g(first, copies):
        for copy in copies:
            copy.wait_recv()
        for h in range(first, first + PAIR):
            run = jnp.zeros((rows_g, HD), F32)
            for other in range(nz):
                run = jnp.exp(buf_h[other, 0, h : h + 1, :]) * run + buf_g[other, h]
            tot_g[y, h] = run
        return y_copies(tot_g, 1 + first, slice(first, first + PAIR))

    def prefix_g(first, copies):
        for copy in copies:
            copy.wait_recv()
        for h in range(first, first + PAIR):
            run = jnp.zeros((rows_g, HD), F32)
            for other in range(ny):
                factor = jnp.exp(tot_h[other, 0, h : h + 1, :])
                run = jnp.where(other < y, factor * run + tot_g[other, h], run)
            for other in range(nz):
                out_g[other, h] = run
                run = jnp.exp(buf_h[other, 0, h : h + 1, :]) * run + buf_g[other, h]
        return give_back(out_g, pre, 2 + HL + first, rows_g, slice(first, first + PAIR))

    loads[3].wait()
    loads[4].wait()
    loads[5].start()
    for h in range(HL):
        hc = slice(h * HD, (h + 1) * HD)
        ridge_m[h] = jnp.broadcast_to(ridge_ref[:, hc], (HD, HD)).T
        g_in[h, HD : 2 * HD, HD : 2 * HD] = jnp.zeros((HD, HD), BF16)
        for i in range(2):
            a1[i * HL + h, 2 * HD : 3 * HD, HD : 2 * HD] = jnp.zeros((HD, HD), BF16)

    def weights_of(j):
        for h in range(HL):
            hc = slice(h * HD, (h + 1) * HD)
            lag = crow[j, h : h + 1, :] - ccols[j][:, h : h + 1]
            causal = place_r <= place_c
            weight = jnp.where(causal, jnp.exp(jnp.where(causal, lag, 0.0)), 0.0) * norms[j, h]
            high, low = parts(lb[j, HL + h])
            a2[j, h, HD : 2 * HD, 0:HD] = high
            a2[j, h, HD : 2 * HD, HD : 2 * HD] = high
            a2[j, h, 2 * HD : 3 * HD, 0:HD] = low
            a2[j, h, 2 * HD : 3 * HD, HD : 2 * HD] = jnp.zeros((HD, HD), BF16)
            w1[j, h] = weight
            w2[j, h] = weight * norms[j, h]
            query = q_ref[j * SPAN : (j + 1) * SPAN, hc].astype(F32).T
            qt[j, h] = query * lax.rsqrt(jnp.sum(query * query, axis=0, keepdims=True) + 1e-06)

    weights_of(0)
    weights_of(1)
    y_sends = total_h(sends)
    sent += y_sends
    weights_of(2)
    back, edges = prefix_h(y_sends)
    sent += back
    weights_of(3)
    firsts = range(0, HL, PAIR)
    gy_sends = [total_g(first, copies) for first, copies in zip(firsts, g_sends)]
    g_back = [prefix_g(first, copies) for first, copies in zip(firsts, gy_sends)]
    for copies in gy_sends + g_back:
        sent += copies
    for copy in back:
        copy.wait_recv()
    for h in range(HL):
        packed = pre_h[h]
        spread = jnp.concatenate([jnp.where(keep, packed, 0.0), jnp.where(keep, 0.0, packed)], axis=0)
        both = jnp.where(near == 0, spread, spread + spread.T)
        gram_in[h] = jnp.where(near == HD // 2, edges[h], both)

    def system(slot, j, h, state):
        high, low = parts(state)
        a1[slot, 0:HD, :] = a2[j, h, 0:HD, :]
        a1[slot, HD : 2 * HD, 0:HD] = high
        a1[slot, HD : 2 * HD, HD : 2 * HD] = high
        a1[slot, 2 * HD : 3 * HD, 0:HD] = low
        b1[slot, :, 0:HD] = high
        b1[slot, :, HD : 2 * HD] = kt2[j, h, :, 0:SPAN]

    def blocks_of(spans):
        return [(i * HL + h, j, h) for i, j in enumerate(spans) for h in range(HL)]

    def solve(spans):
        blocks = blocks_of(spans)
        norm0, opening = [], []
        for slot, j, h in blocks:
            system(slot, j, h, sdec[j, h : h + 1, :] * gram_in[h] + lb[j, h])
            query = qt[j, h]
            xs[slot] = jnp.zeros((HD, SPAN), F32)
            rs[slot] = query
            ps[slot] = query
            norm0.append(jnp.sum(query * query, axis=0, keepdims=True))
            opening.append(jnp.exp(crow[j, h : h + 1, :]))

        def advance(i, slot, norm, image):
            direction = ps[slot]
            alpha = norm / jnp.sum(direction * image, axis=0, keepdims=True)
            xs[slot] = xs[slot] + alpha * direction
            residual = rs[slot] - alpha * image
            fresh = jnp.sum(residual * residual, axis=0, keepdims=True)
            rs[slot] = residual
            ps[slot] = residual + (fresh / norm) * direction
            return fresh

        def sweep(_, norm):
            n = len(blocks)
            outs, locals_, after = [None] * n, [None] * n, [None] * n
            for i, (slot, j, h) in enumerate(blocks):
                outs[i] = dot(a1[slot], stacked(ps[slot]))
            for i, (slot, j, h) in enumerate(blocks):
                locals_[i] = dot(kt2[j, h], stacked(outs[i][0:HD] * w2[j, h]))
            for i, (slot, j, h) in enumerate(blocks):
                carried = outs[i][HD : 2 * HD] + outs[i][2 * HD : 3 * HD]
                image = opening[i] * carried + locals_[i] + ridge_m[h] * ps[slot]
                after[i] = advance(i, slot, norm[i], image)
            return tuple(after)

        def last_sweep(_, norm):
            n = len(blocks)
            outs, images, after = [None] * n, [None] * n, [None] * n
            for i, (slot, j, h) in enumerate(blocks):
                outs[i] = dot(a1[slot, 0:HD, 0:HD], ps[slot].astype(BF16))
            for i, (slot, j, h) in enumerate(blocks):
                lifted = (opening[i] * ps[slot]).astype(BF16)
                scores = (outs[i] * w2[j, h]).astype(BF16)
                images[i] = dot(b1[slot], jnp.concatenate([lifted, scores], axis=0))
            for i, (slot, j, h) in enumerate(blocks):
                image = images[i] + ridge_m[h] * ps[slot]
                after[i] = advance(i, slot, norm[i], image)
            return tuple(after)

        norm = lax.fori_loop(0, FULL, sweep, tuple(norm0), unroll=UNROLL)
        lax.fori_loop(FULL, ITERS, last_sweep, norm, unroll=2)
        return opening

    def read_local(i, j, opening):
        outs = [dot(a2[j, h], stacked(xs[i * HL + h])) for h in range(HL)]
        for h in range(HL):
            near_part = dot(vt2[j, h], stacked(outs[h][0:HD] * w1[j, h]))
            rs[i * HL + h] = near_part + opening[i * HL + h] * (outs[h][HD : 2 * HD] + outs[h][2 * HD :])

    def take_memory(h):
        high, low = parts(pre[h])
        g_in[h, 0:HD, 0:HD] = high
        g_in[h, 0:HD, HD : 2 * HD] = high
        g_in[h, HD : 2 * HD, 0:HD] = low

    def read_out(k, i, j, opening, heads):
        outs = [dot(g_in[h], stacked(xs[i * HL + h])) for h in heads]
        for h, out in zip(heads, outs):
            lifted = opening[i * HL + h] * sdec[j, h : h + 1, :]
            read = rs[i * HL + h] + lifted * (out[0:HD] + out[HD : 2 * HD])
            read = read * lax.rsqrt(jnp.sum(read * read, axis=0, keepdims=True) * (1.0 / HD) + 1e-06)
            nm[k, :, h * HD : (h + 1) * HD] = read.T.astype(BF16)

    half = SPAN // 2
    width = w_vm.shape[1] // NCH

    def p_copy(k, n):
        return pltpu.make_async_remote_copy(
            src_ref=pout.at[k, n], dst_ref=pin.at[k, n], send_sem=p_send.at[k, n], recv_sem=p_recv.at[k, n],
            device_id=(seq, partner), device_id_type=MESH,
        )

    def project(k, order, use):
        mine = pl.multiple_of(c * half, half)
        other = pl.multiple_of((1 - c) * half, half)
        lhs = jnp.concatenate([nm[k, pl.ds(mine, half), :], nm[k, pl.ds(other, half), :]], axis=0)
        copies = {}
        for i in range(NCH + LAG):
            if i < NCH:
                n = order[i]
                out = dot(lhs, w_vm[:, n * width : (n + 1) * width])
                pown[k, n] = out[0:half]
                pout[k, n] = out[half:]
                copies[n] = p_copy(k, n)
                copies[n].start()
            if i >= LAG:
                use(order[i - LAG], copies)
        return copies

    def join(k, n, copies):
        copies[n].wait_recv()
        pown[k, n] = pown[k, n] + pin[k, n]

    def x_copy(src, dst, send, recv, to):
        copy = pltpu.make_async_remote_copy(
            src_ref=src, dst_ref=dst, send_sem=send, recv_sem=recv,
            device_id=(seq, to), device_id_type=MESH,
        )
        copy.start()
        return copy

    middle = NCH // 2
    js = [lax.rem(x + o, nx) for o in ORDER]

    mixed_order = [(i % 2) * middle + i // 2 for i in range(NCH)]
    relay, final1, final2 = {}, {}, {}

    opening = solve(js[0:1])
    read_local(0, js[0], opening)
    loads[5].wait()
    for first, copies in zip(firsts, g_back):
        for copy in copies:
            copy.wait_recv()
        for h in range(first, first + PAIR):
            take_memory(h)
        read_out(0, 0, js[0], opening, tuple(range(first, first + PAIR)))

    def send_relay(n, copies):
        join(0, n, copies)
        if n < middle:
            relay[n] = x_copy(pown.at[0, n], ra.at[n], r_send.at[n], r_recv.at[n], right)
        else:
            relay[n] = x_copy(pown.at[0, n], rb.at[n - middle], r_send.at[n], r_recv.at[n], left)

    copies = project(0, mixed_order, send_relay)
    sent += list(copies.values()) + list(relay.values())

    def send_right(n, copies):
        if n >= middle:
            join(1, n, copies)
            final1[n] = x_copy(pown.at[1, n], f1.at[n], f_send.at[0, n], f_recv.at[0, n], right)

    def send_left(n, copies):
        if n < middle:
            join(2, n, copies)
            final2[n] = x_copy(pown.at[2, n], f2.at[n], f_send.at[1, n], f_recv.at[1, n], left)

    opening = solve(js[1:3])
    every = tuple(range(HL))
    read_local(0, js[1], opening)
    read_out(1, 0, js[1], opening, every)
    copies1 = project(1, list(range(middle, NCH)) + list(range(middle)), send_right)
    read_local(1, js[2], opening)
    read_out(2, 1, js[2], opening, every)
    copies2 = project(2, list(range(NCH)), send_left)
    for n in range(middle):
        relay[n].wait_recv()
        join(1, n, copies1)
        pown[1, n] = pown[1, n] + ra[n]
        final1[n] = x_copy(pown.at[1, n], f1.at[n], f_send.at[0, n], f_recv.at[0, n], right)
        m = n + middle
        relay[m].wait_recv()
        join(2, m, copies2)
        pown[2, m] = pown[2, m] + rb[n]
        final2[m] = x_copy(pown.at[2, m], f2.at[m], f_send.at[1, m], f_recv.at[1, m], left)
    sent += list(copies1.values()) + list(copies2.values())

    opening = solve(js[3:4])
    read_local(0, js[3], opening)
    read_out(3, 0, js[3], opening, every)
    copies3 = project(3, list(range(NCH)), functools.partial(join, 3))
    sent += list(copies3.values())
    for copy in sent:
        copy.wait_send()
    for i in range(NCH):
        n = (i % 2) * middle + i // 2
        m = (n + middle) % NCH
        final1[m].wait_recv()
        final2[n].wait_recv()
        if i % 2 == 1:
            for e in (n, m):
                o_ref[:, e * width : (e + 1) * width] = (pown[3, e] + f1[e] + f2[e]).astype(BF16)
    for copy in list(final1.values()) + list(final2.values()):
        copy.wait_send()


def solution(mesh, ny=4, nz=8):
    nx = mesh.shape["wide"] // 2

    def body(queries, keys, values, log_decay, ridge, out_weight):
        columns = out_weight.shape[1]
        width = columns // NCH
        half = SPAN // 2
        rows_h, rows_g = HD // 2 // nz, HD // nz
        tokens, inner = queries.shape
        vm = pltpu.VMEM
        dma = pltpu.SemaphoreType.DMA
        scratch = [
            vm((tokens, inner), BF16),
            vm((tokens, inner), BF16),
            vm((tokens, inner), BF16),
            vm((HL, tokens), F32),
            vm((1, inner), F32),
            vm(out_weight.shape, BF16),
            vm((HL + 1, HD // 2, HD), F32),
            vm((HL, HD, HD), F32),
            vm((nz, HL + 1, rows_h, HD), F32),
            vm((nz, HL, rows_g, HD), F32),
            vm((ny, HL + 1, rows_h, HD), F32),
            vm((ny, HL, rows_g, HD), F32),
            vm((nz, HL, rows_h, HD), F32),
            vm((nz, HL, rows_g, HD), F32),
            vm((HL, HD // 2, HD), F32),
            vm((HL, HD, HD), F32),
            vm((NJ, 2 * HL, HD, HD), F32),
            vm((NJ, 8, HD), F32),
            vm((NJ, 8, HD), F32),
            vm((NJ, HL, SPAN, SPAN), F32),
            vm((NJ, HL, SPAN, SPAN), F32),
            vm((NJ, HL, HD, 2 * SPAN), BF16),
            vm((NJ, HL, HD, 2 * SPAN), BF16),
            vm((NJ, HL, HD, SPAN), F32),
            vm((HL, HD, SPAN), F32),
            vm((HL, HD, HD), F32),
            vm((HL, 2 * HD, 2 * HD), BF16),
            vm((2 * HL, 3 * HD, 2 * HD), BF16),
            vm((2 * HL, HD, 2 * HD), BF16),
            vm((NJ, HL, 3 * HD, 2 * HD), BF16),
            vm((2 * HL, HD, SPAN), F32),
            vm((2 * HL, HD, SPAN), F32),
            vm((2 * HL, HD, SPAN), F32),
            vm((NJ, SPAN, HL * HD), BF16),
            vm((NJ, NCH, half, width), F32),
            vm((NJ, NCH, half, width), F32),
            vm((NJ, NCH, half, width), F32),
            vm((NCH // 2, half, width), F32),
            vm((NCH // 2, half, width), F32),
            vm((NCH, half, width), F32),
            vm((NCH, half, width), F32),
            dma((6,)),
            dma((2 * HL + 2, nz)),
            dma((2 * HL + 2, nz)),
            dma((HL + 1, ny)),
            dma((HL + 1, ny)),
            dma((NJ, NCH)),
            dma((NJ, NCH)),
            dma((NCH,)),
            dma((NCH,)),
            dma((2, NCH)),
            dma((2, NCH)),
        ]
        space = pl.BlockSpec(memory_space=pltpu.VMEM)
        return pl.pallas_call(
            functools.partial(kernel, ny, nz, nx),
            out_shape=jax.ShapeDtypeStruct((queries.shape[0] // (2 * nx), columns), BF16),
            in_specs=[pl.BlockSpec(memory_space=pl.ANY)] * 6,
            out_specs=space,
            scratch_shapes=scratch,
            compiler_params=pltpu.CompilerParams(
                collective_id=0, has_side_effects=True, vmem_limit_bytes=60 << 20
            ),
        )(queries, keys, values, log_decay.T, ridge[None, :], out_weight)

    placed = (
        P("seq", "wide"),
        P("seq", "wide"),
        P("seq", "wide"),
        P("seq", "wide"),
        P("wide"),
        P("wide", None),
    )
    return jax.shard_map(
        body, mesh=mesh, in_specs=placed, out_specs=P(("seq", "wide"), None), check_vma=False
    )
```

```python
import functools

import jax
import jax.numpy as jnp
from jax import lax
from jax.experimental import pallas as pl
from jax.experimental.pallas import tpu as pltpu
from jax.sharding import PartitionSpec as P

MESH = pl.DeviceIdType.MESH
F32 = jnp.float32
BF16 = jnp.bfloat16
HD = 128
SPAN = 128
ITERS = 8
UNROLL = 3
FULL = 6
LAG = 4
PAIR = 2
HL = 4
NJ = 4
NCH = 8
ORDER = (2, 1, 3, 0)
highest = lax.Precision.HIGHEST


def parts(value):
    high = value.astype(BF16)
    return high, (value - high.astype(F32)).astype(BF16)


def stacked(value):
    return jnp.concatenate(parts(value), axis=0)


def dot(a, b):
    return jnp.dot(a, b, preferred_element_type=F32)


def kernel(
    ny, nz, nx,
    q_hbm, k_hbm, v_hbm, ld_hbm, ridge_hbm, w_hbm, o_ref,
    q_ref, k_ref, v_ref, ld_ref, ridge_ref, w_vm,
    st_h, st_g, buf_h, buf_g, tot_h, tot_g, out_h, out_g, pre_h, pre, lb, sdec, crow, w1, w2, kt2, vt2, qt, ridge_m,
    gram_in, g_in, a1, b1, a2, xs, rs, ps, nm, pown, pout, pin, ra, rb, f1, f2,
    load_sem, z_send, z_recv, y_send, y_recv, p_send, p_recv, r_send, r_recv, f_send, f_recv,
):
    seq = lax.axis_index("seq")
    wide = lax.axis_index("wide")
    y, z = lax.div(seq, nz), lax.rem(seq, nz)
    x, c = lax.div(wide, 2), lax.rem(wide, 2)
    rows_h, rows_g = HD // 2 // nz, HD // nz
    partner = x * 2 + (1 - c)
    right = lax.rem(x + 1, nx) * 2 + c
    left = lax.rem(x + nx - 1, nx) * 2 + c

    loads = [
        pltpu.make_async_copy(src, dst, load_sem.at[i])
        for i, (src, dst) in enumerate(
            (
                (ld_hbm, ld_ref), (k_hbm, k_ref), (v_hbm, v_ref),
                (q_hbm, q_ref), (ridge_hbm, ridge_ref), (w_hbm, w_vm),
            )
        )
    ]
    for load in loads[:5]:
        load.start()

    barrier = pltpu.get_barrier_semaphore()
    for step in range(1, nz):
        to = y * nz + lax.rem(z + step, nz)
        pl.semaphore_signal(barrier, inc=1, device_id=(to, wide), device_id_type=MESH)
    for step in range(1, ny):
        to = lax.rem(y + step, ny) * nz + z
        pl.semaphore_signal(barrier, inc=1, device_id=(to, wide), device_id_type=MESH)
    for to in (partner, right, left):
        pl.semaphore_signal(barrier, inc=1, device_id=(seq, to), device_id_type=MESH)

    place_r = lax.broadcasted_iota(jnp.int32, (SPAN, SPAN), 0)
    place_c = lax.broadcasted_iota(jnp.int32, (SPAN, SPAN), 1)
    lower = (place_r >= place_c).astype(F32)
    upper = (place_r <= place_c).astype(F32)
    ccols, norms = [], {}
    loads[0].wait()
    total = jnp.zeros((1, HL), F32)
    closings = []
    for j in range(NJ):
        decay = ld_ref[:, j * SPAN : (j + 1) * SPAN]
        ccol = lax.dot_general(
            lower, decay, (((1,), (1,)), ((), ())), precision=highest, preferred_element_type=F32
        )
        ccols.append(ccol)
        crow[j, 0:HL, :] = jnp.dot(decay, upper, precision=highest, preferred_element_type=F32)
        for h in range(HL):
            sdec[j, h : h + 1, :] = jnp.exp(jnp.broadcast_to(total[:, h : h + 1], (1, HD)))
        closing = ccol[SPAN - 1 : SPAN, :]
        closings.append(closing)
        total = total + closing
    group = lax.rem(lax.broadcasted_iota(jnp.int32, (HD // 2, HD), 0), rows_h)
    near = lax.rem(place_c - place_r + HD, HD)
    keep = near[0 : HD // 2] < HD // 2
    marks = jnp.zeros((HD // 2, HD), F32)
    loads[1].wait()

    for h in range(HL):
        hc = slice(h * HD, (h + 1) * HD)
        run = jnp.zeros((HD, HD), F32)
        for j in range(NJ):
            keys = k_ref[j * SPAN : (j + 1) * SPAN, hc]
            a2[j, h, 0:HD, 0:HD] = keys
            a2[j, h, 0:HD, HD : 2 * HD] = keys
            keyf = keys.astype(F32)
            norm = lax.rsqrt(jnp.sum(keyf * keyf, axis=1, keepdims=True) + 1e-06)
            norms[j, h] = norm
            keyt = keyf.T.astype(BF16)
            kt2[j, h, :, 0:HD] = keyt
            kt2[j, h, :, HD : 2 * HD] = keyt
            fade = jnp.exp(closings[j][:, h : h + 1] - ccols[j][:, h : h + 1])
            gram = dot(kt2[j, h], stacked(keyf * (fade * norm * norm)))
            lb[j, h] = run
            run = jnp.exp(closings[j][:, h : h + 1]) * run + gram
        st_h[1 + h] = jnp.where(keep, run[0 : HD // 2], run[HD // 2 :])
        edge = jnp.sum(jnp.where(near == HD // 2, run, 0.0), axis=0, keepdims=True)
        marks = jnp.where(group == h, jnp.broadcast_to(total[:, h : h + 1], marks.shape), marks)
        marks = jnp.where(group == HL + h, edge, marks)
    st_h[0] = marks

    pl.semaphore_wait(barrier, nz + ny + 1)

    def z_copy(src, dst, slot, step):
        to = y * nz + lax.rem(z + step, nz)
        return pltpu.make_async_remote_copy(
            src_ref=src, dst_ref=dst, send_sem=z_send.at[slot, step], recv_sem=z_recv.at[slot, step],
            device_id=(to, wide), device_id_type=MESH,
        )

    def scatter(st, buf, slot, rows, part):
        copies = []
        for step in range(1, nz):
            peer = lax.rem(z + step, nz)
            start = pl.multiple_of(peer * rows, rows)
            copies.append(z_copy(st.at[part, pl.ds(start, rows), :], buf.at[z, part], slot, step))
            copies[-1].start()
        mine = pl.multiple_of(z * rows, rows)
        buf[z, part] = st[part, pl.ds(mine, rows), :]
        return copies

    sends = scatter(st_h, buf_h, 0, rows_h, slice(0, HL + 1))
    sent = list(sends)
    g_sends = []
    loads[2].wait()

    for h in range(HL):
        hc = slice(h * HD, (h + 1) * HD)
        run = jnp.zeros((HD, HD), F32)
        for j in range(NJ):
            keyf = k_ref[j * SPAN : (j + 1) * SPAN, hc].astype(F32)
            valt = v_ref[j * SPAN : (j + 1) * SPAN, hc].astype(F32).T.astype(BF16)
            vt2[j, h, :, 0:HD] = valt
            vt2[j, h, :, HD : 2 * HD] = valt
            fade = jnp.exp(closings[j][:, h : h + 1] - ccols[j][:, h : h + 1])
            memory = dot(vt2[j, h], stacked(keyf * (fade * norms[j, h])))
            lb[j, HL + h] = run
            run = jnp.exp(closings[j][:, h : h + 1]) * run + memory
        st_g[h] = run
        if h % PAIR == PAIR - 1:
            g_sends.append(scatter(st_g, buf_g, 1 + h, rows_g, slice(h + 1 - PAIR, h + 1)))
            sent += g_sends[-1]

    def y_copies(buf, slot, part):
        copies = []
        for step in range(1, ny):
            to = lax.rem(y + step, ny) * nz + z
            copies.append(
                pltpu.make_async_remote_copy(
                    src_ref=buf.at[y, part], dst_ref=buf.at[y, part],
                    send_sem=y_send.at[slot, step], recv_sem=y_recv.at[slot, step],
                    device_id=(to, wide), device_id_type=MESH,
                )
            )
            copies[-1].start()
        return copies

    def give_back(buf, pre, slot, rows, part):
        mine = pl.multiple_of(z * rows, rows)
        copies = []
        for step in range(1, nz):
            peer = lax.rem(z + step, nz)
            copies.append(
                z_copy(buf.at[peer, part], pre.at[part, pl.ds(mine, rows), :], slot, step)
            )
            copies[-1].start()
        pre[part, pl.ds(mine, rows), :] = buf[z, part]
        return copies

    def total_h(copies):
        for copy in copies:
            copy.wait_recv()
        sums = [jnp.zeros((rows_h, HD), F32) for _ in range(HL)]
        edges = [jnp.zeros((1, HD), F32) for _ in range(HL)]
        decay = jnp.zeros((8, HD), F32)
        for other in range(nz):
            marks = buf_h[other, 0, 0:8, :]
            factor = jnp.exp(marks[0:HL])
            decay = decay + marks
            for h in range(HL):
                sums[h] = factor[h : h + 1] * sums[h] + buf_h[other, 1 + h]
                edges[h] = factor[h : h + 1] * edges[h] + marks[HL + h : HL + h + 1]
        tot_h[y, 0, 0:8, :] = decay
        for h in range(HL):
            tot_h[y, 1 + h] = sums[h]
            tot_h[y, 0, HL + h : HL + h + 1, :] = edges[h]
        return y_copies(tot_h, 0, slice(0, HL + 1))

    def prefix_h(copies):
        for copy in copies:
            copy.wait_recv()
        runs = [jnp.zeros((rows_h, HD), F32) for _ in range(HL)]
        edges = [jnp.zeros((1, HD), F32) for _ in range(HL)]
        for other in range(ny):
            marks = tot_h[other, 0, 0:8, :]
            factor = jnp.exp(marks[0:HL])
            for h in range(HL):
                runs[h] = jnp.where(other < y, factor[h : h + 1] * runs[h] + tot_h[other, 1 + h], runs[h])
                edges[h] = jnp.where(
                    other < y, factor[h : h + 1] * edges[h] + marks[HL + h : HL + h + 1], edges[h]
                )
        mine = list(edges)
        for other in range(nz):
            marks = buf_h[other, 0, 0:8, :]
            factor = jnp.exp(marks[0:HL])
            for h in range(HL):
                out_h[other, h] = runs[h]
                mine[h] = jnp.where(other == z, edges[h], mine[h])
                runs[h] = factor[h : h + 1] * runs[h] + buf_h[other, 1 + h]
                edges[h] = factor[h : h + 1] * edges[h] + marks[HL + h : HL + h + 1]
        return give_back(out_h, pre_h, 1 + HL, rows_h, slice(0, HL)), mine

    def total_g(first, copies):
        for copy in copies:
            copy.wait_recv()
        for h in range(first, first + PAIR):
            run = jnp.zeros((rows_g, HD), F32)
            for other in range(nz):
                run = jnp.exp(buf_h[other, 0, h : h + 1, :]) * run + buf_g[other, h]
            tot_g[y, h] = run
        return y_copies(tot_g, 1 + first, slice(first, first + PAIR))

    def prefix_g(first, copies):
        for copy in copies:
            copy.wait_recv()
        for h in range(first, first + PAIR):
            run = jnp.zeros((rows_g, HD), F32)
            for other in range(ny):
                factor = jnp.exp(tot_h[other, 0, h : h + 1, :])
                run = jnp.where(other < y, factor * run + tot_g[other, h], run)
            for other in range(nz):
                out_g[other, h] = run
                run = jnp.exp(buf_h[other, 0, h : h + 1, :]) * run + buf_g[other, h]
        return give_back(out_g, pre, 2 + HL + first, rows_g, slice(first, first + PAIR))

    loads[3].wait()
    loads[4].wait()
    loads[5].start()
    for h in range(HL):
        hc = slice(h * HD, (h + 1) * HD)
        ridge_m[h] = jnp.broadcast_to(ridge_ref[:, hc], (HD, HD)).T
        g_in[h, HD : 2 * HD, HD : 2 * HD] = jnp.zeros((HD, HD), BF16)
        for i in range(2):
            a1[i * HL + h, 2 * HD : 3 * HD, HD : 2 * HD] = jnp.zeros((HD, HD), BF16)

    def weights_of(j):
        for h in range(HL):
            hc = slice(h * HD, (h + 1) * HD)
            lag = crow[j, h : h + 1, :] - ccols[j][:, h : h + 1]
            causal = place_r <= place_c
            weight = jnp.where(causal, jnp.exp(jnp.where(causal, lag, 0.0)), 0.0) * norms[j, h]
            high, low = parts(lb[j, HL + h])
            a2[j, h, HD : 2 * HD, 0:HD] = high
            a2[j, h, HD : 2 * HD, HD : 2 * HD] = high
            a2[j, h, 2 * HD : 3 * HD, 0:HD] = low
            a2[j, h, 2 * HD : 3 * HD, HD : 2 * HD] = jnp.zeros((HD, HD), BF16)
            w1[j, h] = weight
            w2[j, h] = weight * norms[j, h]
            query = q_ref[j * SPAN : (j + 1) * SPAN, hc].astype(F32).T
            qt[j, h] = query * lax.rsqrt(jnp.sum(query * query, axis=0, keepdims=True) + 1e-06)

    weights_of(0)
    weights_of(1)
    y_sends = total_h(sends)
    sent += y_sends
    weights_of(2)
    back, edges = prefix_h(y_sends)
    sent += back
    weights_of(3)
    firsts = range(0, HL, PAIR)
    gy_sends = [total_g(first, copies) for first, copies in zip(firsts, g_sends)]
    g_back = [prefix_g(first, copies) for first, copies in zip(firsts, gy_sends)]
    for copies in gy_sends + g_back:
        sent += copies
    for copy in back:
        copy.wait_recv()
    for h in range(HL):
        packed = pre_h[h]
        spread = jnp.concatenate([jnp.where(keep, packed, 0.0), jnp.where(keep, 0.0, packed)], axis=0)
        both = jnp.where(near == 0, spread, spread + spread.T)
        gram_in[h] = jnp.where(near == HD // 2, edges[h], both)

    def system(slot, j, h, state):
        high, low = parts(state)
        a1[slot, 0:HD, :] = a2[j, h, 0:HD, :]
        a1[slot, HD : 2 * HD, 0:HD] = high
        a1[slot, HD : 2 * HD, HD : 2 * HD] = high
        a1[slot, 2 * HD : 3 * HD, 0:HD] = low
        b1[slot, :, 0:HD] = high
        b1[slot, :, HD : 2 * HD] = kt2[j, h, :, 0:SPAN]

    def blocks_of(spans):
        return [(i * HL + h, j, h) for i, j in enumerate(spans) for h in range(HL)]

    def solve(spans):
        blocks = blocks_of(spans)
        norm0, opening = [], []
        for slot, j, h in blocks:
            system(slot, j, h, sdec[j, h : h + 1, :] * gram_in[h] + lb[j, h])
            query = qt[j, h]
            xs[slot] = jnp.zeros((HD, SPAN), F32)
            rs[slot] = query
            ps[slot] = query
            norm0.append(jnp.sum(query * query, axis=0, keepdims=True))
            opening.append(jnp.exp(crow[j, h : h + 1, :]))

        def advance(i, slot, norm, image):
            direction = ps[slot]
            alpha = norm / jnp.sum(direction * image, axis=0, keepdims=True)
            xs[slot] = xs[slot] + alpha * direction
            residual = rs[slot] - alpha * image
            fresh = jnp.sum(residual * residual, axis=0, keepdims=True)
            rs[slot] = residual
            ps[slot] = residual + (fresh / norm) * direction
            return fresh

        def sweep(_, norm):
            n = len(blocks)
            outs, locals_, after = [None] * n, [None] * n, [None] * n
            for i, (slot, j, h) in enumerate(blocks):
                outs[i] = dot(a1[slot], stacked(ps[slot]))
            for i, (slot, j, h) in enumerate(blocks):
                locals_[i] = dot(kt2[j, h], stacked(outs[i][0:HD] * w2[j, h]))
            for i, (slot, j, h) in enumerate(blocks):
                carried = outs[i][HD : 2 * HD] + outs[i][2 * HD : 3 * HD]
                image = opening[i] * carried + locals_[i] + ridge_m[h] * ps[slot]
                after[i] = advance(i, slot, norm[i], image)
            return tuple(after)

        def last_sweep(_, norm):
            n = len(blocks)
            outs, images, after = [None] * n, [None] * n, [None] * n
            for i, (slot, j, h) in enumerate(blocks):
                outs[i] = dot(a1[slot, 0:HD, 0:HD], ps[slot].astype(BF16))
            for i, (slot, j, h) in enumerate(blocks):
                lifted = (opening[i] * ps[slot]).astype(BF16)
                scores = (outs[i] * w2[j, h]).astype(BF16)
                images[i] = dot(b1[slot], jnp.concatenate([lifted, scores], axis=0))
            for i, (slot, j, h) in enumerate(blocks):
                image = images[i] + ridge_m[h] * ps[slot]
                after[i] = advance(i, slot, norm[i], image)
            return tuple(after)

        norm = lax.fori_loop(0, FULL, sweep, tuple(norm0), unroll=UNROLL)
        lax.fori_loop(FULL, ITERS, last_sweep, norm, unroll=2)
        return opening

    def read_local(i, j, opening):
        outs = [dot(a2[j, h], stacked(xs[i * HL + h])) for h in range(HL)]
        for h in range(HL):
            near_part = dot(vt2[j, h], stacked(outs[h][0:HD] * w1[j, h]))
            rs[i * HL + h] = near_part + opening[i * HL + h] * (outs[h][HD : 2 * HD] + outs[h][2 * HD :])

    def take_memory(h):
        high, low = parts(pre[h])
        g_in[h, 0:HD, 0:HD] = high
        g_in[h, 0:HD, HD : 2 * HD] = high
        g_in[h, HD : 2 * HD, 0:HD] = low

    def read_out(k, i, j, opening, heads):
        outs = [dot(g_in[h], stacked(xs[i * HL + h])) for h in heads]
        for h, out in zip(heads, outs):
            lifted = opening[i * HL + h] * sdec[j, h : h + 1, :]
            read = rs[i * HL + h] + lifted * (out[0:HD] + out[HD : 2 * HD])
            read = read * lax.rsqrt(jnp.sum(read * read, axis=0, keepdims=True) * (1.0 / HD) + 1e-06)
            nm[k, :, h * HD : (h + 1) * HD] = read.T.astype(BF16)

    half = SPAN // 2
    width = w_vm.shape[1] // NCH

    def p_copy(k, n):
        return pltpu.make_async_remote_copy(
            src_ref=pout.at[k, n], dst_ref=pin.at[k, n], send_sem=p_send.at[k, n], recv_sem=p_recv.at[k, n],
            device_id=(seq, partner), device_id_type=MESH,
        )

    def project(k, order, use):
        mine = pl.multiple_of(c * half, half)
        other = pl.multiple_of((1 - c) * half, half)
        lhs = jnp.concatenate([nm[k, pl.ds(mine, half), :], nm[k, pl.ds(other, half), :]], axis=0)
        copies = {}
        for i in range(NCH + LAG):
            if i < NCH:
                n = order[i]
                out = dot(lhs, w_vm[:, n * width : (n + 1) * width])
                pown[k, n] = out[0:half]
                pout[k, n] = out[half:]
                copies[n] = p_copy(k, n)
                copies[n].start()
            if i >= LAG:
                use(order[i - LAG], copies)
        return copies

    def join(k, n, copies):
        copies[n].wait_recv()
        pown[k, n] = pown[k, n] + pin[k, n]

    def x_copy(src, dst, send, recv, to):
        copy = pltpu.make_async_remote_copy(
            src_ref=src, dst_ref=dst, send_sem=send, recv_sem=recv,
            device_id=(seq, to), device_id_type=MESH,
        )
        copy.start()
        return copy

    middle = NCH // 2
    js = [lax.rem(x + o, nx) for o in ORDER]

    mixed_order = [(i % 2) * middle + i // 2 for i in range(NCH)]
    relay, final1, final2 = {}, {}, {}

    opening = solve(js[0:1])
    read_local(0, js[0], opening)
    loads[5].wait()
    for first, copies in zip(firsts, g_back):
        for copy in copies:
            copy.wait_recv()
        for h in range(first, first + PAIR):
            take_memory(h)
        read_out(0, 0, js[0], opening, tuple(range(first, first + PAIR)))

    def send_relay(n, copies):
        join(0, n, copies)
        if n < middle:
            relay[n] = x_copy(pown.at[0, n], ra.at[n], r_send.at[n], r_recv.at[n], right)
        else:
            relay[n] = x_copy(pown.at[0, n], rb.at[n - middle], r_send.at[n], r_recv.at[n], left)

    copies = project(0, mixed_order, send_relay)
    sent += list(copies.values()) + list(relay.values())

    def send_right(n, copies):
        if n >= middle:
            join(1, n, copies)
            final1[n] = x_copy(pown.at[1, n], f1.at[n], f_send.at[0, n], f_recv.at[0, n], right)

    def send_left(n, copies):
        if n < middle:
            join(2, n, copies)
            final2[n] = x_copy(pown.at[2, n], f2.at[n], f_send.at[1, n], f_recv.at[1, n], left)

    opening = solve(js[1:3])
    every = tuple(range(HL))
    read_local(0, js[1], opening)
    read_out(1, 0, js[1], opening, every)
    copies1 = project(1, list(range(middle, NCH)) + list(range(middle)), send_right)
    read_local(1, js[2], opening)
    read_out(2, 1, js[2], opening, every)
    copies2 = project(2, list(range(NCH)), send_left)
    for n in range(middle):
        relay[n].wait_recv()
        join(1, n, copies1)
        pown[1, n] = pown[1, n] + ra[n]
        final1[n] = x_copy(pown.at[1, n], f1.at[n], f_send.at[0, n], f_recv.at[0, n], right)
        m = n + middle
        relay[m].wait_recv()
        join(2, m, copies2)
        pown[2, m] = pown[2, m] + rb[n]
        final2[m] = x_copy(pown.at[2, m], f2.at[m], f_send.at[1, m], f_recv.at[1, m], left)
    sent += list(copies1.values()) + list(copies2.values())

    opening = solve(js[3:4])
    read_local(0, js[3], opening)
    read_out(3, 0, js[3], opening, every)
    copies3 = project(3, list(range(NCH)), functools.partial(join, 3))
    sent += list(copies3.values())
    for copy in sent:
        copy.wait_send()
    for i in range(NCH):
        n = (i % 2) * middle + i // 2
        m = (n + middle) % NCH
        final1[m].wait_recv()
        final2[n].wait_recv()
        if i % 2 == 1:
            for e in (n, m):
                o_ref[:, e * width : (e + 1) * width] = (pown[3, e] + f1[e] + f2[e]).astype(BF16)
    for copy in list(final1.values()) + list(final2.values()):
        copy.wait_send()


def solution(mesh, ny=4, nz=8):
    nx = mesh.shape["wide"] // 2

    def body(queries, keys, values, log_decay, ridge, out_weight):
        columns = out_weight.shape[1]
        width = columns // NCH
        half = SPAN // 2
        rows_h, rows_g = HD // 2 // nz, HD // nz
        tokens, inner = queries.shape
        vm = pltpu.VMEM
        dma = pltpu.SemaphoreType.DMA
        scratch = [
            vm((tokens, inner), BF16),
            vm((tokens, inner), BF16),
            vm((tokens, inner), BF16),
            vm((HL, tokens), F32),
            vm((1, inner), F32),
            vm(out_weight.shape, BF16),
            vm((HL + 1, HD // 2, HD), F32),
            vm((HL, HD, HD), F32),
            vm((nz, HL + 1, rows_h, HD), F32),
            vm((nz, HL, rows_g, HD), F32),
            vm((ny, HL + 1, rows_h, HD), F32),
            vm((ny, HL, rows_g, HD), F32),
            vm((nz, HL, rows_h, HD), F32),
            vm((nz, HL, rows_g, HD), F32),
            vm((HL, HD // 2, HD), F32),
            vm((HL, HD, HD), F32),
            vm((NJ, 2 * HL, HD, HD), F32),
            vm((NJ, 8, HD), F32),
            vm((NJ, 8, HD), F32),
            vm((NJ, HL, SPAN, SPAN), F32),
            vm((NJ, HL, SPAN, SPAN), F32),
            vm((NJ, HL, HD, 2 * SPAN), BF16),
            vm((NJ, HL, HD, 2 * SPAN), BF16),
            vm((NJ, HL, HD, SPAN), F32),
            vm((HL, HD, SPAN), F32),
            vm((HL, HD, HD), F32),
            vm((HL, 2 * HD, 2 * HD), BF16),
            vm((2 * HL, 3 * HD, 2 * HD), BF16),
            vm((2 * HL, HD, 2 * HD), BF16),
            vm((NJ, HL, 3 * HD, 2 * HD), BF16),
            vm((2 * HL, HD, SPAN), F32),
            vm((2 * HL, HD, SPAN), F32),
            vm((2 * HL, HD, SPAN), F32),
            vm((NJ, SPAN, HL * HD), BF16),
            vm((NJ, NCH, half, width), F32),
            vm((NJ, NCH, half, width), F32),
            vm((NJ, NCH, half, width), F32),
            vm((NCH // 2, half, width), F32),
            vm((NCH // 2, half, width), F32),
            vm((NCH, half, width), F32),
            vm((NCH, half, width), F32),
            dma((6,)),
            dma((2 * HL + 2, nz)),
            dma((2 * HL + 2, nz)),
            dma((HL + 1, ny)),
            dma((HL + 1, ny)),
            dma((NJ, NCH)),
            dma((NJ, NCH)),
            dma((NCH,)),
            dma((NCH,)),
            dma((2, NCH)),
            dma((2, NCH)),
        ]
        space = pl.BlockSpec(memory_space=pltpu.VMEM)
        return pl.pallas_call(
            functools.partial(kernel, ny, nz, nx),
            out_shape=jax.ShapeDtypeStruct((queries.shape[0] // (2 * nx), columns), BF16),
            in_specs=[pl.BlockSpec(memory_space=pl.ANY)] * 6,
            out_specs=space,
            scratch_shapes=scratch,
            compiler_params=pltpu.CompilerParams(
                collective_id=0, has_side_effects=True, vmem_limit_bytes=50000 << 10
            ),
        )(*(pltpu.with_memory_space_constraint(a, pltpu.HBM) for a in (queries, keys, values, log_decay.T, ridge[None, :], out_weight)))

    placed = (
        P("seq", "wide"),
        P("seq", "wide"),
        P("seq", "wide"),
        P("seq", "wide"),
        P("wide"),
        P("wide", None),
    )
    return jax.shard_map(
        body, mesh=mesh, in_specs=placed, out_specs=P(("seq", "wide"), None), check_vma=False
    )
```

```python
import functools

import jax
import jax.numpy as jnp
from jax import lax
from jax.experimental import pallas as pl
from jax.experimental.pallas import tpu as pltpu
from jax.sharding import PartitionSpec as P

MESH = pl.DeviceIdType.MESH
F32 = jnp.float32
BF16 = jnp.bfloat16
HD = 128
SPAN = 128
ITERS = 8
UNROLL = 3
FULL = 6
LAG = 4
PAIR = 2
HL = 4
NJ = 4
NCH = 8
ORDER = (2, 1, 3, 0)
highest = lax.Precision.HIGHEST


def parts(value):
    high = value.astype(BF16)
    return high, (value - high.astype(F32)).astype(BF16)


def stacked(value):
    return jnp.concatenate(parts(value), axis=0)


def dot(a, b):
    return jnp.dot(a, b, preferred_element_type=F32)


def kernel(
    ny, nz, nx,
    q_hbm, k_hbm, v_hbm, ld_hbm, ridge_hbm, w_hbm, o_ref,
    q_ref, k_ref, v_ref, ld_ref, ridge_ref, w_vm,
    st_h, st_g, buf_h, buf_g, tot_h, tot_g, out_h, out_g, pre_h, pre, lb, sdec, crow, w1, w2, kt2, vt2, qt, ridge_m,
    gram_in, g_in, a1, b1, a2, xs, rs, ps, nm, pown, pout, pin, ra, rb, f1, f2,
    load_sem, z_send, z_recv, y_send, y_recv, p_send, p_recv, r_send, r_recv, f_send, f_recv,
):
    seq = lax.axis_index("seq")
    wide = lax.axis_index("wide")
    y, z = lax.div(seq, nz), lax.rem(seq, nz)
    x, c = lax.div(wide, 2), lax.rem(wide, 2)
    rows_h, rows_g = HD // 2 // nz, HD // nz
    partner = x * 2 + (1 - c)
    right = lax.rem(x + 1, nx) * 2 + c
    left = lax.rem(x + nx - 1, nx) * 2 + c

    loads = [
        pltpu.make_async_copy(src, dst, load_sem.at[i])
        for i, (src, dst) in enumerate(
            (
                (ld_hbm, ld_ref), (k_hbm, k_ref), (v_hbm, v_ref),
                (q_hbm, q_ref), (ridge_hbm, ridge_ref), (w_hbm, w_vm),
            )
        )
    ]
    for load in loads[:5]:
        load.start()

    barrier = pltpu.get_barrier_semaphore()
    for step in range(1, nz):
        to = y * nz + lax.rem(z + step, nz)
        pl.semaphore_signal(barrier, inc=1, device_id=(to, wide), device_id_type=MESH)
    for step in range(1, ny):
        to = lax.rem(y + step, ny) * nz + z
        pl.semaphore_signal(barrier, inc=1, device_id=(to, wide), device_id_type=MESH)
    for to in (partner, right, left):
        pl.semaphore_signal(barrier, inc=1, device_id=(seq, to), device_id_type=MESH)

    place_r = lax.broadcasted_iota(jnp.int32, (SPAN, SPAN), 0)
    place_c = lax.broadcasted_iota(jnp.int32, (SPAN, SPAN), 1)
    lower = (place_r >= place_c).astype(F32)
    upper = (place_r <= place_c).astype(F32)
    ccols, norms = [], {}
    loads[0].wait()
    total = jnp.zeros((1, HL), F32)
    closings = []
    for j in range(NJ):
        decay = ld_ref[:, j * SPAN : (j + 1) * SPAN]
        ccol = lax.dot_general(
            lower, decay, (((1,), (1,)), ((), ())), precision=highest, preferred_element_type=F32
        )
        ccols.append(ccol)
        crow[j, 0:HL, :] = jnp.dot(decay, upper, precision=highest, preferred_element_type=F32)
        for h in range(HL):
            sdec[j, h : h + 1, :] = jnp.exp(jnp.broadcast_to(total[:, h : h + 1], (1, HD)))
        closing = ccol[SPAN - 1 : SPAN, :]
        closings.append(closing)
        total = total + closing
    group = lax.rem(lax.broadcasted_iota(jnp.int32, (HD // 2, HD), 0), rows_h)
    near = lax.rem(place_c - place_r + HD, HD)
    keep = near[0 : HD // 2] < HD // 2
    marks = jnp.zeros((HD // 2, HD), F32)
    loads[1].wait()

    for h in range(HL):
        hc = slice(h * HD, (h + 1) * HD)
        run = jnp.zeros((HD, HD), F32)
        for j in range(NJ):
            keys = k_ref[j * SPAN : (j + 1) * SPAN, hc]
            a2[j, h, 0:HD, 0:HD] = keys
            a2[j, h, 0:HD, HD : 2 * HD] = keys
            keyf = keys.astype(F32)
            norm = lax.rsqrt(jnp.sum(keyf * keyf, axis=1, keepdims=True) + 1e-06)
            norms[j, h] = norm
            keyt = keyf.T.astype(BF16)
            kt2[j, h, :, 0:HD] = keyt
            kt2[j, h, :, HD : 2 * HD] = keyt
            fade = jnp.exp(closings[j][:, h : h + 1] - ccols[j][:, h : h + 1])
            gram = dot(kt2[j, h], stacked(keyf * (fade * norm * norm)))
            lb[j, h] = run
            run = jnp.exp(closings[j][:, h : h + 1]) * run + gram
        st_h[1 + h] = jnp.where(keep, run[0 : HD // 2], run[HD // 2 :])
        edge = jnp.sum(jnp.where(near == HD // 2, run, 0.0), axis=0, keepdims=True)
        marks = jnp.where(group == h, jnp.broadcast_to(total[:, h : h + 1], marks.shape), marks)
        marks = jnp.where(group == HL + h, edge, marks)
    st_h[0] = marks

    pl.semaphore_wait(barrier, nz + ny + 1)

    def z_copy(src, dst, slot, step):
        to = y * nz + lax.rem(z + step, nz)
        return pltpu.make_async_remote_copy(
            src_ref=src, dst_ref=dst, send_sem=z_send.at[slot, step], recv_sem=z_recv.at[slot, step],
            device_id=(to, wide), device_id_type=MESH,
        )

    def scatter(st, buf, slot, rows, part):
        copies = []
        for step in range(1, nz):
            peer = lax.rem(z + step, nz)
            start = pl.multiple_of(peer * rows, rows)
            copies.append(z_copy(st.at[part, pl.ds(start, rows), :], buf.at[z, part], slot, step))
            copies[-1].start()
        mine = pl.multiple_of(z * rows, rows)
        buf[z, part] = st[part, pl.ds(mine, rows), :]
        return copies

    sends = scatter(st_h, buf_h, 0, rows_h, slice(0, HL + 1))
    sent = list(sends)
    g_sends = []
    loads[2].wait()

    for h in range(HL):
        hc = slice(h * HD, (h + 1) * HD)
        run = jnp.zeros((HD, HD), F32)
        for j in range(NJ):
            keyf = k_ref[j * SPAN : (j + 1) * SPAN, hc].astype(F32)
            valt = v_ref[j * SPAN : (j + 1) * SPAN, hc].astype(F32).T.astype(BF16)
            vt2[j, h, :, 0:HD] = valt
            vt2[j, h, :, HD : 2 * HD] = valt
            fade = jnp.exp(closings[j][:, h : h + 1] - ccols[j][:, h : h + 1])
            memory = dot(vt2[j, h], stacked(keyf * (fade * norms[j, h])))
            lb[j, HL + h] = run
            run = jnp.exp(closings[j][:, h : h + 1]) * run + memory
        st_g[h] = run
        if h % PAIR == PAIR - 1:
            g_sends.append(scatter(st_g, buf_g, 1 + h, rows_g, slice(h + 1 - PAIR, h + 1)))
            sent += g_sends[-1]

    def y_copies(buf, slot, part):
        copies = []
        for step in range(1, ny):
            to = lax.rem(y + step, ny) * nz + z
            copies.append(
                pltpu.make_async_remote_copy(
                    src_ref=buf.at[y, part], dst_ref=buf.at[y, part],
                    send_sem=y_send.at[slot, step], recv_sem=y_recv.at[slot, step],
                    device_id=(to, wide), device_id_type=MESH,
                )
            )
            copies[-1].start()
        return copies

    def give_back(buf, pre, slot, rows, part):
        mine = pl.multiple_of(z * rows, rows)
        copies = []
        for step in range(1, nz):
            peer = lax.rem(z + step, nz)
            copies.append(
                z_copy(buf.at[peer, part], pre.at[part, pl.ds(mine, rows), :], slot, step)
            )
            copies[-1].start()
        pre[part, pl.ds(mine, rows), :] = buf[z, part]
        return copies

    def total_h(copies):
        for copy in copies:
            copy.wait_recv()
        sums = [jnp.zeros((rows_h, HD), F32) for _ in range(HL)]
        edges = [jnp.zeros((1, HD), F32) for _ in range(HL)]
        decay = jnp.zeros((8, HD), F32)
        for other in range(nz):
            marks = buf_h[other, 0, 0:8, :]
            factor = jnp.exp(marks[0:HL])
            decay = decay + marks
            for h in range(HL):
                sums[h] = factor[h : h + 1] * sums[h] + buf_h[other, 1 + h]
                edges[h] = factor[h : h + 1] * edges[h] + marks[HL + h : HL + h + 1]
        tot_h[y, 0, 0:8, :] = decay
        for h in range(HL):
            tot_h[y, 1 + h] = sums[h]
            tot_h[y, 0, HL + h : HL + h + 1, :] = edges[h]
        return y_copies(tot_h, 0, slice(0, HL + 1))

    def prefix_h(copies):
        for copy in copies:
            copy.wait_recv()
        runs = [jnp.zeros((rows_h, HD), F32) for _ in range(HL)]
        edges = [jnp.zeros((1, HD), F32) for _ in range(HL)]
        for other in range(ny):
            marks = tot_h[other, 0, 0:8, :]
            factor = jnp.exp(marks[0:HL])
            for h in range(HL):
                runs[h] = jnp.where(other < y, factor[h : h + 1] * runs[h] + tot_h[other, 1 + h], runs[h])
                edges[h] = jnp.where(
                    other < y, factor[h : h + 1] * edges[h] + marks[HL + h : HL + h + 1], edges[h]
                )
        mine = list(edges)
        for other in range(nz):
            marks = buf_h[other, 0, 0:8, :]
            factor = jnp.exp(marks[0:HL])
            for h in range(HL):
                out_h[other, h] = runs[h]
                mine[h] = jnp.where(other == z, edges[h], mine[h])
                runs[h] = factor[h : h + 1] * runs[h] + buf_h[other, 1 + h]
                edges[h] = factor[h : h + 1] * edges[h] + marks[HL + h : HL + h + 1]
        return give_back(out_h, pre_h, 1 + HL, rows_h, slice(0, HL)), mine

    def total_g(first, copies):
        for copy in copies:
            copy.wait_recv()
        for h in range(first, first + PAIR):
            run = jnp.zeros((rows_g, HD), F32)
            for other in range(nz):
                run = jnp.exp(buf_h[other, 0, h : h + 1, :]) * run + buf_g[other, h]
            tot_g[y, h] = run
        return y_copies(tot_g, 1 + first, slice(first, first + PAIR))

    def prefix_g(first, copies):
        for copy in copies:
            copy.wait_recv()
        for h in range(first, first + PAIR):
            run = jnp.zeros((rows_g, HD), F32)
            for other in range(ny):
                factor = jnp.exp(tot_h[other, 0, h : h + 1, :])
                run = jnp.where(other < y, factor * run + tot_g[other, h], run)
            for other in range(nz):
                out_g[other, h] = run
                run = jnp.exp(buf_h[other, 0, h : h + 1, :]) * run + buf_g[other, h]
        return give_back(out_g, pre, 2 + HL + first, rows_g, slice(first, first + PAIR))

    loads[3].wait()
    loads[4].wait()
    loads[5].start()
    for h in range(HL):
        hc = slice(h * HD, (h + 1) * HD)
        ridge_m[h] = jnp.broadcast_to(ridge_ref[:, hc], (HD, HD)).T
        g_in[h, HD : 2 * HD, HD : 2 * HD] = jnp.zeros((HD, HD), BF16)
        for i in range(2):
            a1[i * HL + h, 2 * HD : 3 * HD, HD : 2 * HD] = jnp.zeros((HD, HD), BF16)

    def weights_of(j):
        for h in range(HL):
            hc = slice(h * HD, (h + 1) * HD)
            lag = crow[j, h : h + 1, :] - ccols[j][:, h : h + 1]
            causal = place_r <= place_c
            weight = jnp.where(causal, jnp.exp(jnp.where(causal, lag, 0.0)), 0.0) * norms[j, h]
            high, low = parts(lb[j, HL + h])
            a2[j, h, HD : 2 * HD, 0:HD] = high
            a2[j, h, HD : 2 * HD, HD : 2 * HD] = high
            a2[j, h, 2 * HD : 3 * HD, 0:HD] = low
            a2[j, h, 2 * HD : 3 * HD, HD : 2 * HD] = jnp.zeros((HD, HD), BF16)
            w1[j, h] = weight
            w2[j, h] = weight * norms[j, h]
            query = q_ref[j * SPAN : (j + 1) * SPAN, hc].astype(F32).T
            qt[j, h] = query * lax.rsqrt(jnp.sum(query * query, axis=0, keepdims=True) + 1e-06)

    weights_of(0)
    weights_of(1)
    y_sends = total_h(sends)
    sent += y_sends
    weights_of(2)
    back, edges = prefix_h(y_sends)
    sent += back
    weights_of(3)
    firsts = range(0, HL, PAIR)
    gy_sends = [total_g(first, copies) for first, copies in zip(firsts, g_sends)]
    g_back = [prefix_g(first, copies) for first, copies in zip(firsts, gy_sends)]
    for copies in gy_sends + g_back:
        sent += copies
    for copy in back:
        copy.wait_recv()
    for h in range(HL):
        packed = pre_h[h]
        spread = jnp.concatenate([jnp.where(keep, packed, 0.0), jnp.where(keep, 0.0, packed)], axis=0)
        both = jnp.where(near == 0, spread, spread + spread.T)
        gram_in[h] = jnp.where(near == HD // 2, edges[h], both)

    def system(slot, j, h, state):
        high, low = parts(state)
        a1[slot, 0:HD, :] = a2[j, h, 0:HD, :]
        a1[slot, HD : 2 * HD, 0:HD] = high
        a1[slot, HD : 2 * HD, HD : 2 * HD] = high
        a1[slot, 2 * HD : 3 * HD, 0:HD] = low
        b1[slot, :, 0:HD] = high
        b1[slot, :, HD : 2 * HD] = kt2[j, h, :, 0:SPAN]

    def blocks_of(spans):
        return [(i * HL + h, j, h) for i, j in enumerate(spans) for h in range(HL)]

    def solve(spans):
        blocks = blocks_of(spans)
        norm0, opening = [], []
        for slot, j, h in blocks:
            system(slot, j, h, sdec[j, h : h + 1, :] * gram_in[h] + lb[j, h])
            query = qt[j, h]
            xs[slot] = jnp.zeros((HD, SPAN), F32)
            rs[slot] = query
            ps[slot] = query
            norm0.append(jnp.sum(query * query, axis=0, keepdims=True))
            opening.append(jnp.exp(crow[j, h : h + 1, :]))

        def advance(i, slot, norm, image):
            direction = ps[slot]
            alpha = norm / jnp.sum(direction * image, axis=0, keepdims=True)
            xs[slot] = xs[slot] + alpha * direction
            residual = rs[slot] - alpha * image
            fresh = jnp.sum(residual * residual, axis=0, keepdims=True)
            rs[slot] = residual
            ps[slot] = residual + (fresh / norm) * direction
            return fresh

        def sweep(_, norm):
            n = len(blocks)
            outs, locals_, after = [None] * n, [None] * n, [None] * n
            for i, (slot, j, h) in enumerate(blocks):
                outs[i] = dot(a1[slot], stacked(ps[slot]))
            for i, (slot, j, h) in enumerate(blocks):
                locals_[i] = dot(kt2[j, h], stacked(outs[i][0:HD] * w2[j, h]))
            for i, (slot, j, h) in enumerate(blocks):
                carried = outs[i][HD : 2 * HD] + outs[i][2 * HD : 3 * HD]
                image = opening[i] * carried + locals_[i] + ridge_m[h] * ps[slot]
                after[i] = advance(i, slot, norm[i], image)
            return tuple(after)

        def last_sweep(_, norm):
            n = len(blocks)
            outs, images, after = [None] * n, [None] * n, [None] * n
            for i, (slot, j, h) in enumerate(blocks):
                outs[i] = dot(a1[slot, 0:HD, 0:HD], ps[slot].astype(BF16))
            for i, (slot, j, h) in enumerate(blocks):
                lifted = (opening[i] * ps[slot]).astype(BF16)
                scores = (outs[i] * w2[j, h]).astype(BF16)
                images[i] = dot(b1[slot], jnp.concatenate([lifted, scores], axis=0))
            for i, (slot, j, h) in enumerate(blocks):
                image = images[i] + ridge_m[h] * ps[slot]
                after[i] = advance(i, slot, norm[i], image)
            return tuple(after)

        norm = lax.fori_loop(0, FULL, sweep, tuple(norm0), unroll=UNROLL)
        lax.fori_loop(FULL, ITERS, last_sweep, norm, unroll=2)
        return opening

    def read_local(i, j, opening):
        outs = [dot(a2[j, h], stacked(xs[i * HL + h])) for h in range(HL)]
        for h in range(HL):
            near_part = dot(vt2[j, h], stacked(outs[h][0:HD] * w1[j, h]))
            rs[i * HL + h] = near_part + opening[i * HL + h] * (outs[h][HD : 2 * HD] + outs[h][2 * HD :])

    def take_memory(h):
        high, low = parts(pre[h])
        g_in[h, 0:HD, 0:HD] = high
        g_in[h, 0:HD, HD : 2 * HD] = high
        g_in[h, HD : 2 * HD, 0:HD] = low

    def read_out(k, i, j, opening, heads):
        outs = [dot(g_in[h], stacked(xs[i * HL + h])) for h in heads]
        for h, out in zip(heads, outs):
            lifted = opening[i * HL + h] * sdec[j, h : h + 1, :]
            read = rs[i * HL + h] + lifted * (out[0:HD] + out[HD : 2 * HD])
            read = read * lax.rsqrt(jnp.sum(read * read, axis=0, keepdims=True) * (1.0 / HD) + 1e-06)
            nm[k, :, h * HD : (h + 1) * HD] = read.T.astype(BF16)

    half = SPAN // 2
    width = w_vm.shape[1] // NCH

    def p_copy(k, n):
        return pltpu.make_async_remote_copy(
            src_ref=pout.at[k, n], dst_ref=pin.at[k, n], send_sem=p_send.at[k, n], recv_sem=p_recv.at[k, n],
            device_id=(seq, partner), device_id_type=MESH,
        )

    def project(items, use):
        mine = pl.multiple_of(c * half, half)
        other = pl.multiple_of((1 - c) * half, half)
        lhs = {
            k: jnp.concatenate([nm[k, pl.ds(mine, half), :], nm[k, pl.ds(other, half), :]], axis=0)
            for k in dict(items)
        }
        copies = {}
        for i in range(len(items) + LAG):
            if i < len(items):
                k, n = items[i]
                out = dot(lhs[k], w_vm[:, n * width : (n + 1) * width])
                pown[k, n] = out[0:half]
                pout[k, n] = out[half:]
                copies[k, n] = p_copy(k, n)
                copies[k, n].start()
            if i >= LAG:
                use(*items[i - LAG], copies)
        return copies

    def join(k, n, copies):
        copies[k, n].wait_recv()
        pown[k, n] = pown[k, n] + pin[k, n]

    def x_copy(src, dst, send, recv, to):
        copy = pltpu.make_async_remote_copy(
            src_ref=src, dst_ref=dst, send_sem=send, recv_sem=recv,
            device_id=(seq, to), device_id_type=MESH,
        )
        copy.start()
        return copy

    middle = NCH // 2
    js = [lax.rem(x + o, nx) for o in ORDER]

    mixed_order = [(i % 2) * middle + i // 2 for i in range(NCH)]
    relay, final1, final2 = {}, {}, {}

    opening = solve(js[0:1])
    read_local(0, js[0], opening)
    loads[5].wait()
    for first, copies in zip(firsts, g_back):
        for copy in copies:
            copy.wait_recv()
        for h in range(first, first + PAIR):
            take_memory(h)
        read_out(0, 0, js[0], opening, tuple(range(first, first + PAIR)))

    def send_relay(k, n, copies):
        join(k, n, copies)
        if n < middle:
            relay[n] = x_copy(pown.at[0, n], ra.at[n], r_send.at[n], r_recv.at[n], right)
        else:
            relay[n] = x_copy(pown.at[0, n], rb.at[n - middle], r_send.at[n], r_recv.at[n], left)

    copies = project([(0, n) for n in mixed_order], send_relay)
    sent += list(copies.values()) + list(relay.values())

    def send_first(k, n, copies):
        if k == 1 and n >= middle:
            join(k, n, copies)
            final1[n] = x_copy(pown.at[1, n], f1.at[n], f_send.at[0, n], f_recv.at[0, n], right)
        if k == 2 and n < middle:
            join(k, n, copies)
            final2[n] = x_copy(pown.at[2, n], f2.at[n], f_send.at[1, n], f_recv.at[1, n], left)

    opening = solve(js[1:3])
    every = tuple(range(HL))
    for i in range(2):
        read_local(i, js[1 + i], opening)
        read_out(1 + i, i, js[1 + i], opening, every)
    pairs = [(k, (n + middle * (k % 2)) % NCH) for n in range(NCH) for k in (1, 2)]
    copies = project(pairs, send_first)
    sent += list(copies.values())
    for n in range(middle):
        relay[n].wait_recv()
        join(1, n, copies)
        pown[1, n] = pown[1, n] + ra[n]
        final1[n] = x_copy(pown.at[1, n], f1.at[n], f_send.at[0, n], f_recv.at[0, n], right)
        m = n + middle
        relay[m].wait_recv()
        join(2, m, copies)
        pown[2, m] = pown[2, m] + rb[n]
        final2[m] = x_copy(pown.at[2, m], f2.at[m], f_send.at[1, m], f_recv.at[1, m], left)

    opening = solve(js[3:4])
    read_local(0, js[3], opening)
    read_out(3, 0, js[3], opening, every)
    sent += list(project([(3, n) for n in range(NCH)], join).values())
    for copy in sent:
        copy.wait_send()
    for i in range(NCH):
        n = (i % 2) * middle + i // 2
        m = (n + middle) % NCH
        final1[m].wait_recv()
        final2[n].wait_recv()
        if i % 2 == 1:
            for e in (n, m):
                o_ref[:, e * width : (e + 1) * width] = (pown[3, e] + f1[e] + f2[e]).astype(BF16)
    for copy in list(final1.values()) + list(final2.values()):
        copy.wait_send()


def solution(mesh, ny=4, nz=8):
    nx = mesh.shape["wide"] // 2

    def body(queries, keys, values, log_decay, ridge, out_weight):
        columns = out_weight.shape[1]
        width = columns // NCH
        half = SPAN // 2
        rows_h, rows_g = HD // 2 // nz, HD // nz
        tokens, inner = queries.shape
        vm = pltpu.VMEM
        dma = pltpu.SemaphoreType.DMA
        scratch = [
            vm((tokens, inner), BF16),
            vm((tokens, inner), BF16),
            vm((tokens, inner), BF16),
            vm((HL, tokens), F32),
            vm((1, inner), F32),
            vm(out_weight.shape, BF16),
            vm((HL + 1, HD // 2, HD), F32),
            vm((HL, HD, HD), F32),
            vm((nz, HL + 1, rows_h, HD), F32),
            vm((nz, HL, rows_g, HD), F32),
            vm((ny, HL + 1, rows_h, HD), F32),
            vm((ny, HL, rows_g, HD), F32),
            vm((nz, HL, rows_h, HD), F32),
            vm((nz, HL, rows_g, HD), F32),
            vm((HL, HD // 2, HD), F32),
            vm((HL, HD, HD), F32),
            vm((NJ, 2 * HL, HD, HD), F32),
            vm((NJ, 8, HD), F32),
            vm((NJ, 8, HD), F32),
            vm((NJ, HL, SPAN, SPAN), F32),
            vm((NJ, HL, SPAN, SPAN), F32),
            vm((NJ, HL, HD, 2 * SPAN), BF16),
            vm((NJ, HL, HD, 2 * SPAN), BF16),
            vm((NJ, HL, HD, SPAN), F32),
            vm((HL, HD, SPAN), F32),
            vm((HL, HD, HD), F32),
            vm((HL, 2 * HD, 2 * HD), BF16),
            vm((2 * HL, 3 * HD, 2 * HD), BF16),
            vm((2 * HL, HD, 2 * HD), BF16),
            vm((NJ, HL, 3 * HD, 2 * HD), BF16),
            vm((2 * HL, HD, SPAN), F32),
            vm((2 * HL, HD, SPAN), F32),
            vm((2 * HL, HD, SPAN), F32),
            vm((NJ, SPAN, HL * HD), BF16),
            vm((NJ, NCH, half, width), F32),
            vm((NJ, NCH, half, width), F32),
            vm((NJ, NCH, half, width), F32),
            vm((NCH // 2, half, width), F32),
            vm((NCH // 2, half, width), F32),
            vm((NCH, half, width), F32),
            vm((NCH, half, width), F32),
            dma((6,)),
            dma((2 * HL + 2, nz)),
            dma((2 * HL + 2, nz)),
            dma((HL + 1, ny)),
            dma((HL + 1, ny)),
            dma((NJ, NCH)),
            dma((NJ, NCH)),
            dma((NCH,)),
            dma((NCH,)),
            dma((2, NCH)),
            dma((2, NCH)),
        ]
        space = pl.BlockSpec(memory_space=pltpu.VMEM)
        return pl.pallas_call(
            functools.partial(kernel, ny, nz, nx),
            out_shape=jax.ShapeDtypeStruct((queries.shape[0] // (2 * nx), columns), BF16),
            in_specs=[pl.BlockSpec(memory_space=pl.ANY)] * 6,
            out_specs=space,
            scratch_shapes=scratch,
            compiler_params=pltpu.CompilerParams(
                collective_id=0, has_side_effects=True, vmem_limit_bytes=50000 << 10
            ),
        )(*(pltpu.with_memory_space_constraint(a, pltpu.HBM) for a in (queries, keys, values, log_decay.T, ridge[None, :], out_weight)))

    placed = (
        P("seq", "wide"),
        P("seq", "wide"),
        P("seq", "wide"),
        P("seq", "wide"),
        P("wide"),
        P("wide", None),
    )
    return jax.shard_map(
        body, mesh=mesh, in_specs=placed, out_specs=P(("seq", "wide"), None), check_vma=False
    )
```

```python
import functools

import jax
import jax.numpy as jnp
from jax import lax
from jax.experimental import pallas as pl
from jax.experimental.pallas import tpu as pltpu
from jax.sharding import PartitionSpec as P

MESH = pl.DeviceIdType.MESH
F32 = jnp.float32
BF16 = jnp.bfloat16
HD = 128
SPAN = 128
ITERS = 8
UNROLL = 3
FULL = 6
LAG = 4
PAIR = 4
HL = 4
NJ = 4
NCH = 8
ORDER = (2, 1, 3, 0)
highest = lax.Precision.HIGHEST


def parts(value):
    high = value.astype(BF16)
    return high, (value - high.astype(F32)).astype(BF16)


def stacked(value):
    return jnp.concatenate(parts(value), axis=0)


def dot(a, b):
    return jnp.dot(a, b, preferred_element_type=F32)


def kernel(
    ny, nz, nx,
    q_hbm, k_hbm, v_hbm, ld_hbm, ridge_hbm, w_hbm, o_ref,
    q_ref, k_ref, v_ref, ld_ref, ridge_ref, w_vm,
    st_h, st_g, buf_h, buf_g, tot_h, tot_g, out_h, out_g, pre_h, pre, lb, sdec, crow, w1, w2, kt2, vt2, qt, ridge_m,
    gram_in, g_in, a1, b1, a2, xs, rs, ps, nm, pown, pout, pin, ra, rb, f1, f2,
    load_sem, z_send, z_recv, y_send, y_recv, p_send, p_recv, r_send, r_recv, f_send, f_recv,
):
    seq = lax.axis_index("seq")
    wide = lax.axis_index("wide")
    y, z = lax.div(seq, nz), lax.rem(seq, nz)
    x, c = lax.div(wide, 2), lax.rem(wide, 2)
    rows_h, rows_g = HD // 2 // nz, HD // nz
    partner = x * 2 + (1 - c)
    right = lax.rem(x + 1, nx) * 2 + c
    left = lax.rem(x + nx - 1, nx) * 2 + c

    loads = [
        pltpu.make_async_copy(src, dst, load_sem.at[i])
        for i, (src, dst) in enumerate(
            (
                (ld_hbm, ld_ref), (k_hbm, k_ref), (v_hbm, v_ref),
                (q_hbm, q_ref), (ridge_hbm, ridge_ref), (w_hbm, w_vm),
            )
        )
    ]
    for load in loads[:5]:
        load.start()

    barrier = pltpu.get_barrier_semaphore()
    for step in range(1, nz):
        to = y * nz + lax.rem(z + step, nz)
        pl.semaphore_signal(barrier, inc=1, device_id=(to, wide), device_id_type=MESH)
    for step in range(1, ny):
        to = lax.rem(y + step, ny) * nz + z
        pl.semaphore_signal(barrier, inc=1, device_id=(to, wide), device_id_type=MESH)
    for to in (partner, right, left):
        pl.semaphore_signal(barrier, inc=1, device_id=(seq, to), device_id_type=MESH)

    place_r = lax.broadcasted_iota(jnp.int32, (SPAN, SPAN), 0)
    place_c = lax.broadcasted_iota(jnp.int32, (SPAN, SPAN), 1)
    lower = (place_r >= place_c).astype(F32)
    upper = (place_r <= place_c).astype(F32)
    ccols, norms = [], {}
    loads[0].wait()
    total = jnp.zeros((1, HL), F32)
    closings = []
    for j in range(NJ):
        decay = ld_ref[:, j * SPAN : (j + 1) * SPAN]
        ccol = lax.dot_general(
            lower, decay, (((1,), (1,)), ((), ())), precision=highest, preferred_element_type=F32
        )
        ccols.append(ccol)
        crow[j, 0:HL, :] = jnp.dot(decay, upper, precision=highest, preferred_element_type=F32)
        for h in range(HL):
            sdec[j, h : h + 1, :] = jnp.exp(jnp.broadcast_to(total[:, h : h + 1], (1, HD)))
        closing = ccol[SPAN - 1 : SPAN, :]
        closings.append(closing)
        total = total + closing
    group = lax.rem(lax.broadcasted_iota(jnp.int32, (HD // 2, HD), 0), rows_h)
    near = lax.rem(place_c - place_r + HD, HD)
    keep = near[0 : HD // 2] < HD // 2
    marks = jnp.zeros((HD // 2, HD), F32)
    loads[1].wait()

    for h in range(HL):
        hc = slice(h * HD, (h + 1) * HD)
        run = jnp.zeros((HD, HD), F32)
        for j in range(NJ):
            keys = k_ref[j * SPAN : (j + 1) * SPAN, hc]
            a2[j, h, 0:HD, 0:HD] = keys
            a2[j, h, 0:HD, HD : 2 * HD] = keys
            keyf = keys.astype(F32)
            norm = lax.rsqrt(jnp.sum(keyf * keyf, axis=1, keepdims=True) + 1e-06)
            norms[j, h] = norm
            keyt = keyf.T.astype(BF16)
            kt2[j, h, :, 0:HD] = keyt
            kt2[j, h, :, HD : 2 * HD] = keyt
            fade = jnp.exp(closings[j][:, h : h + 1] - ccols[j][:, h : h + 1])
            gram = dot(kt2[j, h], stacked(keyf * (fade * norm * norm)))
            lb[j, h] = run
            run = jnp.exp(closings[j][:, h : h + 1]) * run + gram
        st_h[1 + h] = jnp.where(keep, run[0 : HD // 2], run[HD // 2 :])
        edge = jnp.sum(jnp.where(near == HD // 2, run, 0.0), axis=0, keepdims=True)
        marks = jnp.where(group == h, jnp.broadcast_to(total[:, h : h + 1], marks.shape), marks)
        marks = jnp.where(group == HL + h, edge, marks)
    st_h[0] = marks

    pl.semaphore_wait(barrier, nz + ny + 1)

    def z_copy(src, dst, slot, step):
        to = y * nz + lax.rem(z + step, nz)
        return pltpu.make_async_remote_copy(
            src_ref=src, dst_ref=dst, send_sem=z_send.at[slot, step], recv_sem=z_recv.at[slot, step],
            device_id=(to, wide), device_id_type=MESH,
        )

    def scatter(st, buf, slot, rows, part):
        copies = []
        for step in range(1, nz):
            peer = lax.rem(z + step, nz)
            start = pl.multiple_of(peer * rows, rows)
            copies.append(z_copy(st.at[part, pl.ds(start, rows), :], buf.at[z, part], slot, step))
            copies[-1].start()
        mine = pl.multiple_of(z * rows, rows)
        buf[z, part] = st[part, pl.ds(mine, rows), :]
        return copies

    sends = scatter(st_h, buf_h, 0, rows_h, slice(0, HL + 1))
    sent = list(sends)
    g_sends = []
    loads[2].wait()

    for h in range(HL):
        hc = slice(h * HD, (h + 1) * HD)
        run = jnp.zeros((HD, HD), F32)
        for j in range(NJ):
            keyf = k_ref[j * SPAN : (j + 1) * SPAN, hc].astype(F32)
            valt = v_ref[j * SPAN : (j + 1) * SPAN, hc].astype(F32).T.astype(BF16)
            vt2[j, h, :, 0:HD] = valt
            vt2[j, h, :, HD : 2 * HD] = valt
            fade = jnp.exp(closings[j][:, h : h + 1] - ccols[j][:, h : h + 1])
            memory = dot(vt2[j, h], stacked(keyf * (fade * norms[j, h])))
            lb[j, HL + h] = run
            run = jnp.exp(closings[j][:, h : h + 1]) * run + memory
        st_g[h] = run
        if h % PAIR == PAIR - 1:
            g_sends.append(scatter(st_g, buf_g, 1 + h, rows_g, slice(h + 1 - PAIR, h + 1)))
            sent += g_sends[-1]

    def y_copies(buf, slot, part):
        copies = []
        for step in range(1, ny):
            to = lax.rem(y + step, ny) * nz + z
            copies.append(
                pltpu.make_async_remote_copy(
                    src_ref=buf.at[y, part], dst_ref=buf.at[y, part],
                    send_sem=y_send.at[slot, step], recv_sem=y_recv.at[slot, step],
                    device_id=(to, wide), device_id_type=MESH,
                )
            )
            copies[-1].start()
        return copies

    def give_back(buf, pre, slot, rows, part):
        mine = pl.multiple_of(z * rows, rows)
        copies = []
        for step in range(1, nz):
            peer = lax.rem(z + step, nz)
            copies.append(
                z_copy(buf.at[peer, part], pre.at[part, pl.ds(mine, rows), :], slot, step)
            )
            copies[-1].start()
        pre[part, pl.ds(mine, rows), :] = buf[z, part]
        return copies

    def total_h(copies):
        for copy in copies:
            copy.wait_recv()
        sums = [jnp.zeros((rows_h, HD), F32) for _ in range(HL)]
        edges = [jnp.zeros((1, HD), F32) for _ in range(HL)]
        decay = jnp.zeros((8, HD), F32)
        for other in range(nz):
            marks = buf_h[other, 0, 0:8, :]
            factor = jnp.exp(marks[0:HL])
            decay = decay + marks
            for h in range(HL):
                sums[h] = factor[h : h + 1] * sums[h] + buf_h[other, 1 + h]
                edges[h] = factor[h : h + 1] * edges[h] + marks[HL + h : HL + h + 1]
        tot_h[y, 0, 0:8, :] = decay
        for h in range(HL):
            tot_h[y, 1 + h] = sums[h]
            tot_h[y, 0, HL + h : HL + h + 1, :] = edges[h]
        return y_copies(tot_h, 0, slice(0, HL + 1))

    def prefix_h(copies):
        for copy in copies:
            copy.wait_recv()
        runs = [jnp.zeros((rows_h, HD), F32) for _ in range(HL)]
        edges = [jnp.zeros((1, HD), F32) for _ in range(HL)]
        for other in range(ny):
            marks = tot_h[other, 0, 0:8, :]
            factor = jnp.exp(marks[0:HL])
            for h in range(HL):
                runs[h] = jnp.where(other < y, factor[h : h + 1] * runs[h] + tot_h[other, 1 + h], runs[h])
                edges[h] = jnp.where(
                    other < y, factor[h : h + 1] * edges[h] + marks[HL + h : HL + h + 1], edges[h]
                )
        mine = list(edges)
        for other in range(nz):
            marks = buf_h[other, 0, 0:8, :]
            factor = jnp.exp(marks[0:HL])
            for h in range(HL):
                out_h[other, h] = runs[h]
                mine[h] = jnp.where(other == z, edges[h], mine[h])
                runs[h] = factor[h : h + 1] * runs[h] + buf_h[other, 1 + h]
                edges[h] = factor[h : h + 1] * edges[h] + marks[HL + h : HL + h + 1]
        return give_back(out_h, pre_h, 1 + HL, rows_h, slice(0, HL)), mine

    def total_g(first, copies):
        for copy in copies:
            copy.wait_recv()
        for h in range(first, first + PAIR):
            run = jnp.zeros((rows_g, HD), F32)
            for other in range(nz):
                run = jnp.exp(buf_h[other, 0, h : h + 1, :]) * run + buf_g[other, h]
            tot_g[y, h] = run
        return y_copies(tot_g, 1 + first, slice(first, first + PAIR))

    def prefix_g(first, copies):
        for copy in copies:
            copy.wait_recv()
        for h in range(first, first + PAIR):
            run = jnp.zeros((rows_g, HD), F32)
            for other in range(ny):
                factor = jnp.exp(tot_h[other, 0, h : h + 1, :])
                run = jnp.where(other < y, factor * run + tot_g[other, h], run)
            for other in range(nz):
                out_g[other, h] = run
                run = jnp.exp(buf_h[other, 0, h : h + 1, :]) * run + buf_g[other, h]
        return give_back(out_g, pre, 2 + HL + first, rows_g, slice(first, first + PAIR))

    loads[3].wait()
    loads[4].wait()
    loads[5].start()
    for h in range(HL):
        hc = slice(h * HD, (h + 1) * HD)
        ridge_m[h] = jnp.broadcast_to(ridge_ref[:, hc], (HD, HD)).T
        g_in[h, HD : 2 * HD, HD : 2 * HD] = jnp.zeros((HD, HD), BF16)
        for i in range(2):
            a1[i * HL + h, 2 * HD : 3 * HD, HD : 2 * HD] = jnp.zeros((HD, HD), BF16)

    def weights_of(j):
        for h in range(HL):
            hc = slice(h * HD, (h + 1) * HD)
            lag = crow[j, h : h + 1, :] - ccols[j][:, h : h + 1]
            causal = place_r <= place_c
            weight = jnp.where(causal, jnp.exp(jnp.where(causal, lag, 0.0)), 0.0) * norms[j, h]
            high, low = parts(lb[j, HL + h])
            a2[j, h, HD : 2 * HD, 0:HD] = high
            a2[j, h, HD : 2 * HD, HD : 2 * HD] = high
            a2[j, h, 2 * HD : 3 * HD, 0:HD] = low
            a2[j, h, 2 * HD : 3 * HD, HD : 2 * HD] = jnp.zeros((HD, HD), BF16)
            w1[j, h] = weight
            w2[j, h] = weight * norms[j, h]
            query = q_ref[j * SPAN : (j + 1) * SPAN, hc].astype(F32).T
            qt[j, h] = query * lax.rsqrt(jnp.sum(query * query, axis=0, keepdims=True) + 1e-06)

    weights_of(0)
    weights_of(1)
    y_sends = total_h(sends)
    sent += y_sends
    weights_of(2)
    back, edges = prefix_h(y_sends)
    sent += back
    weights_of(3)
    firsts = range(0, HL, PAIR)
    gy_sends = [total_g(first, copies) for first, copies in zip(firsts, g_sends)]
    g_back = [prefix_g(first, copies) for first, copies in zip(firsts, gy_sends)]
    for copies in gy_sends + g_back:
        sent += copies
    for copy in back:
        copy.wait_recv()
    for h in range(HL):
        packed = pre_h[h]
        spread = jnp.concatenate([jnp.where(keep, packed, 0.0), jnp.where(keep, 0.0, packed)], axis=0)
        both = jnp.where(near == 0, spread, spread + spread.T)
        gram_in[h] = jnp.where(near == HD // 2, edges[h], both)

    def system(slot, j, h, state):
        high, low = parts(state)
        a1[slot, 0:HD, :] = a2[j, h, 0:HD, :]
        a1[slot, HD : 2 * HD, 0:HD] = high
        a1[slot, HD : 2 * HD, HD : 2 * HD] = high
        a1[slot, 2 * HD : 3 * HD, 0:HD] = low
        b1[slot, :, 0:HD] = high
        b1[slot, :, HD : 2 * HD] = kt2[j, h, :, 0:SPAN]

    def blocks_of(spans):
        return [(i * HL + h, j, h) for i, j in enumerate(spans) for h in range(HL)]

    def solve(spans):
        blocks = blocks_of(spans)
        norm0, opening = [], []
        for slot, j, h in blocks:
            system(slot, j, h, sdec[j, h : h + 1, :] * gram_in[h] + lb[j, h])
            query = qt[j, h]
            xs[slot] = jnp.zeros((HD, SPAN), F32)
            rs[slot] = query
            ps[slot] = query
            norm0.append(jnp.sum(query * query, axis=0, keepdims=True))
            opening.append(jnp.exp(crow[j, h : h + 1, :]))

        def advance(i, slot, norm, image):
            direction = ps[slot]
            alpha = norm / jnp.sum(direction * image, axis=0, keepdims=True)
            xs[slot] = xs[slot] + alpha * direction
            residual = rs[slot] - alpha * image
            fresh = jnp.sum(residual * residual, axis=0, keepdims=True)
            rs[slot] = residual
            ps[slot] = residual + (fresh / norm) * direction
            return fresh

        def sweep(_, norm):
            n = len(blocks)
            outs, locals_, after = [None] * n, [None] * n, [None] * n
            for i, (slot, j, h) in enumerate(blocks):
                outs[i] = dot(a1[slot], stacked(ps[slot]))
            for i, (slot, j, h) in enumerate(blocks):
                locals_[i] = dot(kt2[j, h], stacked(outs[i][0:HD] * w2[j, h]))
            for i, (slot, j, h) in enumerate(blocks):
                carried = outs[i][HD : 2 * HD] + outs[i][2 * HD : 3 * HD]
                image = opening[i] * carried + locals_[i] + ridge_m[h] * ps[slot]
                after[i] = advance(i, slot, norm[i], image)
            return tuple(after)

        def last_sweep(_, norm):
            n = len(blocks)
            outs, images, after = [None] * n, [None] * n, [None] * n
            for i, (slot, j, h) in enumerate(blocks):
                outs[i] = dot(a1[slot, 0:HD, 0:HD], ps[slot].astype(BF16))
            for i, (slot, j, h) in enumerate(blocks):
                lifted = (opening[i] * ps[slot]).astype(BF16)
                scores = (outs[i] * w2[j, h]).astype(BF16)
                images[i] = dot(b1[slot], jnp.concatenate([lifted, scores], axis=0))
            for i, (slot, j, h) in enumerate(blocks):
                image = images[i] + ridge_m[h] * ps[slot]
                after[i] = advance(i, slot, norm[i], image)
            return tuple(after)

        norm = lax.fori_loop(0, FULL, sweep, tuple(norm0), unroll=UNROLL)
        lax.fori_loop(FULL, ITERS, last_sweep, norm, unroll=2)
        return opening

    def read_local(i, j, opening):
        outs = [dot(a2[j, h], stacked(xs[i * HL + h])) for h in range(HL)]
        for h in range(HL):
            near_part = dot(vt2[j, h], stacked(outs[h][0:HD] * w1[j, h]))
            rs[i * HL + h] = near_part + opening[i * HL + h] * (outs[h][HD : 2 * HD] + outs[h][2 * HD :])

    def take_memory(h):
        high, low = parts(pre[h])
        g_in[h, 0:HD, 0:HD] = high
        g_in[h, 0:HD, HD : 2 * HD] = high
        g_in[h, HD : 2 * HD, 0:HD] = low

    def read_out(k, i, j, opening, heads):
        outs = [dot(g_in[h], stacked(xs[i * HL + h])) for h in heads]
        for h, out in zip(heads, outs):
            lifted = opening[i * HL + h] * sdec[j, h : h + 1, :]
            read = rs[i * HL + h] + lifted * (out[0:HD] + out[HD : 2 * HD])
            read = read * lax.rsqrt(jnp.sum(read * read, axis=0, keepdims=True) * (1.0 / HD) + 1e-06)
            nm[k, :, h * HD : (h + 1) * HD] = read.T.astype(BF16)

    half = SPAN // 2
    width = w_vm.shape[1] // NCH

    def p_copy(k, n):
        return pltpu.make_async_remote_copy(
            src_ref=pout.at[k, n], dst_ref=pin.at[k, n], send_sem=p_send.at[k, n], recv_sem=p_recv.at[k, n],
            device_id=(seq, partner), device_id_type=MESH,
        )

    def project(items, use):
        mine = pl.multiple_of(c * half, half)
        other = pl.multiple_of((1 - c) * half, half)
        lhs = {
            k: jnp.concatenate([nm[k, pl.ds(mine, half), :], nm[k, pl.ds(other, half), :]], axis=0)
            for k in dict(items)
        }
        copies = {}
        for i in range(len(items) + LAG):
            if i < len(items):
                k, n = items[i]
                out = dot(lhs[k], w_vm[:, n * width : (n + 1) * width])
                pown[k, n] = out[0:half]
                pout[k, n] = out[half:]
                copies[k, n] = p_copy(k, n)
                copies[k, n].start()
            if i >= LAG:
                use(*items[i - LAG], copies)
        return copies

    def join(k, n, copies):
        copies[k, n].wait_recv()
        pown[k, n] = pown[k, n] + pin[k, n]

    def x_copy(src, dst, send, recv, to):
        copy = pltpu.make_async_remote_copy(
            src_ref=src, dst_ref=dst, send_sem=send, recv_sem=recv,
            device_id=(seq, to), device_id_type=MESH,
        )
        copy.start()
        return copy

    middle = NCH // 2
    js = [lax.rem(x + o, nx) for o in ORDER]

    mixed_order = [(i % 2) * middle + i // 2 for i in range(NCH)]
    relay, final1, final2 = {}, {}, {}

    opening = solve(js[0:1])
    read_local(0, js[0], opening)
    loads[5].wait()
    for first, copies in zip(firsts, g_back):
        for copy in copies:
            copy.wait_recv()
        for h in range(first, first + PAIR):
            take_memory(h)
        read_out(0, 0, js[0], opening, tuple(range(first, first + PAIR)))

    def send_relay(k, n, copies):
        join(k, n, copies)
        if n < middle:
            relay[n] = x_copy(pown.at[0, n], ra.at[n], r_send.at[n], r_recv.at[n], right)
        else:
            relay[n] = x_copy(pown.at[0, n], rb.at[n - middle], r_send.at[n], r_recv.at[n], left)

    copies = project([(0, n) for n in mixed_order], send_relay)
    sent += list(copies.values()) + list(relay.values())

    def send_first(k, n, copies):
        if k == 1 and n >= middle:
            join(k, n, copies)
            final1[n] = x_copy(pown.at[1, n], f1.at[n], f_send.at[0, n], f_recv.at[0, n], right)
        if k == 2 and n < middle:
            join(k, n, copies)
            final2[n] = x_copy(pown.at[2, n], f2.at[n], f_send.at[1, n], f_recv.at[1, n], left)

    opening = solve(js[1:3])
    every = tuple(range(HL))
    for i in range(2):
        read_local(i, js[1 + i], opening)
        read_out(1 + i, i, js[1 + i], opening, every)
    pairs = [(k, (n + middle * (k % 2)) % NCH) for n in range(NCH) for k in (1, 2)]
    copies = project(pairs, send_first)
    sent += list(copies.values())
    for n in range(middle):
        relay[n].wait_recv()
        join(1, n, copies)
        pown[1, n] = pown[1, n] + ra[n]
        final1[n] = x_copy(pown.at[1, n], f1.at[n], f_send.at[0, n], f_recv.at[0, n], right)
        m = n + middle
        relay[m].wait_recv()
        join(2, m, copies)
        pown[2, m] = pown[2, m] + rb[n]
        final2[m] = x_copy(pown.at[2, m], f2.at[m], f_send.at[1, m], f_recv.at[1, m], left)

    opening = solve(js[3:4])
    read_local(0, js[3], opening)
    read_out(3, 0, js[3], opening, every)
    sent += list(project([(3, n) for n in range(NCH)], join).values())
    for copy in sent:
        copy.wait_send()
    for i in range(NCH):
        n = (i % 2) * middle + i // 2
        m = (n + middle) % NCH
        final1[m].wait_recv()
        final2[n].wait_recv()
        if i % 2 == 1:
            for e in (n, m):
                o_ref[:, e * width : (e + 1) * width] = (pown[3, e] + f1[e] + f2[e]).astype(BF16)
    for copy in list(final1.values()) + list(final2.values()):
        copy.wait_send()


def solution(mesh, ny=4, nz=8):
    nx = mesh.shape["wide"] // 2

    def body(queries, keys, values, log_decay, ridge, out_weight):
        columns = out_weight.shape[1]
        width = columns // NCH
        half = SPAN // 2
        rows_h, rows_g = HD // 2 // nz, HD // nz
        tokens, inner = queries.shape
        vm = pltpu.VMEM
        dma = pltpu.SemaphoreType.DMA
        scratch = [
            vm((tokens, inner), BF16),
            vm((tokens, inner), BF16),
            vm((tokens, inner), BF16),
            vm((HL, tokens), F32),
            vm((1, inner), F32),
            vm(out_weight.shape, BF16),
            vm((HL + 1, HD // 2, HD), F32),
            vm((HL, HD, HD), F32),
            vm((nz, HL + 1, rows_h, HD), F32),
            vm((nz, HL, rows_g, HD), F32),
            vm((ny, HL + 1, rows_h, HD), F32),
            vm((ny, HL, rows_g, HD), F32),
            vm((nz, HL, rows_h, HD), F32),
            vm((nz, HL, rows_g, HD), F32),
            vm((HL, HD // 2, HD), F32),
            vm((HL, HD, HD), F32),
            vm((NJ, 2 * HL, HD, HD), F32),
            vm((NJ, 8, HD), F32),
            vm((NJ, 8, HD), F32),
            vm((NJ, HL, SPAN, SPAN), F32),
            vm((NJ, HL, SPAN, SPAN), F32),
            vm((NJ, HL, HD, 2 * SPAN), BF16),
            vm((NJ, HL, HD, 2 * SPAN), BF16),
            vm((NJ, HL, HD, SPAN), F32),
            vm((HL, HD, SPAN), F32),
            vm((HL, HD, HD), F32),
            vm((HL, 2 * HD, 2 * HD), BF16),
            vm((2 * HL, 3 * HD, 2 * HD), BF16),
            vm((2 * HL, HD, 2 * HD), BF16),
            vm((NJ, HL, 3 * HD, 2 * HD), BF16),
            vm((2 * HL, HD, SPAN), F32),
            vm((2 * HL, HD, SPAN), F32),
            vm((2 * HL, HD, SPAN), F32),
            vm((NJ, SPAN, HL * HD), BF16),
            vm((NJ, NCH, half, width), F32),
            vm((NJ, NCH, half, width), F32),
            vm((NJ, NCH, half, width), F32),
            vm((NCH // 2, half, width), F32),
            vm((NCH // 2, half, width), F32),
            vm((NCH, half, width), F32),
            vm((NCH, half, width), F32),
            dma((6,)),
            dma((2 * HL + 2, nz)),
            dma((2 * HL + 2, nz)),
            dma((HL + 1, ny)),
            dma((HL + 1, ny)),
            dma((NJ, NCH)),
            dma((NJ, NCH)),
            dma((NCH,)),
            dma((NCH,)),
            dma((2, NCH)),
            dma((2, NCH)),
        ]
        space = pl.BlockSpec(memory_space=pltpu.VMEM)
        return pl.pallas_call(
            functools.partial(kernel, ny, nz, nx),
            out_shape=jax.ShapeDtypeStruct((queries.shape[0] // (2 * nx), columns), BF16),
            in_specs=[pl.BlockSpec(memory_space=pl.ANY)] * 6,
            out_specs=space,
            scratch_shapes=scratch,
            compiler_params=pltpu.CompilerParams(
                collective_id=0, has_side_effects=True, vmem_limit_bytes=50000 << 10
            ),
        )(*(pltpu.with_memory_space_constraint(a, pltpu.HBM) for a in (queries, keys, values, log_decay.T, ridge[None, :], out_weight)))

    placed = (
        P("seq", "wide"),
        P("seq", "wide"),
        P("seq", "wide"),
        P("seq", "wide"),
        P("wide"),
        P("wide", None),
    )
    return jax.shard_map(
        body, mesh=mesh, in_specs=placed, out_specs=P(("seq", "wide"), None), check_vma=False
    )
```
